32 devices in a mesh: dp: 8 (over y, x, core), tensor: 4 (over z).
Axes of the slice: x: 2, y: 2, z: 4, core: 2. Of those that a mesh axis runs over, the one named last changes fastest.
Arguments:
- tokens: bfloat16 [16, 256, 768], P('dp', 'tensor'), may hold values from -6 to 6
- cotangent: bfloat16 [16, 256, 768], P('dp', 'tensor'), may hold values from -6 to 6
- labels: int32 [16], replicated, may hold values from 0 to 999
- timesteps: int32 [16], replicated, may hold values from 0 to 999
- class_table: bfloat16 [1000, 768], replicated, may hold values from -5 to 5
- modulation_weight: bfloat16 [768, 4608], P('dp', 'tensor'), may hold values from -0.21875 to 0.21875
- modulation_bias: float32 [4608], P('tensor'), may hold values from -3 to 3
- attend_weight: bfloat16 [768, 3, 768], P('dp', None, 'tensor'), may hold values from -0.21875 to 0.21875
- attend_bias: float32 [2, 768], P(None, 'tensor'), may hold values from -3 to 3
- output_weight: bfloat16 [768, 768], P('dp', 'tensor'), may hold values from -0.875 to 0.875
- output_bias: float32 [768], replicated, may hold values from -3 to 3
- expand_weight: bfloat16 [768, 3072], P('dp', 'tensor'), may hold values from -0.21875 to 0.21875
- expand_bias: float32 [3072], P('tensor'), may hold values from -3 to 3
- reduce_weight: bfloat16 [768, 3072], P('dp', 'tensor'), may hold values from -0.109375 to 0.109375
- reduce_bias: float32 [768], replicated, may hold values from -3 to 3
Outputs:
- block_output: bfloat16 [16, 256, 768], P('dp', 'tensor')
- tokens_grad: float32 [16, 256, 768], P('dp', 'tensor')
- table_grad: float32 [1000, 768], P(None, 'dp')
- modulation_weight_grad: float32 [768, 4608], P('dp', 'tensor')
- modulation_bias_grad: float32 [4608], P('tensor')
- attend_weight_grad: float32 [768, 3, 768], P('dp', None, 'tensor')
- attend_bias_grad: float32 [2, 768], P(None, 'tensor')
- output_weight_grad: float32 [768, 768], P('dp', 'tensor')
- output_bias_grad: float32 [768], replicated
- expand_weight_grad: float32 [768, 3072], P('dp', 'tensor')
- expand_bias_grad: float32 [3072], P('tensor')
- reduce_weight_grad: float32 [768, 3072], P('dp', 'tensor')
- reduce_bias_grad: float32 [768], replicated
The draws below stay inside these ranges and needn't reach their ends.
All inputs are finite; a program needn't handle non-finite values.
Results may differ from the reference program's by a relative error of at most 0.02.
The reference program's roundings to bfloat16 on the way count: a program that leaves them out, or rounds other values in their place, can miss the bound.
Values may be sent and summed in bfloat16 or wider, within the bound.
No kernel may reach another device: no remote copies, remote signals or barrier semaphores. Data moves between devices by JAX's collectives and lax.ppermute only.
A program may use at most 128 MiB of HBM per device.

```python
import math
import jax
import jax.numpy as jnp
from jax import lax

D = 768
HD = 64
FF = 3072
SEQ = 256
CLASSES = 1000
TSTEPS = 1000
LATENTS = 16


def set_ends(entries, rng, least, top_value):
    extent = entries.shape
    place = [jax.random.randint(jax.random.fold_in(rng, axis), (), 0, extent[axis]) for axis in range(len(extent))]
    entries = entries.at[tuple(place)].set(least)
    longest = extent.index(max(extent))
    place[longest] = (place[longest] + 1) % extent[longest]
    return entries.at[tuple(place)].set(top_value)


def raised(entries, rng, source, target, parts, factor):
    def block_of(axis_at):
        return (jnp.arange(entries.shape[axis_at]) // (entries.shape[axis_at] // parts)).reshape((-1,) + (1,) * (entries.ndim - 1 - axis_at))

    near = jax.random.permutation(rng, parts)[block_of(target)]
    far = (block_of(target) + parts // 2) % parts
    return jnp.where((block_of(source) == near) | (block_of(source) == far), factor * entries, entries)


def shard_levels(key, shape, shards, least, top_value):
    def one(axis_at, parts):
        heights = jax.random.uniform(jax.random.fold_in(jax.random.fold_in(key, 6), axis_at), (parts,), jnp.float32, least / len(shards), top_value / len(shards))
        return jnp.repeat(jnp.exp(heights), shape[axis_at] // parts).reshape((-1,) + (1,) * (len(shape) - axis_at - 1))

    level = one(*shards[0])
    for cut in shards[1:]:
        level = level * one(*cut)
    return level


def centred(rng, dims, deviation, bound, cuts=(), held_as=jnp.bfloat16):
    factor_of = shard_levels(rng, dims, cuts, -0.22, 0.18) if cuts else 1.0
    drawn = jax.random.normal(rng, dims, jnp.float32) * deviation * factor_of
    return jnp.minimum(jnp.maximum(drawn, -bound), bound).astype(held_as)


def noise_with(rng, dims, spread, limit, split, heavy, kind=jnp.bfloat16):
    drawn = spread * jax.random.normal(rng, dims, jnp.float32)
    if split:
        drawn = drawn * shard_levels(rng, dims, split, -0.22, 0.18)
    return jnp.clip(raised(drawn, jax.random.fold_in(rng, 3), *heavy), -limit, limit).astype(kind)


def setup_inputs(seed: int = 0) -> dict:
    key_list = jax.random.split(jax.random.key(seed), 16)
    return {
        "tokens": centred(key_list[0], (LATENTS, SEQ, D), 1.0, 6.0, ((0, 8), (1, 4))),
        "cotangent": noise_with(key_list[1], (LATENTS, SEQ, D), 1.0, 6.0, ((0, 8), (1, 4)), (0, 2, 8, 2.0)),
        "labels": set_ends(jax.random.randint(key_list[2], (LATENTS,), 0, CLASSES), jax.random.fold_in(key_list[2], 1), 0, CLASSES - 1).astype(jnp.int32),
        "timesteps": set_ends(jax.random.randint(key_list[3], (LATENTS,), 0, TSTEPS), jax.random.fold_in(key_list[3], 1), 0, TSTEPS - 1).astype(jnp.int32),
        "class_table": centred(key_list[4], (CLASSES, D), 1.0, 5.0),
        "modulation_weight": centred(key_list[5], (D, 6 * D), D ** -0.5, 0.21875, ((0, 8), (1, 4))),
        "modulation_bias": centred(key_list[6], (6 * D,), 0.5, 3.0, ((0, 4),), jnp.float32),
        "attend_weight": centred(key_list[7], (D, 3, D), D ** -0.5, 0.21875, ((0, 8), (2, 4))),
        "attend_bias": centred(key_list[8], (2, D), 0.5, 3.0, ((1, 4),), jnp.float32),
        "output_weight": centred(key_list[9], (D, D), (D // 16) ** -0.5, 0.875, ((0, 8), (1, 4))),
        "output_bias": centred(key_list[10], (D,), 0.5, 3.0, (), jnp.float32),
        "expand_weight": centred(key_list[11], (D, FF), D ** -0.5, 0.21875, ((0, 8), (1, 4))),
        "expand_bias": centred(key_list[12], (FF,), 0.5, 3.0, ((0, 4),), jnp.float32),
        "reduce_weight": centred(key_list[13], (D, FF), FF ** -0.5, 0.109375, ((0, 8), (1, 4))),
        "reduce_bias": centred(key_list[14], (D,), 0.5, 3.0, (), jnp.float32),
    }


norm_eps = 1e-06

def timestep_features(steps_in, model_width):
    halfway = model_width // 2
    frequency = jnp.exp(-math.log(10000.0) * jnp.arange(halfway, dtype=jnp.float32) / halfway)
    angles = steps_in.astype(jnp.float32)[:, None] * frequency[None, :]
    return jnp.concatenate([jnp.cos(angles), jnp.sin(angles)], axis=1)

def condition(label_ids, steps_in, class_table):
    looked = jnp.take(class_table, label_ids, axis=0).astype(jnp.float32)
    return looked + timestep_features(steps_in, class_table.shape[1])

def silu_back(inputs, upstream):
    sigmoid = jax.nn.sigmoid(inputs)
    return upstream * sigmoid * (1.0 + inputs * (1.0 - sigmoid))

def gelu_back(inputs, upstream):
    outputs, pullback = jax.vjp(lambda inner: jax.nn.gelu(inner, approximate=True), inputs)
    return pullback(upstream)[0]

def normalize(inputs):
    centered = inputs - lax.optimization_barrier(jnp.mean(inputs, axis=-1, keepdims=True))
    inverse = lax.rsqrt(lax.optimization_barrier(jnp.mean(centered * centered, axis=-1, keepdims=True)) + norm_eps)
    return (centered * inverse, inverse)

def norm_back(upstream, normed, inverse):
    return inverse * (upstream - lax.optimization_barrier(jnp.mean(upstream, axis=-1, keepdims=True)) - normed * lax.optimization_barrier(jnp.mean(upstream * normed, axis=-1, keepdims=True)))

def wide(array):
    return array.astype(jnp.float32)

def block_pass(tokens, cotangent, modulation, attend_weight, attend_bias, output_weight, output_bias, expand_weight, expand_bias, reduce_weight, reduce_bias):
    latent_count, seq_len, model_width = tokens.shape
    head_count = model_width // HD
    score_scale = 1.0 / math.sqrt(HD)
    pieces = modulation.reshape(latent_count, 6, 1, model_width)
    shift_attend, scale_attend, gate_attend = (pieces[:, 0], pieces[:, 1], pieces[:, 2])
    shift_hidden, scale_hidden, gate_hidden = (pieces[:, 3], pieces[:, 4], pieces[:, 5])
    tokens_wide = wide(tokens)
    normed_first, inverse_first = normalize(tokens_wide)
    attend_in = (normed_first * (1.0 + scale_attend) + shift_attend).astype(jnp.bfloat16)
    bias_rows = jnp.stack([attend_bias[0], jnp.zeros_like(attend_bias[0]), attend_bias[1]])
    projected = (jnp.einsum('bsd,dje->jbse', wide(attend_in), wide(attend_weight)) + bias_rows[:, None, None, :]).astype(jnp.bfloat16)
    split_heads = projected.reshape(3, latent_count, seq_len, head_count, HD)
    query_heads, key_heads, value_heads = (split_heads[0], split_heads[1], split_heads[2])
    scores = jnp.einsum('bqhe,bkhe->bhqk', wide(query_heads), wide(key_heads)) * score_scale
    log_total = jax.nn.logsumexp(scores, axis=-1)
    probs = jnp.exp(scores - log_total[..., None]).astype(jnp.bfloat16)
    mixed = jnp.einsum('bhqk,bkhe->bqhe', wide(probs), wide(value_heads)).astype(jnp.bfloat16)
    mixed_rows = mixed.reshape(latent_count, seq_len, model_width)
    attend_out = jnp.einsum('bsi,oi->bso', wide(mixed_rows), wide(output_weight)) + output_bias
    residual = tokens_wide + gate_attend * attend_out
    normed_second, inverse_second = normalize(residual)
    hidden_in = (normed_second * (1.0 + scale_hidden) + shift_hidden).astype(jnp.bfloat16)
    pre_act = jnp.einsum('bsd,df->bsf', wide(hidden_in), wide(expand_weight)) + expand_bias
    activated = jax.nn.gelu(pre_act, approximate=True).astype(jnp.bfloat16)
    hidden_out = jnp.einsum('bsf,of->bso', wide(activated), wide(reduce_weight)) + reduce_bias
    block_output = (residual + gate_hidden * hidden_out).astype(jnp.bfloat16)
    upstream = wide(cotangent)
    grad_gate_hidden = lax.optimization_barrier(jnp.sum(upstream * hidden_out, axis=1))
    reduce_term = upstream * gate_hidden
    grad_reduce_bias = lax.optimization_barrier(jnp.sum(reduce_term, axis=(0, 1)))
    reduce_in = reduce_term.astype(jnp.bfloat16)
    grad_act = jnp.einsum('bso,of->bsf', wide(reduce_in), wide(reduce_weight))
    grad_reduce = jnp.einsum('bso,bsf->of', wide(reduce_in), wide(activated))
    grad_pre = gelu_back(pre_act, grad_act)
    grad_expand_bias = lax.optimization_barrier(jnp.sum(grad_pre, axis=(0, 1)))
    grad_pre_low = grad_pre.astype(jnp.bfloat16)
    grad_expand = jnp.einsum('bsd,bsf->df', wide(hidden_in), wide(grad_pre_low))
    grad_hidden_in = jnp.einsum('bsf,df->bsd', wide(grad_pre_low), wide(expand_weight))
    grad_shift_hidden = lax.optimization_barrier(jnp.sum(grad_hidden_in, axis=1))
    grad_scale_hidden = lax.optimization_barrier(jnp.sum(grad_hidden_in * normed_second, axis=1))
    grad_residual = upstream + norm_back(grad_hidden_in * (1.0 + scale_hidden), normed_second, inverse_second)
    grad_gate_attend = lax.optimization_barrier(jnp.sum(grad_residual * attend_out, axis=1))
    output_term = grad_residual * gate_attend
    grad_output_bias = lax.optimization_barrier(jnp.sum(output_term, axis=(0, 1)))
    output_in = output_term.astype(jnp.bfloat16)
    grad_output = jnp.einsum('bso,bsi->oi', wide(output_in), wide(mixed_rows))
    grad_mixed = jnp.einsum('bso,oi->bsi', wide(output_in), wide(output_weight)).astype(jnp.bfloat16)
    grad_mixed_heads = grad_mixed.reshape(latent_count, seq_len, head_count, HD)
    recomputed = jnp.exp(scores - log_total[..., None])
    row_dot = jnp.einsum('bqhe,bqhe->bhq', wide(grad_mixed_heads), wide(mixed))
    grad_probs = jnp.einsum('bqhe,bkhe->bhqk', wide(grad_mixed_heads), wide(value_heads))
    grad_logit = (recomputed * (grad_probs - row_dot[..., None])).astype(jnp.bfloat16)
    grad_query = jnp.einsum('bhqk,bkhe->bqhe', wide(grad_logit), wide(key_heads)) * score_scale
    grad_key = jnp.einsum('bhqk,bqhe->bkhe', wide(grad_logit), wide(query_heads)) * score_scale
    grad_value = jnp.einsum('bhqk,bqhe->bkhe', wide(probs), wide(grad_mixed_heads))
    grad_projected = jnp.stack([grad_query, grad_key, grad_value]).reshape(3, latent_count, seq_len, model_width)
    grad_attend_bias = jnp.stack([lax.optimization_barrier(jnp.sum(grad_projected[0], axis=(0, 1))), lax.optimization_barrier(jnp.sum(grad_projected[2], axis=(0, 1)))])
    grad_projected_low = grad_projected.astype(jnp.bfloat16)
    grad_attend = jnp.einsum('bsd,jbse->dje', wide(attend_in), wide(grad_projected_low))
    grad_attend_in = jnp.einsum('jbse,dje->bsd', wide(grad_projected_low), wide(attend_weight))
    grad_shift_attend = lax.optimization_barrier(jnp.sum(grad_attend_in, axis=1))
    grad_scale_attend = lax.optimization_barrier(jnp.sum(grad_attend_in * normed_first, axis=1))
    tokens_grad = grad_residual + norm_back(grad_attend_in * (1.0 + scale_attend), normed_first, inverse_first)
    grad_modulation = jnp.concatenate([grad_shift_attend, grad_scale_attend, grad_gate_attend, grad_shift_hidden, grad_scale_hidden, grad_gate_hidden], axis=1)
    grads = (grad_attend, grad_attend_bias, grad_output, grad_output_bias, grad_expand, grad_expand_bias, grad_reduce, grad_reduce_bias)
    return (block_output, tokens_grad, grad_modulation, grads)

def reference(tokens, cotangent, labels, timesteps, class_table, modulation_weight, modulation_bias, attend_weight, attend_bias, output_weight, output_bias, expand_weight, expand_bias, reduce_weight, reduce_bias):
    cond_all = condition(labels, timesteps, class_table)
    silu_all = jax.nn.silu(cond_all).astype(jnp.bfloat16)
    modulation = jnp.dot(silu_all, modulation_weight, preferred_element_type=jnp.float32) + modulation_bias
    group = math.gcd(LATENTS, 16)
    blocks = LATENTS // group

    def regroup(array):
        return array.reshape((blocks, group) + array.shape[1:])
    params = (attend_weight, attend_bias, output_weight, output_bias, expand_weight, expand_bias, reduce_weight, reduce_bias)
    initial = tuple((jnp.zeros(param.shape, jnp.float32) for param in params))

    def step(carry, inputs):
        tokens_block, cotangent_block, modulation_block = inputs
        block_output, tokens_grad, grad_modulation, grads = block_pass(tokens_block, cotangent_block, modulation_block, *params)
        return (jax.tree.map(jnp.add, carry, grads), (block_output, tokens_grad, grad_modulation))
    totals, stacked = lax.scan(step, initial, (regroup(tokens), regroup(cotangent), regroup(modulation)))
    block_output = stacked[0].reshape(LATENTS, SEQ, D)
    tokens_grad = stacked[1].reshape(LATENTS, SEQ, D)
    grad_modulation = stacked[2].reshape(LATENTS, 6 * D)
    grad_modulation_bias = lax.optimization_barrier(jnp.sum(grad_modulation, axis=0))
    grad_modulation_low = grad_modulation.astype(jnp.bfloat16)
    grad_modulation_weight = jnp.dot(silu_all.T, grad_modulation_low, preferred_element_type=jnp.float32)
    grad_silu = jnp.dot(grad_modulation_low, modulation_weight.T, preferred_element_type=jnp.float32)
    grad_cond = silu_back(cond_all, grad_silu)
    onehot = (labels[:, None] == jnp.arange(CLASSES, dtype=jnp.int32)[None, :]).astype(jnp.float32)
    table_grad = jnp.dot(onehot.T, grad_cond, precision=lax.Precision.HIGHEST, preferred_element_type=jnp.float32)
    return (block_output, tokens_grad, table_grad, grad_modulation_weight, grad_modulation_bias, totals[0], totals[1], totals[2], totals[3], totals[4], totals[5], totals[6], totals[7])
```

```python
import math

import jax
import jax.numpy as jnp
from jax import lax
from jax.sharding import PartitionSpec as P

HD = 64


norm_eps = 1e-06


def timestep_features(steps_in, model_width):
    halfway = model_width // 2
    frequency = jnp.exp(-math.log(10000.0) * jnp.arange(halfway, dtype=jnp.float32) / halfway)
    angles = steps_in.astype(jnp.float32)[:, None] * frequency[None, :]
    return jnp.concatenate([jnp.cos(angles), jnp.sin(angles)], axis=1)


def condition(label_ids, steps_in, class_table):
    looked = jnp.take(class_table, label_ids, axis=0).astype(jnp.float32)
    return looked + timestep_features(steps_in, class_table.shape[1])


def silu_back(inputs, upstream):
    sigmoid = jax.nn.sigmoid(inputs)
    return upstream * sigmoid * (1.0 + inputs * (1.0 - sigmoid))


def gelu_back(inputs, upstream):
    outputs, pullback = jax.vjp(lambda inner: jax.nn.gelu(inner, approximate=True), inputs)
    return pullback(upstream)[0]


def normalize(inputs):
    centered = inputs - jnp.mean(inputs, axis=-1, keepdims=True)
    inverse = lax.rsqrt(jnp.mean(centered * centered, axis=-1, keepdims=True) + norm_eps)
    return (centered * inverse, inverse)


def norm_back(upstream, normed, inverse):
    return inverse * (
        upstream
        - jnp.mean(upstream, axis=-1, keepdims=True)
        - normed * jnp.mean(upstream * normed, axis=-1, keepdims=True)
    )


def collect(local_rows):
    return lax.all_gather(local_rows, "tensor", axis=1, tiled=True)


def spread(partial_rows):
    return lax.psum_scatter(partial_rows, "tensor", scatter_dimension=1, tiled=True)


def on_device(
    tokens,
    cotangent,
    labels,
    timesteps,
    class_table,
    modulation_weight,
    modulation_bias,
    attend_weight,
    attend_bias,
    output_weight,
    output_bias,
    expand_weight,
    expand_bias,
    reduce_weight,
    reduce_bias,
):
    tensor_count = lax.axis_size("tensor")
    data_index = lax.axis_index("dp")
    tensor_index = lax.axis_index("tensor")
    latent_count = tokens.shape[0]
    model_width = tokens.shape[2]
    row_share = modulation_weight.shape[0]
    head_width = attend_weight.shape[2]
    head_count = head_width // HD
    classes_total = class_table.shape[0]
    score_scale = 1.0 / math.sqrt(HD)
    row_start = data_index * row_share
    zero_index = jnp.zeros((), jnp.int32)
    modulation_full, attend_full, output_full, expand_full, reduce_full = (
        lax.all_gather(modulation_weight, "dp", axis=0, tiled=True),
        lax.all_gather(attend_weight, "dp", axis=0, tiled=True),
        lax.all_gather(output_weight, "dp", axis=0, tiled=True),
        lax.all_gather(expand_weight, "dp", axis=0, tiled=True),
        lax.all_gather(reduce_weight, "dp", axis=0, tiled=True),
    )
    own_labels = lax.dynamic_slice_in_dim(labels, data_index * latent_count, latent_count)
    own_steps = lax.dynamic_slice_in_dim(timesteps, data_index * latent_count, latent_count)
    cond_own = condition(own_labels, own_steps, class_table)
    silu_own = jax.nn.silu(cond_own).astype(jnp.bfloat16)
    modulation_share = jnp.dot(silu_own, modulation_full, preferred_element_type=jnp.float32)
    modulation = lax.all_gather(modulation_share + modulation_bias, "tensor", axis=1, tiled=True)
    pieces = modulation.reshape(latent_count, 6, 1, model_width)
    shift_attend, scale_attend, gate_attend = (pieces[:, 0], pieces[:, 1], pieces[:, 2])
    shift_hidden, scale_hidden, gate_hidden = (pieces[:, 3], pieces[:, 4], pieces[:, 5])
    tokens_wide = tokens.astype(jnp.float32)
    normed_first, inverse_first = normalize(tokens_wide)
    attend_in = (normed_first * (1.0 + scale_attend) + shift_attend).astype(jnp.bfloat16)
    attend_rows = collect(attend_in)
    seq_len = attend_rows.shape[1]
    bias_rows = jnp.stack([attend_bias[0], jnp.zeros_like(attend_bias[0]), attend_bias[1]])
    projected = (
        jnp.einsum("bsd,dje->jbse", attend_rows, attend_full, preferred_element_type=jnp.float32)
        + bias_rows[:, None, None, :]
    ).astype(jnp.bfloat16)
    split_heads = projected.reshape(3, latent_count, seq_len, head_count, HD)
    query_heads, key_heads, value_heads = (split_heads[0], split_heads[1], split_heads[2])
    scores = (
        jnp.einsum("bqhe,bkhe->bhqk", query_heads, key_heads, preferred_element_type=jnp.float32)
        * score_scale
    )
    log_total = jax.nn.logsumexp(scores, axis=-1)
    probs = jnp.exp(scores - log_total[..., None]).astype(jnp.bfloat16)
    mixed = jnp.einsum(
        "bhqk,bkhe->bqhe", probs, value_heads, preferred_element_type=jnp.float32
    ).astype(jnp.bfloat16)
    mixed_rows = mixed.reshape(latent_count, seq_len, head_width)
    attend_out = (
        spread(
            jnp.einsum("bsi,oi->bso", mixed_rows, output_full, preferred_element_type=jnp.float32)
        )
        + output_bias
    )
    residual = tokens_wide + gate_attend * attend_out
    normed_second, inverse_second = normalize(residual)
    hidden_in = (normed_second * (1.0 + scale_hidden) + shift_hidden).astype(jnp.bfloat16)
    hidden_rows = collect(hidden_in)
    pre_act = (
        jnp.einsum("bsd,df->bsf", hidden_rows, expand_full, preferred_element_type=jnp.float32)
        + expand_bias
    )
    activated = jax.nn.gelu(pre_act, approximate=True).astype(jnp.bfloat16)
    hidden_out = (
        spread(
            jnp.einsum("bsf,of->bso", activated, reduce_full, preferred_element_type=jnp.float32)
        )
        + reduce_bias
    )
    block_output = (residual + gate_hidden * hidden_out).astype(jnp.bfloat16)
    upstream = cotangent.astype(jnp.float32)
    grad_gate_hidden = jnp.sum(upstream * hidden_out, axis=1)
    reduce_term = upstream * gate_hidden
    grad_reduce_bias = jnp.sum(reduce_term, axis=(0, 1))
    reduce_rows = collect(reduce_term.astype(jnp.bfloat16))
    grad_act = jnp.einsum(
        "bso,of->bsf", reduce_rows, reduce_full, preferred_element_type=jnp.float32
    )
    grad_reduce = jnp.einsum(
        "bso,bsf->of", reduce_rows, activated, preferred_element_type=jnp.float32
    )
    grad_pre = gelu_back(pre_act, grad_act)
    grad_expand_bias = jnp.sum(grad_pre, axis=(0, 1))
    grad_pre_low = grad_pre.astype(jnp.bfloat16)
    grad_expand = jnp.einsum(
        "bsd,bsf->df", hidden_rows, grad_pre_low, preferred_element_type=jnp.float32
    )
    grad_hidden_in = spread(
        jnp.einsum("bsf,df->bsd", grad_pre_low, expand_full, preferred_element_type=jnp.float32)
    )
    grad_shift_hidden = jnp.sum(grad_hidden_in, axis=1)
    grad_scale_hidden = jnp.sum(grad_hidden_in * normed_second, axis=1)
    grad_residual = upstream + norm_back(
        grad_hidden_in * (1.0 + scale_hidden), normed_second, inverse_second
    )
    grad_gate_attend = jnp.sum(grad_residual * attend_out, axis=1)
    output_term = grad_residual * gate_attend
    grad_output_bias = jnp.sum(output_term, axis=(0, 1))
    output_rows = collect(output_term.astype(jnp.bfloat16))
    grad_output = jnp.einsum(
        "bso,bsi->oi", output_rows, mixed_rows, preferred_element_type=jnp.float32
    )
    grad_mixed = jnp.einsum(
        "bso,oi->bsi", output_rows, output_full, preferred_element_type=jnp.float32
    ).astype(jnp.bfloat16)
    grad_mixed_heads = grad_mixed.reshape(latent_count, seq_len, head_count, HD)
    recomputed = jnp.exp(
        jnp.einsum("bqhe,bkhe->bhqk", query_heads, key_heads, preferred_element_type=jnp.float32)
        * score_scale
        - log_total[..., None]
    )
    row_dot = jnp.einsum(
        "bqhe,bqhe->bhq", grad_mixed_heads, mixed, preferred_element_type=jnp.float32
    )
    grad_probs = jnp.einsum(
        "bqhe,bkhe->bhqk", grad_mixed_heads, value_heads, preferred_element_type=jnp.float32
    )
    grad_logit = (recomputed * (grad_probs - row_dot[..., None])).astype(jnp.bfloat16)
    grad_query = (
        jnp.einsum("bhqk,bkhe->bqhe", grad_logit, key_heads, preferred_element_type=jnp.float32)
        * score_scale
    )
    grad_key = (
        jnp.einsum("bhqk,bqhe->bkhe", grad_logit, query_heads, preferred_element_type=jnp.float32)
        * score_scale
    )
    grad_value = jnp.einsum(
        "bhqk,bqhe->bkhe", probs, grad_mixed_heads, preferred_element_type=jnp.float32
    )
    grad_projected = jnp.stack([grad_query, grad_key, grad_value]).reshape(
        3, latent_count, seq_len, head_width
    )
    grad_attend_bias = jnp.stack(
        [jnp.sum(grad_projected[0], axis=(0, 1)), jnp.sum(grad_projected[2], axis=(0, 1))]
    )
    grad_projected_low = grad_projected.astype(jnp.bfloat16)
    grad_attend = jnp.einsum(
        "bsd,jbse->dje", attend_rows, grad_projected_low, preferred_element_type=jnp.float32
    )
    grad_attend_in = spread(
        jnp.einsum(
            "jbse,dje->bsd", grad_projected_low, attend_full, preferred_element_type=jnp.float32
        )
    )
    grad_shift_attend = jnp.sum(grad_attend_in, axis=1)
    grad_scale_attend = jnp.sum(grad_attend_in * normed_first, axis=1)
    tokens_grad = grad_residual + norm_back(
        grad_attend_in * (1.0 + scale_attend), normed_first, inverse_first
    )
    grad_modulation_rows = jnp.concatenate(
        [
            grad_shift_attend,
            grad_scale_attend,
            grad_gate_attend,
            grad_shift_hidden,
            grad_scale_hidden,
            grad_gate_hidden,
        ],
        axis=1,
    )
    grad_modulation = lax.psum_scatter(
        grad_modulation_rows, "tensor", scatter_dimension=1, tiled=True
    )
    grad_modulation_bias = jnp.sum(grad_modulation, axis=0)
    grad_modulation_low = grad_modulation.astype(jnp.bfloat16)
    grad_modulation_weight = jnp.einsum(
        "ld,lc->dc", silu_own, grad_modulation_low, preferred_element_type=jnp.float32
    )
    grad_modulation_weight, grad_attend, grad_output, grad_expand, grad_reduce = (
        lax.psum_scatter(grad_modulation_weight, "dp", scatter_dimension=0, tiled=True),
        lax.psum_scatter(grad_attend, "dp", scatter_dimension=0, tiled=True),
        lax.psum_scatter(grad_output, "dp", scatter_dimension=0, tiled=True),
        lax.psum_scatter(grad_expand, "dp", scatter_dimension=0, tiled=True),
        lax.psum_scatter(grad_reduce, "dp", scatter_dimension=0, tiled=True),
    )
    grad_silu = jnp.einsum(
        "lc,dc->ld", grad_modulation_low, modulation_full, preferred_element_type=jnp.float32
    )
    grad_cond = silu_back(cond_own, grad_silu)
    shard_rows = lax.all_gather(grad_cond, ("dp", "tensor"), axis=0, tiled=True)
    row_count = shard_rows.shape[0]
    positions = jnp.arange(row_count, dtype=jnp.int32)
    latent_ids = positions // latent_count // tensor_count * latent_count + positions % latent_count
    picked = jnp.take(labels, latent_ids)
    onehot = (picked[:, None] == jnp.arange(classes_total, dtype=jnp.int32)[None, :]).astype(
        jnp.float32
    )
    columns = lax.dynamic_slice_in_dim(shard_rows, row_start, row_share, 1)
    table_grad = jnp.einsum(
        "rc,rd->cd",
        onehot,
        columns,
        precision=lax.Precision.HIGHEST,
        preferred_element_type=jnp.float32,
    )
    expand_share = grad_expand_bias.shape[0]
    modulation_cols = grad_modulation_bias.shape[0]
    padded_attend = lax.dynamic_update_slice(
        jnp.zeros((2, head_width * tensor_count), jnp.float32),
        grad_attend_bias,
        (zero_index, tensor_index * head_width),
    )
    padded_expand = lax.dynamic_update_slice(
        jnp.zeros((expand_share * tensor_count,), jnp.float32),
        grad_expand_bias,
        (tensor_index * expand_share,),
    )
    padded_modulation = lax.dynamic_update_slice(
        jnp.zeros((modulation_cols * tensor_count,), jnp.float32),
        grad_modulation_bias,
        (tensor_index * modulation_cols,),
    )
    summed_attend, summed_expand, summed_modulation, summed_output, summed_reduce = lax.psum(
        (padded_attend, padded_expand, padded_modulation, grad_output_bias, grad_reduce_bias),
        ("dp", "tensor"),
    )
    attend_bias_grad = lax.dynamic_slice_in_dim(
        summed_attend, tensor_index * head_width, head_width, 1
    )
    expand_bias_grad = lax.dynamic_slice_in_dim(
        summed_expand, tensor_index * expand_share, expand_share, 0
    )
    modulation_bias_grad = lax.dynamic_slice_in_dim(
        summed_modulation, tensor_index * modulation_cols, modulation_cols, 0
    )
    return (
        block_output,
        tokens_grad,
        table_grad,
        grad_modulation_weight,
        modulation_bias_grad,
        grad_attend,
        attend_bias_grad,
        grad_output,
        summed_output,
        grad_expand,
        expand_bias_grad,
        grad_reduce,
        summed_reduce,
    )


def swap(values, axis, mask):
    count = lax.axis_size(axis)
    return lax.ppermute(values, axis, [(place, place ^ mask) for place in range(count)])


def unxor(parts, own):
    bit = 1
    while bit < len(parts):
        odd = (own & bit) != 0
        parts = [jnp.where(odd, parts[r ^ bit], parts[r]) for r in range(len(parts))]
        bit *= 2
    return parts


def pick(values, place):
    return lax.dynamic_index_in_dim(values, place, 0, keepdims=False)


def spread_pairs(partial):
    both = partial[0] + swap(partial[1], "dp", 1)
    rows = both.shape[0] // 2
    return both[:rows] + swap(both[rows:].astype(jnp.bfloat16), "tensor", 1).astype(jnp.float32)


def collect_pairs(rows):
    near = swap(rows, "tensor", 1)
    return jnp.concatenate([rows, near, swap(rows, "dp", 1), swap(near, "dp", 1)], axis=0)


def gather_weight(shard, is_own, core, chip):
    far = swap(shard, "tensor", 2)
    mine = jnp.where(is_own, shard, far)
    other = swap(jnp.where(is_own, far, shard), "dp", 1)
    first = core == 0
    share = jnp.concatenate(
        [jnp.where(first, mine, other), jnp.where(first, other, mine)], axis=0
    )
    shares = [share] + [swap(share, "dp", 2 * r) for r in (1, 2, 3)]
    return shares


def in_order(shares, chip, start, stop):
    return jnp.concatenate(unxor([s[:, start:stop] for s in shares], chip), axis=0)


def scatter_weight(partial, is_own, core, chip):
    blocks = partial.reshape(4, -1, partial.shape[1])
    total = pick(blocks, chip)
    for r in (1, 2, 3):
        sent = pick(blocks, chip ^ r).astype(jnp.bfloat16)
        total = total + swap(sent, "dp", 2 * r).astype(jnp.float32)
    halves = total.reshape(2, -1, total.shape[1])
    mine = pick(halves, core)
    other = swap(pick(halves, 1 - core), "dp", 1)
    kept = jnp.where(is_own, mine, other)
    sent = jnp.where(is_own, other, mine).astype(jnp.bfloat16)
    return kept + swap(sent, "tensor", 2).astype(jnp.float32)


def on_paired_device(
    tokens,
    cotangent,
    labels,
    timesteps,
    class_table,
    modulation_weight,
    modulation_bias,
    attend_weight,
    attend_bias,
    output_weight,
    output_bias,
    expand_weight,
    expand_bias,
    reduce_weight,
    reduce_bias,
):
    data_index = lax.axis_index("dp")
    tensor_index = lax.axis_index("tensor")
    core, chip = data_index & 1, data_index >> 1
    half = tensor_index >> 1
    is_own = half == core
    model_width = tokens.shape[2]
    row_share = modulation_weight.shape[0]
    head_width = attend_weight.shape[2]
    head_count = head_width // HD
    ff_width = expand_weight.shape[1]
    mod_width = modulation_weight.shape[1]
    latent_total = labels.shape[0]
    classes_total = class_table.shape[0]
    score_scale = 1.0 / math.sqrt(HD)

    slot = jnp.arange(latent_total, dtype=jnp.int32)
    latent_ids = ((slot >> 1) ^ data_index) * 2 + (slot & 1)
    chosen = latent_ids[:, None] == slot[None, :]
    labels_rel = jnp.sum(jnp.where(chosen, labels[None, :], 0), axis=1)
    steps_rel = jnp.sum(jnp.where(chosen, timesteps[None, :], 0), axis=1)
    looked = lax.dynamic_slice_in_dim(
        jnp.take(class_table, labels_rel, axis=0), data_index * row_share, row_share, 1
    ).astype(jnp.float32)
    halfway = model_width // 2
    column = data_index * row_share + jnp.arange(row_share, dtype=jnp.int32)
    is_cos = column < halfway
    place = jnp.where(is_cos, column, column - halfway).astype(jnp.float32)
    frequency = jnp.exp(-math.log(10000.0) * place / halfway)
    angles = steps_rel.astype(jnp.float32)[:, None] * frequency[None, :]
    cond = looked + jnp.where(is_cos[None, :], jnp.cos(angles), jnp.sin(angles))
    silu_act = jax.nn.silu(cond).astype(jnp.bfloat16)
    partial = jnp.dot(silu_act, modulation_weight, preferred_element_type=jnp.float32)
    partial = partial.reshape(8, 2, mod_width)
    partial = partial[:4] + swap(partial[4:], "dp", 4)
    partial = partial[:2] + swap(partial[2:], "dp", 2)
    crossed = swap(partial, "dp", 1)
    mod_cols = jnp.stack([partial[0] + crossed[1], partial[1] + crossed[0]]) + modulation_bias
    mod_parts = [mod_cols] + [swap(mod_cols, "tensor", r) for r in (1, 2, 3)]
    mod_full = jnp.concatenate(
        unxor([jnp.where(half == 0, m[:, 0], m[:, 1]) for m in mod_parts], tensor_index), axis=1
    )
    pieces = mod_full.reshape(2, 6, 1, model_width)
    own_pieces = pieces[0]

    paired = jnp.stack([tokens, cotangent], axis=1)
    kept, sent = pick(paired, half), pick(paired, 1 - half)
    own_pair = jnp.concatenate([kept, swap(sent, "tensor", 2)], axis=1)
    line = jnp.concatenate([own_pair, swap(own_pair, "tensor", 1)], axis=1)
    across = swap(line, "dp", 1)
    tokens_all = jnp.stack([line[0], across[0]]).astype(jnp.float32)
    upstream_all = jnp.stack([line[1], across[1]]).astype(jnp.float32)
    tokens_own = own_pair[0].astype(jnp.float32)
    upstream = own_pair[1].astype(jnp.float32)

    attn_shares = gather_weight(
        jnp.concatenate([attend_weight.reshape(row_share, -1), output_weight], axis=1),
        is_own,
        core,
        chip,
    )
    attend_full = in_order(attn_shares, chip, 0, 3 * head_width)
    output_full = in_order(attn_shares, chip, 3 * head_width, 4 * head_width)
    ff_shares = gather_weight(
        jnp.concatenate([expand_weight, reduce_weight], axis=1), is_own, core, chip
    )
    expand_full = in_order(ff_shares, chip, 0, ff_width)
    reduce_full = in_order(ff_shares, chip, ff_width, 2 * ff_width)
    bias_vec = jnp.concatenate([attend_bias.reshape(-1), expand_bias])
    bias_vec = jnp.where(is_own, bias_vec, swap(bias_vec, "tensor", 2))
    query_bias = bias_vec[:head_width]
    value_bias = bias_vec[head_width : 2 * head_width]
    expand_bias_q = bias_vec[2 * head_width :]

    normed_all, _ = normalize(tokens_all)
    attend_rows = (normed_all * (1.0 + pieces[:, 1]) + pieces[:, 0]).astype(jnp.bfloat16)
    seq_len = attend_rows.shape[1]
    bias_rows = jnp.concatenate([query_bias, jnp.zeros_like(query_bias), value_bias])
    projected = (
        jnp.einsum("bsd,de->bse", attend_rows, attend_full, preferred_element_type=jnp.float32)
        + bias_rows
    ).astype(jnp.bfloat16)
    split_heads = projected.reshape(2, seq_len, 3, head_count, HD)
    query_heads, key_heads, value_heads = (
        split_heads[:, :, 0],
        split_heads[:, :, 1],
        split_heads[:, :, 2],
    )
    scores = (
        jnp.einsum("bqhe,bkhe->bhqk", query_heads, key_heads, preferred_element_type=jnp.float32)
        * score_scale
    )
    log_total = jax.nn.logsumexp(scores, axis=-1)
    prob_wide = jnp.exp(scores - log_total[..., None])
    probs = prob_wide.astype(jnp.bfloat16)
    mixed = jnp.einsum(
        "bhqk,bkhe->bqhe", probs, value_heads, preferred_element_type=jnp.float32
    ).astype(jnp.bfloat16)
    mixed_rows = mixed.reshape(2, seq_len, head_width)
    attend_out = (
        spread_pairs(
            jnp.einsum("bsi,oi->bso", mixed_rows, output_full, preferred_element_type=jnp.float32)
        )
        + output_bias
    )
    normed_first, inverse_first = normalize(tokens_own)
    residual = tokens_own + own_pieces[2] * attend_out
    normed_second, inverse_second = normalize(residual)
    hidden_in = (normed_second * (1.0 + own_pieces[4]) + own_pieces[3]).astype(jnp.bfloat16)
    hidden_rows = collect_pairs(hidden_in)

    pre_act = (
        jnp.dot(hidden_rows, expand_full, preferred_element_type=jnp.float32) + expand_bias_q
    )
    activated = jax.nn.gelu(pre_act, approximate=True).astype(jnp.bfloat16)
    reduce_term = upstream_all * pieces[:, 5]
    reduce_rows = reduce_term.astype(jnp.bfloat16).reshape(-1, model_width)
    blocks = jnp.sum(reduce_term.reshape(4, -1, model_width), axis=1)
    grad_reduce_bias = (blocks[0] + blocks[1]) + (blocks[2] + blocks[3])
    grad_act = jnp.dot(reduce_rows, reduce_full, preferred_element_type=jnp.float32)
    grad_pre = gelu_back(pre_act, grad_act)
    grad_expand_bias = jnp.sum(grad_pre, axis=0)
    grad_pre_low = grad_pre.astype(jnp.bfloat16)
    grad_hidden_in = spread_pairs(
        jnp.einsum(
            "sf,df->sd", grad_pre_low, expand_full, preferred_element_type=jnp.float32
        ).reshape(2, seq_len, model_width)
    )
    hidden_out = (
        spread_pairs(
            jnp.einsum(
                "sf,of->so", activated, reduce_full, preferred_element_type=jnp.float32
            ).reshape(2, seq_len, model_width)
        )
        + reduce_bias
    )
    block_own = (residual + own_pieces[5] * hidden_out).astype(jnp.bfloat16)
    grad_gate_hidden = jnp.sum(upstream * hidden_out, axis=0)
    grad_reduce = jnp.einsum(
        "so,sf->of", reduce_rows, activated, preferred_element_type=jnp.float32
    )
    grad_expand = jnp.einsum(
        "sd,sf->df", hidden_rows, grad_pre_low, preferred_element_type=jnp.float32
    )

    grad_shift_hidden = jnp.sum(grad_hidden_in, axis=0)
    grad_scale_hidden = jnp.sum(grad_hidden_in * normed_second, axis=0)
    grad_residual = upstream + norm_back(
        grad_hidden_in * (1.0 + own_pieces[4]), normed_second, inverse_second
    )
    grad_gate_attend = jnp.sum(grad_residual * attend_out, axis=0)
    output_term = grad_residual * own_pieces[2]
    grad_output_bias = jnp.sum(output_term, axis=0)
    output_rows = collect_pairs(output_term.astype(jnp.bfloat16)).reshape(2, seq_len, model_width)

    grad_mixed = jnp.einsum(
        "bso,oi->bsi", output_rows, output_full, preferred_element_type=jnp.float32
    ).astype(jnp.bfloat16)
    grad_mixed_heads = grad_mixed.reshape(2, seq_len, head_count, HD)
    row_dot = jnp.einsum(
        "bqhe,bqhe->bhq", grad_mixed_heads, mixed, preferred_element_type=jnp.float32
    )
    grad_probs = jnp.einsum(
        "bqhe,bkhe->bhqk", grad_mixed_heads, value_heads, preferred_element_type=jnp.float32
    )
    grad_logit = (prob_wide * (grad_probs - row_dot[..., None])).astype(jnp.bfloat16)
    grad_query = (
        jnp.einsum("bhqk,bkhe->bqhe", grad_logit, key_heads, preferred_element_type=jnp.float32)
        * score_scale
    )
    grad_key = (
        jnp.einsum("bhqk,bqhe->bkhe", grad_logit, query_heads, preferred_element_type=jnp.float32)
        * score_scale
    )
    grad_value = jnp.einsum(
        "bhqk,bqhe->bkhe", probs, grad_mixed_heads, preferred_element_type=jnp.float32
    )
    grad_projected = jnp.concatenate(
        [g.reshape(2, seq_len, head_width) for g in (grad_query, grad_key, grad_value)], axis=2
    )
    summed_projected = jnp.sum(grad_projected, axis=(0, 1))
    grad_projected_low = grad_projected.astype(jnp.bfloat16)
    grad_attend_in = spread_pairs(
        jnp.einsum(
            "bse,de->bsd", grad_projected_low, attend_full, preferred_element_type=jnp.float32
        )
    )
    grad_attend = jnp.einsum(
        "bsd,bse->de", attend_rows, grad_projected_low, preferred_element_type=jnp.float32
    )
    grad_output = jnp.einsum(
        "bso,bsi->oi", output_rows, mixed_rows, preferred_element_type=jnp.float32
    )
    grad_shift_attend = jnp.sum(grad_attend_in, axis=0)
    grad_scale_attend = jnp.sum(grad_attend_in * normed_first, axis=0)
    tokens_grad_own = grad_residual + norm_back(
        grad_attend_in * (1.0 + own_pieces[1]), normed_first, inverse_first
    )

    ff_grad = scatter_weight(
        jnp.concatenate([grad_expand, grad_reduce], axis=1), is_own, core, chip
    )
    attn_grad = scatter_weight(
        jnp.concatenate([grad_attend, grad_output], axis=1), is_own, core, chip
    )

    def back(rows):
        count = rows.shape[0] // 2
        own, far = rows[:count], swap(rows[count:], "tensor", 2)
        return jnp.where(half == 0, jnp.stack([own, far]), jnp.stack([far, own]))

    block_output = back(block_own)
    tokens_grad = back(tokens_grad_own)

    grad_rows = jnp.concatenate(
        [
            grad_shift_attend,
            grad_scale_attend,
            grad_gate_attend,
            grad_shift_hidden,
            grad_scale_hidden,
            grad_gate_hidden,
        ]
    ).reshape(4, mod_width)
    here = pick(grad_rows, tensor_index) + swap(pick(grad_rows, tensor_index ^ 1), "tensor", 1)
    there = swap(pick(grad_rows, tensor_index ^ 2), "tensor", 2) + swap(
        pick(grad_rows, tensor_index ^ 3), "tensor", 3
    )
    grad_mod = jnp.where(half == 0, jnp.stack([here, there]), jnp.stack([there, here]))
    for mask in (1, 2, 4):
        grad_mod = jnp.concatenate([grad_mod, swap(grad_mod, "dp", mask)], axis=0)
    bias_sum = grad_mod
    while bias_sum.shape[0] > 1:
        bias_sum = bias_sum.reshape(-1, 2, mod_width)
        bias_sum = bias_sum[:, 0] + bias_sum[:, 1]
    modulation_bias_grad = bias_sum[0]
    grad_mod_low = grad_mod.astype(jnp.bfloat16)
    modulation_weight_grad = jnp.einsum(
        "ld,lc->dc", silu_act, grad_mod_low, preferred_element_type=jnp.float32
    )
    grad_silu = jnp.einsum(
        "lc,dc->ld", grad_mod_low, modulation_weight, preferred_element_type=jnp.float32
    )
    near = grad_silu + swap(grad_silu, "tensor", 1)
    grad_silu = near + swap(near, "tensor", 2)
    grad_cond = silu_back(cond, grad_silu)
    onehot = (
        labels_rel[:, None] == jnp.arange(classes_total, dtype=jnp.int32)[None, :]
    ).astype(jnp.float32)
    table_grad = jnp.einsum(
        "rc,rd->cd",
        onehot,
        grad_cond,
        precision=lax.Precision.HIGHEST,
        preferred_element_type=jnp.float32,
    )

    grad_output_bias = grad_output_bias + swap(grad_output_bias, "dp", 1)
    grad_output_bias = grad_output_bias + swap(grad_output_bias, "tensor", 1)
    sums = jnp.concatenate(
        [
            grad_output_bias,
            grad_reduce_bias,
            grad_expand_bias,
            summed_projected[:head_width],
            summed_projected[2 * head_width :],
        ]
    )
    sums = sums + swap(sums, "dp", 2)
    sums = sums + swap(sums, "dp", 4)
    sums = sums + swap(sums, "tensor", 2)
    split = sums[2 * model_width :]
    split = jnp.where(is_own, split, swap(split, "dp", 1))
    return (
        block_output,
        tokens_grad,
        table_grad,
        modulation_weight_grad,
        modulation_bias_grad,
        attn_grad[:, : 3 * head_width].reshape(row_share, 3, head_width),
        split[ff_width:].reshape(2, head_width),
        attn_grad[:, 3 * head_width :],
        sums[:model_width],
        ff_grad[:, :ff_width],
        split[:ff_width],
        ff_grad[:, ff_width:],
        sums[model_width : 2 * model_width],
    )


def solution(mesh):
    paired = mesh.shape["dp"] == 8 and mesh.shape["tensor"] == 4
    per_device = on_paired_device if paired else on_device
    placed = (
        P("dp", "tensor", None),
        P("dp", "tensor", None),
        P(),
        P(),
        P(),
        P("dp", "tensor"),
        P("tensor"),
        P("dp", None, "tensor"),
        P(None, "tensor"),
        P("dp", "tensor"),
        P(),
        P("dp", "tensor"),
        P("tensor"),
        P("dp", "tensor"),
        P(),
    )
    return jax.shard_map(
        per_device,
        mesh=mesh,
        in_specs=placed,
        out_specs=(
            P("dp", "tensor", None),
            P("dp", "tensor", None),
            P(None, "dp"),
            P("dp", "tensor"),
            P("tensor"),
            P("dp", None, "tensor"),
            P(None, "tensor"),
            P("dp", "tensor"),
            P(),
            P("dp", "tensor"),
            P("tensor"),
            P("dp", "tensor"),
            P(),
        ),
        check_vma=False,
    )
```

```python
import functools
import math

import jax
import jax.numpy as jnp
from jax import lax
from jax.experimental import pallas as pl
from jax.experimental.pallas import tpu as pltpu
from jax.sharding import PartitionSpec as P

HD = 64


norm_eps = 1e-06


def timestep_features(steps_in, model_width):
    halfway = model_width // 2
    frequency = jnp.exp(-math.log(10000.0) * jnp.arange(halfway, dtype=jnp.float32) / halfway)
    angles = steps_in.astype(jnp.float32)[:, None] * frequency[None, :]
    return jnp.concatenate([jnp.cos(angles), jnp.sin(angles)], axis=1)


def condition(label_ids, steps_in, class_table):
    looked = jnp.take(class_table, label_ids, axis=0).astype(jnp.float32)
    return looked + timestep_features(steps_in, class_table.shape[1])


def silu_back(inputs, upstream):
    sigmoid = jax.nn.sigmoid(inputs)
    return upstream * sigmoid * (1.0 + inputs * (1.0 - sigmoid))


def gelu_back(inputs, upstream):
    outputs, pullback = jax.vjp(lambda inner: jax.nn.gelu(inner, approximate=True), inputs)
    return pullback(upstream)[0]


def normalize(inputs):
    centered = inputs - jnp.mean(inputs, axis=-1, keepdims=True)
    inverse = lax.rsqrt(jnp.mean(centered * centered, axis=-1, keepdims=True) + norm_eps)
    return (centered * inverse, inverse)


def norm_back(upstream, normed, inverse):
    return inverse * (
        upstream
        - jnp.mean(upstream, axis=-1, keepdims=True)
        - normed * jnp.mean(upstream * normed, axis=-1, keepdims=True)
    )


def collect(local_rows):
    return lax.all_gather(local_rows, "tensor", axis=1, tiled=True)


def spread(partial_rows):
    return lax.psum_scatter(partial_rows, "tensor", scatter_dimension=1, tiled=True)


def on_device(
    tokens,
    cotangent,
    labels,
    timesteps,
    class_table,
    modulation_weight,
    modulation_bias,
    attend_weight,
    attend_bias,
    output_weight,
    output_bias,
    expand_weight,
    expand_bias,
    reduce_weight,
    reduce_bias,
):
    tensor_count = lax.axis_size("tensor")
    data_index = lax.axis_index("dp")
    tensor_index = lax.axis_index("tensor")
    latent_count = tokens.shape[0]
    model_width = tokens.shape[2]
    row_share = modulation_weight.shape[0]
    head_width = attend_weight.shape[2]
    head_count = head_width // HD
    classes_total = class_table.shape[0]
    score_scale = 1.0 / math.sqrt(HD)
    row_start = data_index * row_share
    zero_index = jnp.zeros((), jnp.int32)
    modulation_full, attend_full, output_full, expand_full, reduce_full = (
        lax.all_gather(modulation_weight, "dp", axis=0, tiled=True),
        lax.all_gather(attend_weight, "dp", axis=0, tiled=True),
        lax.all_gather(output_weight, "dp", axis=0, tiled=True),
        lax.all_gather(expand_weight, "dp", axis=0, tiled=True),
        lax.all_gather(reduce_weight, "dp", axis=0, tiled=True),
    )
    own_labels = lax.dynamic_slice_in_dim(labels, data_index * latent_count, latent_count)
    own_steps = lax.dynamic_slice_in_dim(timesteps, data_index * latent_count, latent_count)
    cond_own = condition(own_labels, own_steps, class_table)
    silu_own = jax.nn.silu(cond_own).astype(jnp.bfloat16)
    modulation_share = jnp.dot(silu_own, modulation_full, preferred_element_type=jnp.float32)
    modulation = lax.all_gather(modulation_share + modulation_bias, "tensor", axis=1, tiled=True)
    pieces = modulation.reshape(latent_count, 6, 1, model_width)
    shift_attend, scale_attend, gate_attend = (pieces[:, 0], pieces[:, 1], pieces[:, 2])
    shift_hidden, scale_hidden, gate_hidden = (pieces[:, 3], pieces[:, 4], pieces[:, 5])
    tokens_wide = tokens.astype(jnp.float32)
    normed_first, inverse_first = normalize(tokens_wide)
    attend_in = (normed_first * (1.0 + scale_attend) + shift_attend).astype(jnp.bfloat16)
    attend_rows = collect(attend_in)
    seq_len = attend_rows.shape[1]
    bias_rows = jnp.stack([attend_bias[0], jnp.zeros_like(attend_bias[0]), attend_bias[1]])
    projected = (
        jnp.einsum("bsd,dje->jbse", attend_rows, attend_full, preferred_element_type=jnp.float32)
        + bias_rows[:, None, None, :]
    ).astype(jnp.bfloat16)
    split_heads = projected.reshape(3, latent_count, seq_len, head_count, HD)
    query_heads, key_heads, value_heads = (split_heads[0], split_heads[1], split_heads[2])
    scores = (
        jnp.einsum("bqhe,bkhe->bhqk", query_heads, key_heads, preferred_element_type=jnp.float32)
        * score_scale
    )
    log_total = jax.nn.logsumexp(scores, axis=-1)
    probs = jnp.exp(scores - log_total[..., None]).astype(jnp.bfloat16)
    mixed = jnp.einsum(
        "bhqk,bkhe->bqhe", probs, value_heads, preferred_element_type=jnp.float32
    ).astype(jnp.bfloat16)
    mixed_rows = mixed.reshape(latent_count, seq_len, head_width)
    attend_out = (
        spread(
            jnp.einsum("bsi,oi->bso", mixed_rows, output_full, preferred_element_type=jnp.float32)
        )
        + output_bias
    )
    residual = tokens_wide + gate_attend * attend_out
    normed_second, inverse_second = normalize(residual)
    hidden_in = (normed_second * (1.0 + scale_hidden) + shift_hidden).astype(jnp.bfloat16)
    hidden_rows = collect(hidden_in)
    pre_act = (
        jnp.einsum("bsd,df->bsf", hidden_rows, expand_full, preferred_element_type=jnp.float32)
        + expand_bias
    )
    activated = jax.nn.gelu(pre_act, approximate=True).astype(jnp.bfloat16)
    hidden_out = (
        spread(
            jnp.einsum("bsf,of->bso", activated, reduce_full, preferred_element_type=jnp.float32)
        )
        + reduce_bias
    )
    block_output = (residual + gate_hidden * hidden_out).astype(jnp.bfloat16)
    upstream = cotangent.astype(jnp.float32)
    grad_gate_hidden = jnp.sum(upstream * hidden_out, axis=1)
    reduce_term = upstream * gate_hidden
    grad_reduce_bias = jnp.sum(reduce_term, axis=(0, 1))
    reduce_rows = collect(reduce_term.astype(jnp.bfloat16))
    grad_act = jnp.einsum(
        "bso,of->bsf", reduce_rows, reduce_full, preferred_element_type=jnp.float32
    )
    grad_reduce = jnp.einsum(
        "bso,bsf->of", reduce_rows, activated, preferred_element_type=jnp.float32
    )
    grad_pre = gelu_back(pre_act, grad_act)
    grad_expand_bias = jnp.sum(grad_pre, axis=(0, 1))
    grad_pre_low = grad_pre.astype(jnp.bfloat16)
    grad_expand = jnp.einsum(
        "bsd,bsf->df", hidden_rows, grad_pre_low, preferred_element_type=jnp.float32
    )
    grad_hidden_in = spread(
        jnp.einsum("bsf,df->bsd", grad_pre_low, expand_full, preferred_element_type=jnp.float32)
    )
    grad_shift_hidden = jnp.sum(grad_hidden_in, axis=1)
    grad_scale_hidden = jnp.sum(grad_hidden_in * normed_second, axis=1)
    grad_residual = upstream + norm_back(
        grad_hidden_in * (1.0 + scale_hidden), normed_second, inverse_second
    )
    grad_gate_attend = jnp.sum(grad_residual * attend_out, axis=1)
    output_term = grad_residual * gate_attend
    grad_output_bias = jnp.sum(output_term, axis=(0, 1))
    output_rows = collect(output_term.astype(jnp.bfloat16))
    grad_output = jnp.einsum(
        "bso,bsi->oi", output_rows, mixed_rows, preferred_element_type=jnp.float32
    )
    grad_mixed = jnp.einsum(
        "bso,oi->bsi", output_rows, output_full, preferred_element_type=jnp.float32
    ).astype(jnp.bfloat16)
    grad_mixed_heads = grad_mixed.reshape(latent_count, seq_len, head_count, HD)
    recomputed = jnp.exp(
        jnp.einsum("bqhe,bkhe->bhqk", query_heads, key_heads, preferred_element_type=jnp.float32)
        * score_scale
        - log_total[..., None]
    )
    row_dot = jnp.einsum(
        "bqhe,bqhe->bhq", grad_mixed_heads, mixed, preferred_element_type=jnp.float32
    )
    grad_probs = jnp.einsum(
        "bqhe,bkhe->bhqk", grad_mixed_heads, value_heads, preferred_element_type=jnp.float32
    )
    grad_logit = (recomputed * (grad_probs - row_dot[..., None])).astype(jnp.bfloat16)
    grad_query = (
        jnp.einsum("bhqk,bkhe->bqhe", grad_logit, key_heads, preferred_element_type=jnp.float32)
        * score_scale
    )
    grad_key = (
        jnp.einsum("bhqk,bqhe->bkhe", grad_logit, query_heads, preferred_element_type=jnp.float32)
        * score_scale
    )
    grad_value = jnp.einsum(
        "bhqk,bqhe->bkhe", probs, grad_mixed_heads, preferred_element_type=jnp.float32
    )
    grad_projected = jnp.stack([grad_query, grad_key, grad_value]).reshape(
        3, latent_count, seq_len, head_width
    )
    grad_attend_bias = jnp.stack(
        [jnp.sum(grad_projected[0], axis=(0, 1)), jnp.sum(grad_projected[2], axis=(0, 1))]
    )
    grad_projected_low = grad_projected.astype(jnp.bfloat16)
    grad_attend = jnp.einsum(
        "bsd,jbse->dje", attend_rows, grad_projected_low, preferred_element_type=jnp.float32
    )
    grad_attend_in = spread(
        jnp.einsum(
            "jbse,dje->bsd", grad_projected_low, attend_full, preferred_element_type=jnp.float32
        )
    )
    grad_shift_attend = jnp.sum(grad_attend_in, axis=1)
    grad_scale_attend = jnp.sum(grad_attend_in * normed_first, axis=1)
    tokens_grad = grad_residual + norm_back(
        grad_attend_in * (1.0 + scale_attend), normed_first, inverse_first
    )
    grad_modulation_rows = jnp.concatenate(
        [
            grad_shift_attend,
            grad_scale_attend,
            grad_gate_attend,
            grad_shift_hidden,
            grad_scale_hidden,
            grad_gate_hidden,
        ],
        axis=1,
    )
    grad_modulation = lax.psum_scatter(
        grad_modulation_rows, "tensor", scatter_dimension=1, tiled=True
    )
    grad_modulation_bias = jnp.sum(grad_modulation, axis=0)
    grad_modulation_low = grad_modulation.astype(jnp.bfloat16)
    grad_modulation_weight = jnp.einsum(
        "ld,lc->dc", silu_own, grad_modulation_low, preferred_element_type=jnp.float32
    )
    grad_modulation_weight, grad_attend, grad_output, grad_expand, grad_reduce = (
        lax.psum_scatter(grad_modulation_weight, "dp", scatter_dimension=0, tiled=True),
        lax.psum_scatter(grad_attend, "dp", scatter_dimension=0, tiled=True),
        lax.psum_scatter(grad_output, "dp", scatter_dimension=0, tiled=True),
        lax.psum_scatter(grad_expand, "dp", scatter_dimension=0, tiled=True),
        lax.psum_scatter(grad_reduce, "dp", scatter_dimension=0, tiled=True),
    )
    grad_silu = jnp.einsum(
        "lc,dc->ld", grad_modulation_low, modulation_full, preferred_element_type=jnp.float32
    )
    grad_cond = silu_back(cond_own, grad_silu)
    shard_rows = lax.all_gather(grad_cond, ("dp", "tensor"), axis=0, tiled=True)
    row_count = shard_rows.shape[0]
    positions = jnp.arange(row_count, dtype=jnp.int32)
    latent_ids = positions // latent_count // tensor_count * latent_count + positions % latent_count
    picked = jnp.take(labels, latent_ids)
    onehot = (picked[:, None] == jnp.arange(classes_total, dtype=jnp.int32)[None, :]).astype(
        jnp.float32
    )
    columns = lax.dynamic_slice_in_dim(shard_rows, row_start, row_share, 1)
    table_grad = jnp.einsum(
        "rc,rd->cd",
        onehot,
        columns,
        precision=lax.Precision.HIGHEST,
        preferred_element_type=jnp.float32,
    )
    expand_share = grad_expand_bias.shape[0]
    modulation_cols = grad_modulation_bias.shape[0]
    padded_attend = lax.dynamic_update_slice(
        jnp.zeros((2, head_width * tensor_count), jnp.float32),
        grad_attend_bias,
        (zero_index, tensor_index * head_width),
    )
    padded_expand = lax.dynamic_update_slice(
        jnp.zeros((expand_share * tensor_count,), jnp.float32),
        grad_expand_bias,
        (tensor_index * expand_share,),
    )
    padded_modulation = lax.dynamic_update_slice(
        jnp.zeros((modulation_cols * tensor_count,), jnp.float32),
        grad_modulation_bias,
        (tensor_index * modulation_cols,),
    )
    summed_attend, summed_expand, summed_modulation, summed_output, summed_reduce = lax.psum(
        (padded_attend, padded_expand, padded_modulation, grad_output_bias, grad_reduce_bias),
        ("dp", "tensor"),
    )
    attend_bias_grad = lax.dynamic_slice_in_dim(
        summed_attend, tensor_index * head_width, head_width, 1
    )
    expand_bias_grad = lax.dynamic_slice_in_dim(
        summed_expand, tensor_index * expand_share, expand_share, 0
    )
    modulation_bias_grad = lax.dynamic_slice_in_dim(
        summed_modulation, tensor_index * modulation_cols, modulation_cols, 0
    )
    return (
        block_output,
        tokens_grad,
        table_grad,
        grad_modulation_weight,
        modulation_bias_grad,
        grad_attend,
        attend_bias_grad,
        grad_output,
        summed_output,
        grad_expand,
        expand_bias_grad,
        grad_reduce,
        summed_reduce,
    )


def swap(values, axis, mask):
    count = lax.axis_size(axis)
    return lax.ppermute(values, axis, [(place, place ^ mask) for place in range(count)])


def unxor(parts, own):
    bit = 1
    while bit < len(parts):
        odd = (own & bit) != 0
        parts = [jnp.where(odd, parts[r ^ bit], parts[r]) for r in range(len(parts))]
        bit *= 2
    return parts


def pick(values, place):
    return lax.dynamic_index_in_dim(values, place, 0, keepdims=False)


def exchange_latents(pair, half):
    return jnp.concatenate([pick(pair, half), swap(pick(pair, 1 - half), "tensor", 2)])


def spread_pairs(own_half, other_half):
    return spread_rows(own_half + swap(other_half, "dp", 1))


def spread_rows(both):
    rows = both.shape[0] // 2
    return both[:rows] + swap(both[rows:].astype(jnp.bfloat16), "tensor", 1).astype(jnp.float32)


def collect_pairs(rows):
    near = swap(rows, "tensor", 1)
    return [rows, near, swap(rows, "dp", 1), swap(near, "dp", 1)]


def after(values, *earlier):
    return lax.optimization_barrier((values,) + earlier)[0]


def near_weight(shard, far, is_own, core):
    mine = jnp.where(is_own, shard, far)
    other = swap(jnp.where(is_own, far, shard), "dp", 1)
    first = core == 0
    return jnp.concatenate(
        [jnp.where(first, mine, other), jnp.where(first, other, mine)], axis=0
    )


def chip_rows(share):
    count = share.shape[0] // 2
    first, second = share[:count], share[count:]
    first_x, second_y = swap(first, "dp", 2), swap(second, "dp", 4)
    first_y = swap(jnp.concatenate([first, first_x]), "dp", 4)
    second_x = swap(jnp.concatenate([second, second_y]), "dp", 2)
    return [share, first_x, second_y, first_y, second_x]


def place_rows(chip, parts, out_refs):
    share, first_x, second_y, first_y, second_x = parts
    count = first_x.shape[0]
    plan = [
        (0, 0, share, 0),
        (0, 1, share, 1),
        (1, 0, first_x, 0),
        (1, 1, second_x, 0),
        (2, 0, first_y, 0),
        (2, 1, second_y, 0),
        (3, 0, first_y, 1),
        (3, 1, second_x, 1),
    ]
    for r, part, source, block in plan:
        target = pl.ds(pl.multiple_of((chip ^ r) * (2 * count) + part * count, 16), count)
        start = 0
        for out_ref in out_refs:
            stop = start + out_ref.shape[1]
            out_ref[target, :] = source[block * count : (block + 1) * count, start:stop]
            start = stop


def dot(left, right, left_dim=1, right_dim=0):
    return lax.dot_general(
        left, right, (((left_dim,), (right_dim,)), ((), ())), preferred_element_type=jnp.float32
    )


def join_rows(pieces, target):
    start = 0
    for piece in pieces:
        target[start : start + piece.shape[0], :] = piece[...]
        start += piece.shape[0]


def attend_probs(query, key, scale):
    scores = dot(query, key, 1, 1) * scale
    top = jnp.max(scores, axis=1, keepdims=True)
    total = jnp.log(jnp.sum(jnp.exp(scores - top), axis=1, keepdims=True)) + top
    return jnp.exp(scores - total)


def attend_forward_body(heads, scale, chip_ref, *refs):
    pieces, mod_ref, bias_ref, parts = refs[:3], refs[3], refs[4], refs[5:10]
    rows_ref, normed_ref, qkv_ref, mixed_ref, attend_ref, output_ref = refs[10:16]
    partials, joined = refs[16:18], refs[18]
    place_rows(chip_ref[0], parts, (attend_ref, output_ref))
    join_rows(pieces, joined)
    seq = joined.shape[0] // 2
    model_width = joined.shape[1]
    width = output_ref.shape[1]
    for n in (1, 0):
        rows = slice(n * seq, (n + 1) * seq)
        normed, _ = normalize(joined[rows, :].astype(jnp.float32))
        normed_ref[rows, :] = normed
        shift = mod_ref[n : n + 1, :model_width]
        gain = mod_ref[n : n + 1, model_width : 2 * model_width]
        attend_in = (normed * (1.0 + gain) + shift).astype(jnp.bfloat16)
        rows_ref[rows, :] = attend_in
        qkv_ref[rows, :] = (dot(attend_in, attend_ref[...]) + bias_ref[...]).astype(jnp.bfloat16)
        mixed = []
        for head in range(heads):
            query, key, value = (
                qkv_ref[rows, j * width + head * HD : j * width + (head + 1) * HD]
                for j in range(3)
            )
            probs = attend_probs(query, key, scale).astype(jnp.bfloat16)
            mixed.append(dot(probs, value))
        mixed = jnp.concatenate(mixed, axis=1).astype(jnp.bfloat16)
        mixed_ref[rows, :] = mixed
        partials[n][...] = dot(mixed, output_ref[...], 1, 1)


def kernel_call(body, name, outs, operands, scratch, limit, flops, transcendentals=0):
    specs = [
        pl.BlockSpec(memory_space=pltpu.SMEM if x.dtype == jnp.int32 else pltpu.VMEM)
        for x in operands
    ]
    shapes = [jax.ShapeDtypeStruct(*out) for out in outs]
    moved = sum(x.size * x.dtype.itemsize for x in list(operands) + shapes)
    return pl.pallas_call(
        body,
        out_shape=shapes,
        in_specs=specs,
        out_specs=[pl.BlockSpec(memory_space=pltpu.VMEM)] * len(outs),
        scratch_shapes=scratch,
        compiler_params=pltpu.CompilerParams(vmem_limit_bytes=limit * 2**20),
        cost_estimate=pl.CostEstimate(
            flops=flops, bytes_accessed=moved, transcendentals=transcendentals
        ),
        name=name,
    )(*operands)


def attend_forward(chip, pieces, mod_full, bias_rows, parts, heads, scale):
    seq = pieces[-1].shape[0]
    rows, model_width = 2 * seq, pieces[0].shape[1]
    width = heads * HD
    return kernel_call(
        functools.partial(attend_forward_body, heads, scale),
        "attend_forward",
        [
            ((rows, model_width), jnp.bfloat16),
            ((rows, model_width), jnp.float32),
            ((rows, 3 * width), jnp.bfloat16),
            ((rows, width), jnp.bfloat16),
            ((model_width, 3 * width), jnp.bfloat16),
            ((model_width, width), jnp.bfloat16),
            ((seq, model_width), jnp.float32),
            ((seq, model_width), jnp.float32),
        ],
        [chip.reshape(1), *pieces, mod_full, bias_rows, *parts],
        [pltpu.VMEM((rows, model_width), jnp.bfloat16)],
        20,
        2 * rows * model_width * 4 * width + 8 * seq * seq * width,
        2 * 2 * heads * seq * seq,
    )


def feed_forward_body(chip_ref, *refs):
    pieces, ups, mod_ref, bias_ref, parts = refs[:4], refs[4:7], refs[7], refs[8], refs[9:14]
    act_ref, sums_ref, reduce_ref = refs[14:17]
    partials, blocks, expand_ref, joined = refs[17:19], refs[19:23], refs[23], refs[24]
    rows_ref, back_ref, low_ref, grad_ref = refs[25:29]
    place_rows(chip_ref[0], parts, (expand_ref, reduce_ref))
    join_rows(pieces, rows_ref)
    join_rows(ups, joined)
    seq = joined.shape[0] // 2
    model_width = joined.shape[1]
    sums = None
    for n in (1, 0):
        rows = slice(n * seq, (n + 1) * seq)
        value = dot(rows_ref[rows, :], expand_ref[...]) + bias_ref[...]
        gate = mod_ref[n : n + 1, 5 * model_width : 6 * model_width]
        back = (joined[rows, :].astype(jnp.float32) * gate).astype(jnp.bfloat16)
        back_ref[rows, :] = back
        grad_act = dot(back, reduce_ref[...])
        square = value * value
        slope = math.sqrt(2.0 / math.pi)
        bent = jnp.tanh(slope * (value + 0.044715 * (square * value)))
        share = 0.5 * (1.0 + bent)
        act_ref[rows, :] = (value * share).astype(jnp.bfloat16)
        curve = 0.5 * value * (1.0 - bent * bent) * (slope * (1.0 + 3 * 0.044715 * square))
        grad_pre = grad_act * (share + curve)
        part = jnp.sum(grad_pre, axis=0, keepdims=True)
        sums = part if sums is None else sums + part
        low = grad_pre.astype(jnp.bfloat16)
        low_ref[rows, :] = low
        partials[n][...] = dot(low, expand_ref[...], 1, 1)
    sums_ref[...] = sums
    width = act_ref.shape[1]
    grad_ref[:, :width] = dot(rows_ref[...], low_ref[...], 0, 0)
    grad_ref[:, width:] = dot(back_ref[...], act_ref[...], 0, 0)
    write_blocks(chip_ref[0], grad_ref, blocks)


def feed_forward(chip, pieces, ups, mod_full, bias, parts):
    seq = ups[-1].shape[0]
    rows, model_width = 2 * seq, pieces[0].shape[1]
    width = bias.shape[1]
    return kernel_call(
        feed_forward_body,
        "feed_forward",
        [
            ((rows, width), jnp.bfloat16),
            ((1, width), jnp.float32),
            ((model_width, width), jnp.bfloat16),
            ((seq, model_width), jnp.float32),
            ((seq, model_width), jnp.float32),
        ]
        + block_shapes(model_width, 2 * width),
        [chip.reshape(1), *pieces, *ups, mod_full, bias, *parts],
        [
            pltpu.VMEM((model_width, width), jnp.bfloat16),
            pltpu.VMEM((rows, model_width), jnp.bfloat16),
            pltpu.VMEM((rows, model_width), jnp.bfloat16),
            pltpu.VMEM((rows, model_width), jnp.bfloat16),
            pltpu.VMEM((rows, width), jnp.bfloat16),
            pltpu.VMEM((model_width, 2 * width), jnp.float32),
        ],
        36,
        10 * rows * model_width * width,
        rows * width,
    )


def write_blocks(chip, grad_ref, out_refs):
    keep_first, keep_second, send_first, send_second = out_refs
    count = keep_first.shape[0] // 2
    plan = [
        (keep_first, 0, (0, 2)),
        (keep_second, 1, (0, 1)),
        (send_first, 0, (1, 3)),
        (send_second, 1, (2, 3)),
    ]
    for out_ref, part, places in plan:
        for block, r in enumerate(places):
            source = pl.ds(pl.multiple_of((chip ^ r) * (2 * count) + part * count, 8), count)
            out_ref[block * count : (block + 1) * count, :] = grad_ref[source, :].astype(
                out_ref.dtype
            )


def block_shapes(height, width):
    shape = (height // 4, width)
    return [(shape, jnp.float32)] * 2 + [(shape, jnp.bfloat16)] * 2


def grad_blocks_body(chip_ref, *refs):
    out_refs, grad_ref = refs[-5:-1], refs[-1]
    start = 0
    for rows, cols in zip(refs[:-5:2], refs[1:-5:2]):
        stop = start + cols.shape[1]
        grad_ref[:, start:stop] = dot(rows[...], cols[...], 0, 0)
        start = stop
    write_blocks(chip_ref[0], grad_ref, out_refs)


def grad_blocks(pairs, chip):
    height = pairs[0][0].shape[1]
    width = sum(cols.shape[1] for _, cols in pairs)
    return kernel_call(
        grad_blocks_body,
        "grad_blocks",
        block_shapes(height, width),
        [chip.reshape(1)] + [part for pair in pairs for part in pair],
        [pltpu.VMEM((height, width), jnp.float32)],
        16,
        sum(2 * rows.size * cols.shape[1] for rows, cols in pairs),
    )


def first_step(sends):
    return [swap(sends[0], "dp", 2), swap(sends[1], "dp", 4)]


def middle_body(keep_first, keep_second, got_first, got_second, *outs):
    count = keep_first.shape[0] // 2
    for keep, got, base, going in (
        (keep_first, got_first, outs[0], outs[2]),
        (keep_second, got_second, outs[1], outs[3]),
    ):
        total = keep[...] + got[...].astype(jnp.float32)
        base[...] = total[:count]
        going[...] = total[count:].astype(jnp.bfloat16)


def middle_step(keeps, received):
    rows, width = keeps[0].shape
    shape = (rows // 2, width)
    outs = [(shape, jnp.float32)] * 2 + [(shape, jnp.bfloat16)] * 2
    return kernel_call(middle_body, "middle_step", outs, [*keeps, *received], [], 16, 0)


def second_step(going):
    return [swap(going[0], "dp", 4), swap(going[1], "dp", 2)]


def core_body(core_ref, base_first, base_second, got_first, got_second, mine, other):
    first = base_first[...] + got_first[...].astype(jnp.float32)
    second = base_second[...] + got_second[...].astype(jnp.float32)
    is_first = core_ref[0] == 0
    mine[...] = jnp.where(is_first, first, second)
    other[...] = jnp.where(is_first, second, first)


def core_step(core, bases, received):
    outs = [(bases[0].shape, jnp.float32)] * 2
    operands = [core.reshape(1), *bases, *received]
    return kernel_call(core_body, "core_step", outs, operands, [], 12, 0)


def half_body(own_ref, mine, other, kept, sent):
    is_own = own_ref[0] == 1
    kept[...] = jnp.where(is_own, mine[...], other[...])
    sent[...] = jnp.where(is_own, other[...], mine[...]).astype(jnp.bfloat16)


def half_step(is_own, mine, other):
    outs = [(mine.shape, jnp.float32), (mine.shape, jnp.bfloat16)]
    operands = [is_own.astype(jnp.int32).reshape(1), mine, other]
    return kernel_call(half_body, "half_step", outs, operands, [], 12, 0)


def pack_body(norm, got, gate_a, shift_m, scale_m, gate_m, out_b, red_b, expand, bias, packed):
    wide = gate_a.shape[1]
    part = packed.shape[1] - wide
    packed[...] = jnp.zeros_like(packed)
    both = norm[0:1, :] + got[...]
    packed[0:1, :wide] = both[:, :wide]
    packed[0:1, wide:] = both[:, wide : wide + part]
    packed[1:2, : wide - part] = both[:, wide + part :]
    packed[1:2, wide - part :] = gate_a[...]
    packed[2:3, :wide] = shift_m[...]
    packed[2:3, wide:] = scale_m[:, :part]
    packed[3:4, : wide - part] = scale_m[:, part:]
    packed[3:4, wide - part :] = gate_m[...]
    packed[4:5, :wide] = out_b[...]
    packed[4:5, wide:] = red_b[:, :part]
    packed[5:6, : wide - part] = red_b[:, part:]
    heads = bias.shape[1] // 3
    packed[6:7, :wide] = expand[...]
    packed[6:7, wide : wide + heads] = bias[:, :heads]
    packed[6:7, wide + heads : wide + 2 * heads] = bias[:, 2 * heads :]


def choose_body(place_ref, line, far, packed):
    z, half, own = place_ref[0], place_ref[1], place_ref[2]
    packed[pl.ds(half, 1), :] = line[pl.ds(z, 1), :]
    packed[pl.ds(1 - half, 1), :] = far[pl.ds(z, 1), :]
    packed[2:3, :] = jnp.where(own == 1, line[6:7, :] + far[6:7, :], 0.0)
    packed[3:5, :] = line[4:6, :] + far[4:6, :]


def modulation_back_body(gathered, silu, weight, weight_grad, grad_silu, bias_grad, rest, rows):
    parts = [gathered[m] for m in range(gathered.shape[0])]
    for m, part in enumerate(parts):
        rows[2 * m : 2 * m + 2, :] = part[0:2, :]
    low = rows[...].astype(jnp.bfloat16)
    weight_grad[...] = dot(silu[...], low, 0, 0)
    grad_silu[...] = dot(low, weight[...], 1, 1)
    while len(parts) > 1:
        parts = [left + right for left, right in zip(parts[::2], parts[1::2])]
    bias_grad[...] = parts[0][0:1, :] + parts[0][1:2, :]
    rest[...] = parts[0][2:5, :]


def table_body(labels, cond, near, far, table):
    value = cond[...]
    share = 1.0 / (1.0 + jnp.exp(-value))
    grad = (near[...] + far[...]) * share * (1.0 + value * (1.0 - share))
    table[...] = jnp.zeros_like(table)
    for row in range(grad.shape[0]):
        place = pl.ds(labels[row], 1)
        table[place, :] = table[place, :] + grad[row : row + 1, :]


def attend_back_body(heads, scale, *refs):
    pieces = refs[:4]
    output_ref, qkv_ref, mixed_ref, attend_ref, normed_ref = refs[4:9]
    rows_ref, low_ref, sums_ref, norm_sums_ref = refs[9:13]
    partials = refs[13:15]
    join_rows(pieces, rows_ref)
    seq = rows_ref.shape[0] // 2
    model_width, width = output_ref.shape
    sums = None
    for n in (1, 0):
        rows = slice(n * seq, (n + 1) * seq)
        grad_mixed = dot(rows_ref[rows, :], output_ref[...]).astype(jnp.bfloat16)
        grads = [[], [], []]
        for head in range(heads):
            query, key, value = (
                qkv_ref[rows, j * width + head * HD : j * width + (head + 1) * HD]
                for j in range(3)
            )
            mixed = mixed_ref[rows, head * HD : (head + 1) * HD]
            up = grad_mixed[:, head * HD : (head + 1) * HD]
            probs = attend_probs(query, key, scale)
            delta = jnp.sum(
                up.astype(jnp.float32) * mixed.astype(jnp.float32), axis=1, keepdims=True
            )
            logit = (probs * (dot(up, value, 1, 1) - delta)).astype(jnp.bfloat16)
            grads[0].append(dot(logit, key) * scale)
            grads[1].append(dot(logit, query, 0, 0) * scale)
            grads[2].append(dot(probs.astype(jnp.bfloat16), up, 0, 0))
        whole = jnp.concatenate([part for group in grads for part in group], axis=1)
        part = jnp.sum(whole, axis=0, keepdims=True)
        sums = part if sums is None else sums + part
        low = whole.astype(jnp.bfloat16)
        low_ref[rows, :] = low
        partial = dot(low, attend_ref[...], 1, 1)
        partials[n][...] = partial
        norm_sums_ref[n : n + 1, :model_width] = jnp.sum(partial, axis=0, keepdims=True)
        norm_sums_ref[n : n + 1, model_width:] = jnp.sum(
            partial * normed_ref[rows, :], axis=0, keepdims=True
        )
    sums_ref[...] = sums


def attend_back(pieces, output_full, qkv, mixed, attend_full, normed, heads, scale):
    rows, model_width = normed.shape
    seq, width = rows // 2, mixed.shape[1]
    return kernel_call(
        functools.partial(attend_back_body, heads, scale),
        "attend_back",
        [
            ((rows, model_width), jnp.bfloat16),
            ((rows, 3 * width), jnp.bfloat16),
            ((1, 3 * width), jnp.float32),
            ((2, 2 * model_width), jnp.float32),
            ((seq, model_width), jnp.float32),
            ((seq, model_width), jnp.float32),
        ],
        [*pieces, output_full, qkv, mixed, attend_full, normed],
        [],
        20,
        2 * rows * model_width * 4 * width + 20 * seq * seq * width,
        2 * 2 * heads * seq * seq,
    )


def on_paired_device(
    tokens,
    cotangent,
    labels,
    timesteps,
    class_table,
    modulation_weight,
    modulation_bias,
    attend_weight,
    attend_bias,
    output_weight,
    output_bias,
    expand_weight,
    expand_bias,
    reduce_weight,
    reduce_bias,
):
    data_index = lax.axis_index("dp")
    tensor_index = lax.axis_index("tensor")
    core, chip = data_index & 1, data_index >> 1
    half = tensor_index >> 1
    is_own = half == core
    model_width = tokens.shape[2]
    row_share = modulation_weight.shape[0]
    head_width = attend_weight.shape[2]
    head_count = head_width // HD
    ff_width = expand_weight.shape[1]
    mod_width = modulation_weight.shape[1]
    latent_total = labels.shape[0]
    classes_total = class_table.shape[0]
    score_scale = 1.0 / math.sqrt(HD)

    slot = jnp.arange(latent_total, dtype=jnp.int32)
    latent_ids = ((slot >> 1) ^ data_index) * 2 + (slot & 1)
    chosen = latent_ids[:, None] == slot[None, :]
    labels_rel = jnp.sum(jnp.where(chosen, labels[None, :], 0), axis=1)
    steps_rel = jnp.sum(jnp.where(chosen, timesteps[None, :], 0), axis=1)
    looked = lax.dynamic_slice_in_dim(
        jnp.take(class_table, labels_rel, axis=0), data_index * row_share, row_share, 1
    ).astype(jnp.float32)
    halfway = model_width // 2
    column = data_index * row_share + jnp.arange(row_share, dtype=jnp.int32)
    is_cos = column < halfway
    place = jnp.where(is_cos, column, column - halfway).astype(jnp.float32)
    frequency = jnp.exp(-math.log(10000.0) * place / halfway)
    angles = steps_rel.astype(jnp.float32)[:, None] * frequency[None, :]
    cond = looked + jnp.where(is_cos[None, :], jnp.cos(angles), jnp.sin(angles))
    silu_act = jax.nn.silu(cond).astype(jnp.bfloat16)
    partial = jnp.dot(silu_act, modulation_weight, preferred_element_type=jnp.float32)
    attn_shard = jnp.concatenate([attend_weight.reshape(row_share, -1), output_weight], axis=1)
    attn_far = swap(attn_shard, "tensor", 2)
    attn_share = near_weight(attn_shard, attn_far, is_own, core)
    partial = partial[:8] + swap(partial[8:], "dp", 4)
    partial = partial[:4] + swap(after(partial, attn_far)[4:], "dp", 2)
    crossed = swap(after(partial, attn_share), "dp", 1)
    bias_vec = jnp.concatenate([attend_bias.reshape(-1), expand_bias])
    mod_cols = jnp.concatenate(
        [
            partial + jnp.concatenate([crossed[2:], crossed[:2]]) + modulation_bias,
            bias_vec[None],
        ]
    )
    mod_near = jnp.stack([mod_cols, swap(mod_cols, "tensor", 1)])
    mod_far = swap(mod_near, "tensor", 2)
    mod_parts = [mod_near[0], mod_near[1], mod_far[0], mod_far[1]]
    mod_full = jnp.concatenate(
        unxor([jnp.where(half == 0, m[0:4:2], m[1:4:2]) for m in mod_parts], tensor_index), axis=1
    )
    bias_vec = jnp.where(is_own, bias_vec, mod_parts[2][4])
    pieces = mod_full.reshape(2, 6, 1, model_width)
    own_pieces = pieces[0]

    tokens_half = exchange_latents(after(tokens, attn_shard), half)
    own_rows = tokens_half.shape[0]
    tokens_near = swap(tokens_half, "tensor", 1)
    tokens_across = swap(jnp.concatenate([tokens_half, tokens_near]), "dp", 1)
    tokens_own = tokens_half.astype(jnp.float32)

    attn_parts = chip_rows(attn_share)
    ff_shard = after(
        jnp.concatenate([expand_weight, reduce_weight], axis=1), attn_far, tokens_half
    )
    ff_far = swap(ff_shard, "tensor", 2)
    ff_share = near_weight(ff_shard, ff_far, is_own, core)
    ff_parts = chip_rows(after(ff_share, *attn_parts))

    upstream_half = exchange_latents(after(cotangent, mod_far), half)
    upstream_near = swap(upstream_half, "tensor", 1)
    upstream_across = swap(jnp.concatenate([upstream_half, upstream_near]), "dp", 1)
    upstream = upstream_half.astype(jnp.float32)
    query_bias = bias_vec[:head_width]
    value_bias = bias_vec[head_width : 2 * head_width]
    expand_bias_q = bias_vec[2 * head_width :]

    bias_rows = jnp.concatenate([query_bias, jnp.zeros_like(query_bias), value_bias])[None]
    (
        attend_rows,
        normed_all,
        projected,
        mixed_rows,
        attend_full,
        output_full,
        own_partial,
        other_partial,
    ) = attend_forward(
        chip,
        [tokens_half, tokens_near, tokens_across],
        mod_full,
        bias_rows,
        attn_parts,
        head_count,
        score_scale,
    )
    attend_out = spread_pairs(own_partial, other_partial) + output_bias
    normed_first, inverse_first = normalize(tokens_own)
    residual = tokens_own + own_pieces[2] * attend_out
    normed_second, inverse_second = normalize(residual)
    hidden_in = (normed_second * (1.0 + own_pieces[4]) + own_pieces[3]).astype(jnp.bfloat16)
    hidden_pieces = collect_pairs(hidden_in)

    (
        activated,
        grad_expand_bias,
        reduce_full,
        own_partial,
        other_partial,
        *ff_blocks,
    ) = feed_forward(
        chip,
        hidden_pieces,
        [upstream_half, upstream_near, upstream_across],
        mod_full,
        expand_bias_q[None],
        ff_parts,
    )
    ff_first = first_step(ff_blocks[2:])
    grad_reduce_bias = jnp.sum(upstream * own_pieces[5], axis=0, keepdims=True)
    seq_len = tokens_across.shape[0]
    hidden_sum = own_partial + swap(other_partial, "dp", 1)
    grad_hidden_in = spread_rows(hidden_sum)
    act_later = after(activated, own_partial)
    other_out, own_out = (
        jnp.einsum("sf,of->so", act_half, reduce_full, preferred_element_type=jnp.float32)
        for act_half in (act_later[seq_len:], act_later[:seq_len])
    )
    out_sum = own_out + swap(other_out, "dp", 1)

    grad_shift_hidden = jnp.sum(grad_hidden_in, axis=0, keepdims=True)
    grad_scale_hidden = jnp.sum(grad_hidden_in * normed_second, axis=0, keepdims=True)
    grad_residual = upstream + norm_back(
        grad_hidden_in * (1.0 + own_pieces[4]), normed_second, inverse_second
    )
    grad_gate_attend = jnp.sum(grad_residual * attend_out, axis=0, keepdims=True)
    output_term = grad_residual * own_pieces[2]
    grad_output_bias = jnp.sum(output_term, axis=0, keepdims=True)
    output_pieces = collect_pairs(output_term.astype(jnp.bfloat16))
    *ff_bases, ff_going, ff_going_second = middle_step(ff_blocks[:2], after(ff_first, output_term))
    ff_second = second_step([ff_going, ff_going_second])
    hidden_out = spread_rows(after(out_sum, output_term)) + reduce_bias
    block_own = (residual + own_pieces[5] * hidden_out).astype(jnp.bfloat16)
    grad_gate_hidden = jnp.sum(upstream * hidden_out, axis=0, keepdims=True)

    (
        output_rows,
        projected_low,
        bias_sums,
        norm_sums,
        own_partial,
        other_partial,
    ) = attend_back(
        after(output_pieces, out_sum, ff_going),
        output_full,
        projected,
        mixed_rows,
        attend_full,
        normed_all,
        head_count,
        score_scale,
    )
    attend_sum = own_partial + swap(other_partial, "dp", 1)
    norm_crossed = swap(norm_sums[1:], "dp", 1)
    grad_attend_in = spread_rows(attend_sum)
    attn_blocks = grad_blocks(
        [(attend_rows, after(projected_low, norm_crossed)), (output_rows, mixed_rows)], chip
    )
    attn_first = first_step(attn_blocks[2:])
    tokens_grad_own = grad_residual + norm_back(
        grad_attend_in * (1.0 + own_pieces[1]), normed_first, inverse_first
    )

    count = tokens_grad_own.shape[0] // 2
    far = swap(
        jnp.concatenate([block_own[count:], tokens_grad_own[count:].astype(jnp.bfloat16)]),
        "tensor",
        2,
    )
    block_output, tokens_grad = (
        jnp.where(half == 0, jnp.stack([own, moved]), jnp.stack([moved, own]))
        for own, moved in (
            (block_own[:count], far[:count]),
            (tokens_grad_own[:count], far[count:].astype(jnp.float32)),
        )
    )

    line = kernel_call(
        pack_body,
        "pack",
        [((8, mod_width), jnp.float32)],
        [
            norm_sums,
            norm_crossed,
            grad_gate_attend,
            grad_shift_hidden,
            grad_scale_hidden,
            grad_gate_hidden,
            grad_output_bias,
            grad_reduce_bias,
            grad_expand_bias,
            bias_sums,
        ],
        [],
        4,
        0,
    )[0]
    summed = lax.broadcasted_iota(jnp.int32, line.shape, 0) < 6
    line = line + jnp.where(summed, swap(line, "tensor", 1), 0.0)
    far = swap(line, "tensor", 2)
    ff_mine, ff_other = core_step(core, ff_bases, ff_second)
    ff_kept, ff_sent = half_step(is_own, ff_mine, swap(ff_other, "dp", 1))
    ff_moved = swap(after(ff_sent, far), "tensor", 2)
    place = jnp.stack([tensor_index, half, is_own.astype(jnp.int32)])
    packed = kernel_call(
        choose_body, "choose", [((5, mod_width), jnp.float32)], [place, line, far], [], 4, 0
    )[0][None]
    packed = jnp.concatenate([packed, swap(packed, "dp", 1)], axis=0)
    *attn_bases, attn_going, attn_going_second = middle_step(attn_blocks[:2], attn_first)
    packed = after(packed, attn_going, grad_attend_in, ff_sent)
    packed = jnp.concatenate([packed, swap(packed, "dp", 2)], axis=0)
    attn_second = second_step([attn_going, attn_going_second])
    packed = jnp.concatenate([packed, swap(packed, "dp", 4)], axis=0)
    modulation_weight_grad, grad_silu, modulation_bias_grad, rest = kernel_call(
        modulation_back_body,
        "modulation_back",
        [
            ((row_share, mod_width), jnp.float32),
            ((latent_total, row_share), jnp.float32),
            ((1, mod_width), jnp.float32),
            ((3, mod_width), jnp.float32),
        ],
        [packed, silu_act, modulation_weight],
        [pltpu.VMEM((latent_total, mod_width), jnp.float32)],
        8,
        4 * latent_total * row_share * mod_width,
    )
    attn_mine, attn_other = core_step(core, attn_bases, attn_second)
    grad_silu = after(grad_silu, attn_mine, tokens_grad_own)
    near = grad_silu + swap(grad_silu, "tensor", 1)
    attn_kept, attn_sent = half_step(is_own, attn_mine, swap(attn_other, "dp", 1))
    attn_grad = attn_kept + swap(attn_sent, "tensor", 2).astype(jnp.float32)
    ff_grad = ff_kept + after(ff_moved, near).astype(jnp.float32)
    table_grad = kernel_call(
        table_body,
        "table",
        [((classes_total, row_share), jnp.float32)],
        [labels_rel, cond, near, swap(near, "tensor", 2)],
        [],
        4,
        0,
    )[0]
    wide = model_width
    return (
        block_output,
        tokens_grad,
        table_grad,
        modulation_weight_grad,
        modulation_bias_grad[0],
        attn_grad[:, : 3 * head_width].reshape(row_share, 3, head_width),
        rest[0, wide:].reshape(2, head_width),
        attn_grad[:, 3 * head_width :],
        rest[1, :wide],
        ff_grad[:, :ff_width],
        rest[0, :wide],
        ff_grad[:, ff_width:],
        jnp.concatenate([rest[1, wide:], rest[2, : 2 * wide - mod_width]]),
    )


def solution(mesh):
    paired = mesh.shape["dp"] == 8 and mesh.shape["tensor"] == 4
    per_device = on_paired_device if paired else on_device
    placed = (
        P("dp", "tensor", None),
        P("dp", "tensor", None),
        P(),
        P(),
        P(),
        P("dp", "tensor"),
        P("tensor"),
        P("dp", None, "tensor"),
        P(None, "tensor"),
        P("dp", "tensor"),
        P(),
        P("dp", "tensor"),
        P("tensor"),
        P("dp", "tensor"),
        P(),
    )
    return jax.shard_map(
        per_device,
        mesh=mesh,
        in_specs=placed,
        out_specs=(
            P("dp", "tensor", None),
            P("dp", "tensor", None),
            P(None, "dp"),
            P("dp", "tensor"),
            P("tensor"),
            P("dp", None, "tensor"),
            P(None, "tensor"),
            P("dp", "tensor"),
            P(),
            P("dp", "tensor"),
            P("tensor"),
            P("dp", "tensor"),
            P(),
        ),
        check_vma=False,
    )
```

```python
import functools
import math

import jax
import jax.numpy as jnp
from jax import lax
from jax.experimental import pallas as pl
from jax.experimental.pallas import tpu as pltpu
from jax.sharding import PartitionSpec as P

HD = 64


norm_eps = 1e-06


def timestep_features(steps_in, model_width):
    halfway = model_width // 2
    frequency = jnp.exp(-math.log(10000.0) * jnp.arange(halfway, dtype=jnp.float32) / halfway)
    angles = steps_in.astype(jnp.float32)[:, None] * frequency[None, :]
    return jnp.concatenate([jnp.cos(angles), jnp.sin(angles)], axis=1)


def condition(label_ids, steps_in, class_table):
    looked = jnp.take(class_table, label_ids, axis=0).astype(jnp.float32)
    return looked + timestep_features(steps_in, class_table.shape[1])


def silu_back(inputs, upstream):
    sigmoid = jax.nn.sigmoid(inputs)
    return upstream * sigmoid * (1.0 + inputs * (1.0 - sigmoid))


def gelu_back(inputs, upstream):
    outputs, pullback = jax.vjp(lambda inner: jax.nn.gelu(inner, approximate=True), inputs)
    return pullback(upstream)[0]


def normalize(inputs):
    centered = inputs - jnp.mean(inputs, axis=-1, keepdims=True)
    inverse = lax.rsqrt(jnp.mean(centered * centered, axis=-1, keepdims=True) + norm_eps)
    return (centered * inverse, inverse)


def norm_back(upstream, normed, inverse):
    return inverse * (
        upstream
        - jnp.mean(upstream, axis=-1, keepdims=True)
        - normed * jnp.mean(upstream * normed, axis=-1, keepdims=True)
    )


def collect(local_rows):
    return lax.all_gather(local_rows, "tensor", axis=1, tiled=True)


def spread(partial_rows):
    return lax.psum_scatter(partial_rows, "tensor", scatter_dimension=1, tiled=True)


def on_device(
    tokens,
    cotangent,
    labels,
    timesteps,
    class_table,
    modulation_weight,
    modulation_bias,
    attend_weight,
    attend_bias,
    output_weight,
    output_bias,
    expand_weight,
    expand_bias,
    reduce_weight,
    reduce_bias,
):
    tensor_count = lax.axis_size("tensor")
    data_index = lax.axis_index("dp")
    tensor_index = lax.axis_index("tensor")
    latent_count = tokens.shape[0]
    model_width = tokens.shape[2]
    row_share = modulation_weight.shape[0]
    head_width = attend_weight.shape[2]
    head_count = head_width // HD
    classes_total = class_table.shape[0]
    score_scale = 1.0 / math.sqrt(HD)
    row_start = data_index * row_share
    zero_index = jnp.zeros((), jnp.int32)
    modulation_full, attend_full, output_full, expand_full, reduce_full = (
        lax.all_gather(modulation_weight, "dp", axis=0, tiled=True),
        lax.all_gather(attend_weight, "dp", axis=0, tiled=True),
        lax.all_gather(output_weight, "dp", axis=0, tiled=True),
        lax.all_gather(expand_weight, "dp", axis=0, tiled=True),
        lax.all_gather(reduce_weight, "dp", axis=0, tiled=True),
    )
    own_labels = lax.dynamic_slice_in_dim(labels, data_index * latent_count, latent_count)
    own_steps = lax.dynamic_slice_in_dim(timesteps, data_index * latent_count, latent_count)
    cond_own = condition(own_labels, own_steps, class_table)
    silu_own = jax.nn.silu(cond_own).astype(jnp.bfloat16)
    modulation_share = jnp.dot(silu_own, modulation_full, preferred_element_type=jnp.float32)
    modulation = lax.all_gather(modulation_share + modulation_bias, "tensor", axis=1, tiled=True)
    pieces = modulation.reshape(latent_count, 6, 1, model_width)
    shift_attend, scale_attend, gate_attend = (pieces[:, 0], pieces[:, 1], pieces[:, 2])
    shift_hidden, scale_hidden, gate_hidden = (pieces[:, 3], pieces[:, 4], pieces[:, 5])
    tokens_wide = tokens.astype(jnp.float32)
    normed_first, inverse_first = normalize(tokens_wide)
    attend_in = (normed_first * (1.0 + scale_attend) + shift_attend).astype(jnp.bfloat16)
    attend_rows = collect(attend_in)
    seq_len = attend_rows.shape[1]
    bias_rows = jnp.stack([attend_bias[0], jnp.zeros_like(attend_bias[0]), attend_bias[1]])
    projected = (
        jnp.einsum("bsd,dje->jbse", attend_rows, attend_full, preferred_element_type=jnp.float32)
        + bias_rows[:, None, None, :]
    ).astype(jnp.bfloat16)
    split_heads = projected.reshape(3, latent_count, seq_len, head_count, HD)
    query_heads, key_heads, value_heads = (split_heads[0], split_heads[1], split_heads[2])
    scores = (
        jnp.einsum("bqhe,bkhe->bhqk", query_heads, key_heads, preferred_element_type=jnp.float32)
        * score_scale
    )
    log_total = jax.nn.logsumexp(scores, axis=-1)
    probs = jnp.exp(scores - log_total[..., None]).astype(jnp.bfloat16)
    mixed = jnp.einsum(
        "bhqk,bkhe->bqhe", probs, value_heads, preferred_element_type=jnp.float32
    ).astype(jnp.bfloat16)
    mixed_rows = mixed.reshape(latent_count, seq_len, head_width)
    attend_out = (
        spread(
            jnp.einsum("bsi,oi->bso", mixed_rows, output_full, preferred_element_type=jnp.float32)
        )
        + output_bias
    )
    residual = tokens_wide + gate_attend * attend_out
    normed_second, inverse_second = normalize(residual)
    hidden_in = (normed_second * (1.0 + scale_hidden) + shift_hidden).astype(jnp.bfloat16)
    hidden_rows = collect(hidden_in)
    pre_act = (
        jnp.einsum("bsd,df->bsf", hidden_rows, expand_full, preferred_element_type=jnp.float32)
        + expand_bias
    )
    activated = jax.nn.gelu(pre_act, approximate=True).astype(jnp.bfloat16)
    hidden_out = (
        spread(
            jnp.einsum("bsf,of->bso", activated, reduce_full, preferred_element_type=jnp.float32)
        )
        + reduce_bias
    )
    block_output = (residual + gate_hidden * hidden_out).astype(jnp.bfloat16)
    upstream = cotangent.astype(jnp.float32)
    grad_gate_hidden = jnp.sum(upstream * hidden_out, axis=1)
    reduce_term = upstream * gate_hidden
    grad_reduce_bias = jnp.sum(reduce_term, axis=(0, 1))
    reduce_rows = collect(reduce_term.astype(jnp.bfloat16))
    grad_act = jnp.einsum(
        "bso,of->bsf", reduce_rows, reduce_full, preferred_element_type=jnp.float32
    )
    grad_reduce = jnp.einsum(
        "bso,bsf->of", reduce_rows, activated, preferred_element_type=jnp.float32
    )
    grad_pre = gelu_back(pre_act, grad_act)
    grad_expand_bias = jnp.sum(grad_pre, axis=(0, 1))
    grad_pre_low = grad_pre.astype(jnp.bfloat16)
    grad_expand = jnp.einsum(
        "bsd,bsf->df", hidden_rows, grad_pre_low, preferred_element_type=jnp.float32
    )
    grad_hidden_in = spread(
        jnp.einsum("bsf,df->bsd", grad_pre_low, expand_full, preferred_element_type=jnp.float32)
    )
    grad_shift_hidden = jnp.sum(grad_hidden_in, axis=1)
    grad_scale_hidden = jnp.sum(grad_hidden_in * normed_second, axis=1)
    grad_residual = upstream + norm_back(
        grad_hidden_in * (1.0 + scale_hidden), normed_second, inverse_second
    )
    grad_gate_attend = jnp.sum(grad_residual * attend_out, axis=1)
    output_term = grad_residual * gate_attend
    grad_output_bias = jnp.sum(output_term, axis=(0, 1))
    output_rows = collect(output_term.astype(jnp.bfloat16))
    grad_output = jnp.einsum(
        "bso,bsi->oi", output_rows, mixed_rows, preferred_element_type=jnp.float32
    )
    grad_mixed = jnp.einsum(
        "bso,oi->bsi", output_rows, output_full, preferred_element_type=jnp.float32
    ).astype(jnp.bfloat16)
    grad_mixed_heads = grad_mixed.reshape(latent_count, seq_len, head_count, HD)
    recomputed = jnp.exp(
        jnp.einsum("bqhe,bkhe->bhqk", query_heads, key_heads, preferred_element_type=jnp.float32)
        * score_scale
        - log_total[..., None]
    )
    row_dot = jnp.einsum(
        "bqhe,bqhe->bhq", grad_mixed_heads, mixed, preferred_element_type=jnp.float32
    )
    grad_probs = jnp.einsum(
        "bqhe,bkhe->bhqk", grad_mixed_heads, value_heads, preferred_element_type=jnp.float32
    )
    grad_logit = (recomputed * (grad_probs - row_dot[..., None])).astype(jnp.bfloat16)
    grad_query = (
        jnp.einsum("bhqk,bkhe->bqhe", grad_logit, key_heads, preferred_element_type=jnp.float32)
        * score_scale
    )
    grad_key = (
        jnp.einsum("bhqk,bqhe->bkhe", grad_logit, query_heads, preferred_element_type=jnp.float32)
        * score_scale
    )
    grad_value = jnp.einsum(
        "bhqk,bqhe->bkhe", probs, grad_mixed_heads, preferred_element_type=jnp.float32
    )
    grad_projected = jnp.stack([grad_query, grad_key, grad_value]).reshape(
        3, latent_count, seq_len, head_width
    )
    grad_attend_bias = jnp.stack(
        [jnp.sum(grad_projected[0], axis=(0, 1)), jnp.sum(grad_projected[2], axis=(0, 1))]
    )
    grad_projected_low = grad_projected.astype(jnp.bfloat16)
    grad_attend = jnp.einsum(
        "bsd,jbse->dje", attend_rows, grad_projected_low, preferred_element_type=jnp.float32
    )
    grad_attend_in = spread(
        jnp.einsum(
            "jbse,dje->bsd", grad_projected_low, attend_full, preferred_element_type=jnp.float32
        )
    )
    grad_shift_attend = jnp.sum(grad_attend_in, axis=1)
    grad_scale_attend = jnp.sum(grad_attend_in * normed_first, axis=1)
    tokens_grad = grad_residual + norm_back(
        grad_attend_in * (1.0 + scale_attend), normed_first, inverse_first
    )
    grad_modulation_rows = jnp.concatenate(
        [
            grad_shift_attend,
            grad_scale_attend,
            grad_gate_attend,
            grad_shift_hidden,
            grad_scale_hidden,
            grad_gate_hidden,
        ],
        axis=1,
    )
    grad_modulation = lax.psum_scatter(
        grad_modulation_rows, "tensor", scatter_dimension=1, tiled=True
    )
    grad_modulation_bias = jnp.sum(grad_modulation, axis=0)
    grad_modulation_low = grad_modulation.astype(jnp.bfloat16)
    grad_modulation_weight = jnp.einsum(
        "ld,lc->dc", silu_own, grad_modulation_low, preferred_element_type=jnp.float32
    )
    grad_modulation_weight, grad_attend, grad_output, grad_expand, grad_reduce = (
        lax.psum_scatter(grad_modulation_weight, "dp", scatter_dimension=0, tiled=True),
        lax.psum_scatter(grad_attend, "dp", scatter_dimension=0, tiled=True),
        lax.psum_scatter(grad_output, "dp", scatter_dimension=0, tiled=True),
        lax.psum_scatter(grad_expand, "dp", scatter_dimension=0, tiled=True),
        lax.psum_scatter(grad_reduce, "dp", scatter_dimension=0, tiled=True),
    )
    grad_silu = jnp.einsum(
        "lc,dc->ld", grad_modulation_low, modulation_full, preferred_element_type=jnp.float32
    )
    grad_cond = silu_back(cond_own, grad_silu)
    shard_rows = lax.all_gather(grad_cond, ("dp", "tensor"), axis=0, tiled=True)
    row_count = shard_rows.shape[0]
    positions = jnp.arange(row_count, dtype=jnp.int32)
    latent_ids = positions // latent_count // tensor_count * latent_count + positions % latent_count
    picked = jnp.take(labels, latent_ids)
    onehot = (picked[:, None] == jnp.arange(classes_total, dtype=jnp.int32)[None, :]).astype(
        jnp.float32
    )
    columns = lax.dynamic_slice_in_dim(shard_rows, row_start, row_share, 1)
    table_grad = jnp.einsum(
        "rc,rd->cd",
        onehot,
        columns,
        precision=lax.Precision.HIGHEST,
        preferred_element_type=jnp.float32,
    )
    expand_share = grad_expand_bias.shape[0]
    modulation_cols = grad_modulation_bias.shape[0]
    padded_attend = lax.dynamic_update_slice(
        jnp.zeros((2, head_width * tensor_count), jnp.float32),
        grad_attend_bias,
        (zero_index, tensor_index * head_width),
    )
    padded_expand = lax.dynamic_update_slice(
        jnp.zeros((expand_share * tensor_count,), jnp.float32),
        grad_expand_bias,
        (tensor_index * expand_share,),
    )
    padded_modulation = lax.dynamic_update_slice(
        jnp.zeros((modulation_cols * tensor_count,), jnp.float32),
        grad_modulation_bias,
        (tensor_index * modulation_cols,),
    )
    summed_attend, summed_expand, summed_modulation, summed_output, summed_reduce = lax.psum(
        (padded_attend, padded_expand, padded_modulation, grad_output_bias, grad_reduce_bias),
        ("dp", "tensor"),
    )
    attend_bias_grad = lax.dynamic_slice_in_dim(
        summed_attend, tensor_index * head_width, head_width, 1
    )
    expand_bias_grad = lax.dynamic_slice_in_dim(
        summed_expand, tensor_index * expand_share, expand_share, 0
    )
    modulation_bias_grad = lax.dynamic_slice_in_dim(
        summed_modulation, tensor_index * modulation_cols, modulation_cols, 0
    )
    return (
        block_output,
        tokens_grad,
        table_grad,
        grad_modulation_weight,
        modulation_bias_grad,
        grad_attend,
        attend_bias_grad,
        grad_output,
        summed_output,
        grad_expand,
        expand_bias_grad,
        grad_reduce,
        summed_reduce,
    )


def swap(values, axis, mask):
    count = lax.axis_size(axis)
    return lax.ppermute(values, axis, [(place, place ^ mask) for place in range(count)])


def pick(values, place):
    return lax.dynamic_index_in_dim(values, place, 0, keepdims=False)


def collect_pairs(rows):
    near = swap(rows, "tensor", 1)
    return [rows, near, swap(rows, "dp", 1), swap(near, "dp", 1)]


(
    ACTIVATED,
    ATTEND,
    ATTEND_BACK,
    ATTEND_SEND,
    ATTN_BLOCKS,
    ATTN_CORE,
    ATTN_FAR,
    ATTN_HALF,
    ATTN_OWNER,
    ATTN_PARTS,
    ATTN_SHARD,
    ATTN_SHARE,
    BACK_SENT,
    BLOCK_MOVED,
    BLOCK_OUT,
    FAR,
    FEED,
    FEED_SEND,
    FF_BLOCKS,
    FF_CORE,
    FF_FAR,
    FF_GOING,
    FF_HALF,
    FF_MIDDLE,
    FF_MOVED,
    FF_OWNER,
    FF_SECOND,
    FF_SHARE,
    GRAD_SILU,
    HIDDEN_BACK,
    LINE,
    LINE_FAR,
    LINE_NEAR,
    MOD_LINE,
    MOD_PLACE,
    MODULATION_BACK,
    NEAR,
    NORM_CROSSED,
    OUT_SEND,
    OUTPUT_NEAR,
    OUTPUTS,
    PACK,
    PACKED_X,
    PACKED_Y,
    PARTIAL_CORE,
    RESIDUAL,
    TABLE,
    TOKENS_HALF,
    TOKENS_SENT,
    UPSTREAM_HALF,
    UPSTREAM_SENT,
) = range(51)

HOLDS = {
    TOKENS_SENT: (ATTN_SHARD,),
    PARTIAL_CORE: (ATTN_FAR, ATTN_SHARE, TOKENS_HALF,),
    MOD_PLACE: (ATTN_PARTS,),
    FF_FAR: (MOD_LINE,),
    UPSTREAM_SENT: (FF_FAR, FF_SHARE,),
    ATTEND: (FF_SHARE,),
    FF_SECOND: (ATTEND_SEND,),
    RESIDUAL: (UPSTREAM_HALF,),
    FF_BLOCKS: (FEED_SEND,),
    ACTIVATED: (FEED,),
    HIDDEN_BACK: (OUT_SEND,),
    FF_MIDDLE: (BLOCK_OUT, OUTPUT_NEAR,),
    ATTEND_BACK: (BLOCK_OUT, FF_GOING,),
    BLOCK_MOVED: (OUTPUT_NEAR,),
    PACK: (FF_CORE,),
    ATTN_BLOCKS: (PACK,),
    LINE_NEAR: (FF_CORE,),
    LINE: (FF_HALF,),
    LINE_FAR: (ATTN_BLOCKS, FF_HALF,),
    FF_CORE: (NORM_CROSSED,),
    BACK_SENT: (FAR,),
    PACKED_X: (FF_CORE, FF_HALF,),
    PACKED_Y: (FF_MOVED,),
    MODULATION_BACK: (ATTN_CORE,),
    ATTN_HALF: (MODULATION_BACK,),
    GRAD_SILU: (FF_MOVED,),
    FF_OWNER: (NEAR,),
    ATTN_OWNER: (TABLE,),
    OUTPUTS: (MODULATION_BACK,),
}


class Order:
    def __init__(self):
        self.marks = {}

    def mark(self, name, values):
        self.marks[name] = values
        return values

    def hold(self, name, values):
        earlier = [self.marks[mark] for mark in HOLDS.get(name, ())]
        return lax.optimization_barrier((values, earlier))[0] if earlier else values


def near_weight(shard, far, is_own, core):
    mine = jnp.where(is_own, shard, far)
    other = swap(jnp.where(is_own, far, shard), "dp", 1)
    first = core == 0
    return jnp.concatenate(
        [jnp.where(first, mine, other), jnp.where(first, other, mine)], axis=0
    )


def chip_first(share):
    count = share.shape[0] // 2
    return swap(share[:count], "dp", 2), swap(share[count:], "dp", 4)


def chip_second(share, first_x, second_y):
    count = share.shape[0] // 2
    first_y = swap(jnp.concatenate([share[:count], first_x]), "dp", 4)
    second_x = swap(jnp.concatenate([share[count:], second_y]), "dp", 2)
    return [share, first_x, second_y, first_y, second_x]


def place_rows(chip, parts, out_refs):
    share, first_x, second_y, first_y, second_x = parts
    count = first_x.shape[0]
    plan = [
        (0, 0, share, 0),
        (0, 1, share, 1),
        (1, 0, first_x, 0),
        (1, 1, second_x, 0),
        (2, 0, first_y, 0),
        (2, 1, second_y, 0),
        (3, 0, first_y, 1),
        (3, 1, second_x, 1),
    ]
    for r, part, source, block in plan:
        target = pl.ds(pl.multiple_of((chip ^ r) * (2 * count) + part * count, 16), count)
        start = 0
        for out_ref in out_refs:
            stop = start + out_ref.shape[1]
            out_ref[target, :] = source[block * count : (block + 1) * count, start:stop]
            start = stop


def dot(left, right, left_dim=1, right_dim=0):
    return lax.dot_general(
        left, right, (((left_dim,), (right_dim,)), ((), ())), preferred_element_type=jnp.float32
    )


def join_rows(pieces, target):
    start = 0
    for piece in pieces:
        target[start : start + piece.shape[0], :] = piece[...]
        start += piece.shape[0]


def attend_probs(query, key, scale):
    scores = dot(query, key, 1, 1) * scale
    top = jnp.max(scores, axis=1, keepdims=True)
    total = jnp.log(jnp.sum(jnp.exp(scores - top), axis=1, keepdims=True)) + top
    return jnp.exp(scores - total)


def attend_forward_body(heads, scale, chip_ref, *refs):
    pieces, mod_ref, bias_ref, parts = refs[:3], refs[3], refs[4], refs[5:10]
    rows_ref, normed_ref, qkv_ref, mixed_ref, attend_ref, output_ref = refs[10:16]
    partials, joined = refs[16:18], refs[18]
    place_rows(chip_ref[0], parts, (attend_ref, output_ref))
    join_rows(pieces, joined)
    seq = joined.shape[0] // 2
    model_width = joined.shape[1]
    width = output_ref.shape[1]
    for n in (1, 0):
        rows = slice(n * seq, (n + 1) * seq)
        normed, _ = normalize(joined[rows, :].astype(jnp.float32))
        normed_ref[rows, :] = normed
        shift = mod_ref[n : n + 1, :model_width]
        gain = mod_ref[n : n + 1, model_width : 2 * model_width]
        attend_in = (normed * (1.0 + gain) + shift).astype(jnp.bfloat16)
        rows_ref[rows, :] = attend_in
        qkv_ref[rows, :] = (dot(attend_in, attend_ref[...]) + bias_ref[...]).astype(jnp.bfloat16)
        mixed = []
        for head in range(heads):
            query, key, value = (
                qkv_ref[rows, j * width + head * HD : j * width + (head + 1) * HD]
                for j in range(3)
            )
            probs = attend_probs(query, key, scale).astype(jnp.bfloat16)
            mixed.append(dot(probs, value))
        mixed = jnp.concatenate(mixed, axis=1).astype(jnp.bfloat16)
        mixed_ref[rows, :] = mixed
        partials[n][...] = dot(mixed, output_ref[...], 1, 1)


def kernel_call(body, name, outs, operands, scratch, limit, flops, transcendentals=0):
    specs = [
        pl.BlockSpec(memory_space=pltpu.SMEM if x.dtype == jnp.int32 else pltpu.VMEM)
        for x in operands
    ]
    shapes = [jax.ShapeDtypeStruct(*out) for out in outs]
    moved = sum(x.size * x.dtype.itemsize for x in list(operands) + shapes)
    return pl.pallas_call(
        body,
        out_shape=shapes,
        in_specs=specs,
        out_specs=[pl.BlockSpec(memory_space=pltpu.VMEM)] * len(outs),
        scratch_shapes=scratch,
        compiler_params=pltpu.CompilerParams(vmem_limit_bytes=limit * 2**20),
        cost_estimate=pl.CostEstimate(
            flops=flops, bytes_accessed=moved, transcendentals=transcendentals
        ),
        name=name,
    )(*operands)


def attend_forward(chip, pieces, mod_full, bias_rows, parts, heads, scale):
    seq = pieces[-1].shape[0]
    rows, model_width = 2 * seq, pieces[0].shape[1]
    width = heads * HD
    return kernel_call(
        functools.partial(attend_forward_body, heads, scale),
        "attend_forward",
        [
            ((rows, model_width), jnp.bfloat16),
            ((rows, model_width), jnp.float32),
            ((rows, 3 * width), jnp.bfloat16),
            ((rows, width), jnp.bfloat16),
            ((model_width, 3 * width), jnp.bfloat16),
            ((model_width, width), jnp.bfloat16),
            ((seq, model_width), jnp.float32),
            ((seq, model_width), jnp.float32),
        ],
        [chip.reshape(1), *pieces, mod_full, bias_rows, *parts],
        [pltpu.VMEM((rows, model_width), jnp.bfloat16)],
        20,
        2 * rows * model_width * 4 * width + 8 * seq * seq * width,
        2 * 2 * heads * seq * seq,
    )


def feed_forward_body(chip_ref, *refs):
    pieces, ups, mod_ref, bias_ref, parts = refs[:4], refs[4:7], refs[7], refs[8], refs[9:14]
    act_ref, sums_ref, reduce_ref = refs[14:17]
    partials, blocks, expand_ref, joined = refs[17:19], refs[19:23], refs[23], refs[24]
    rows_ref, back_ref, low_ref, grad_ref = refs[25:29]
    place_rows(chip_ref[0], parts, (expand_ref, reduce_ref))
    join_rows(pieces, rows_ref)
    join_rows(ups, joined)
    seq = joined.shape[0] // 2
    model_width = joined.shape[1]
    sums = None
    for n in (1, 0):
        rows = slice(n * seq, (n + 1) * seq)
        value = dot(rows_ref[rows, :], expand_ref[...]) + bias_ref[...]
        gate = mod_ref[n : n + 1, 5 * model_width : 6 * model_width]
        back = (joined[rows, :].astype(jnp.float32) * gate).astype(jnp.bfloat16)
        back_ref[rows, :] = back
        grad_act = dot(back, reduce_ref[...])
        square = value * value
        slope = math.sqrt(2.0 / math.pi)
        bent = jnp.tanh(slope * (value + 0.044715 * (square * value)))
        share = 0.5 * (1.0 + bent)
        act_ref[rows, :] = (value * share).astype(jnp.bfloat16)
        curve = 0.5 * value * (1.0 - bent * bent) * (slope * (1.0 + 3 * 0.044715 * square))
        grad_pre = grad_act * (share + curve)
        part = jnp.sum(grad_pre, axis=0, keepdims=True)
        sums = part if sums is None else sums + part
        low = grad_pre.astype(jnp.bfloat16)
        low_ref[rows, :] = low
        partials[n][...] = dot(low, expand_ref[...], 1, 1)
    sums_ref[...] = sums
    width = act_ref.shape[1]
    grad_ref[:, :width] = dot(rows_ref[...], low_ref[...], 0, 0)
    grad_ref[:, width:] = dot(back_ref[...], act_ref[...], 0, 0)
    write_blocks(chip_ref[0], grad_ref, blocks)


def feed_forward(chip, pieces, ups, mod_full, bias, parts):
    seq = ups[-1].shape[0]
    rows, model_width = 2 * seq, pieces[0].shape[1]
    width = bias.shape[1]
    return kernel_call(
        feed_forward_body,
        "feed_forward",
        [
            ((rows, width), jnp.bfloat16),
            ((1, width), jnp.float32),
            ((model_width, width), jnp.bfloat16),
            ((seq, model_width), jnp.float32),
            ((seq, model_width), jnp.float32),
        ]
        + block_shapes(model_width, 2 * width),
        [chip.reshape(1), *pieces, *ups, mod_full, bias, *parts],
        [
            pltpu.VMEM((model_width, width), jnp.bfloat16),
            pltpu.VMEM((rows, model_width), jnp.bfloat16),
            pltpu.VMEM((rows, model_width), jnp.bfloat16),
            pltpu.VMEM((rows, model_width), jnp.bfloat16),
            pltpu.VMEM((rows, width), jnp.bfloat16),
            pltpu.VMEM((model_width, 2 * width), jnp.float32),
        ],
        36,
        10 * rows * model_width * width,
        rows * width,
    )


def write_blocks(chip, grad_ref, out_refs):
    keep_first, keep_second, send_first, send_second = out_refs
    count = keep_first.shape[0] // 2
    plan = [
        (keep_first, 0, (0, 2)),
        (keep_second, 1, (0, 1)),
        (send_first, 0, (1, 3)),
        (send_second, 1, (2, 3)),
    ]
    for out_ref, part, places in plan:
        for block, r in enumerate(places):
            source = pl.ds(pl.multiple_of((chip ^ r) * (2 * count) + part * count, 8), count)
            out_ref[block * count : (block + 1) * count, :] = grad_ref[source, :].astype(
                out_ref.dtype
            )


def block_shapes(height, width):
    shape = (height // 4, width)
    return [(shape, jnp.float32)] * 2 + [(shape, jnp.bfloat16)] * 2


def grad_blocks_body(chip_ref, *refs):
    out_refs, grad_ref = refs[-5:-1], refs[-1]
    start = 0
    for rows, cols in zip(refs[:-5:2], refs[1:-5:2]):
        stop = start + cols.shape[1]
        grad_ref[:, start:stop] = dot(rows[...], cols[...], 0, 0)
        start = stop
    write_blocks(chip_ref[0], grad_ref, out_refs)


def grad_blocks(pairs, chip):
    height = pairs[0][0].shape[1]
    width = sum(cols.shape[1] for _, cols in pairs)
    return kernel_call(
        grad_blocks_body,
        "grad_blocks",
        block_shapes(height, width),
        [chip.reshape(1)] + [part for pair in pairs for part in pair],
        [pltpu.VMEM((height, width), jnp.float32)],
        16,
        sum(2 * rows.size * cols.shape[1] for rows, cols in pairs),
    )


def first_step(sends):
    return [swap(sends[0], "dp", 2), swap(sends[1], "dp", 4)]


def middle_body(keep_first, keep_second, got_first, got_second, *outs):
    count = keep_first.shape[0] // 2
    for keep, got, base, going in (
        (keep_first, got_first, outs[0], outs[2]),
        (keep_second, got_second, outs[1], outs[3]),
    ):
        total = keep[...] + got[...].astype(jnp.float32)
        base[...] = total[:count]
        going[...] = total[count:].astype(jnp.bfloat16)


def middle_step(keeps, received):
    rows, width = keeps[0].shape
    shape = (rows // 2, width)
    outs = [(shape, jnp.float32)] * 2 + [(shape, jnp.bfloat16)] * 2
    return kernel_call(middle_body, "middle_step", outs, [*keeps, *received], [], 16, 0)


def second_step(going):
    return [swap(going[0], "dp", 4), swap(going[1], "dp", 2)]


def core_body(core_ref, base_first, base_second, got_first, got_second, mine, other):
    first = base_first[...] + got_first[...].astype(jnp.float32)
    second = base_second[...] + got_second[...].astype(jnp.float32)
    is_first = core_ref[0] == 0
    mine[...] = jnp.where(is_first, first, second)
    other[...] = jnp.where(is_first, second, first)


def core_step(core, bases, received):
    outs = [(bases[0].shape, jnp.float32)] * 2
    operands = [core.reshape(1), *bases, *received]
    return kernel_call(core_body, "core_step", outs, operands, [], 12, 0)


def half_body(own_ref, mine, other, kept, sent):
    is_own = own_ref[0] == 1
    kept[...] = jnp.where(is_own, mine[...], other[...])
    sent[...] = jnp.where(is_own, other[...], mine[...]).astype(jnp.bfloat16)


def half_step(is_own, mine, other):
    outs = [(mine.shape, jnp.float32), (mine.shape, jnp.bfloat16)]
    operands = [is_own.astype(jnp.int32).reshape(1), mine, other]
    return kernel_call(half_body, "half_step", outs, operands, [], 12, 0)


def mod_sum_body(partial, crossed, mod_bias, attend_bias, expand_bias, out):
    heads = attend_bias.shape[1]
    out[...] = jnp.zeros_like(out)
    out[0:2, :] = partial[0:2, :] + crossed[2:4, :] + mod_bias[...]
    out[2:4, :] = partial[2:4, :] + crossed[0:2, :] + mod_bias[...]
    out[4:5, :heads] = attend_bias[0:1, :]
    out[4:5, heads : 2 * heads] = attend_bias[1:2, :]
    out[4:5, 2 * heads :] = expand_bias[...]


def mod_place_body(place_ref, own, near, far, mod, qkv_bias, expand_bias, *pieces):
    z, half, is_own = place_ref[0], place_ref[1], place_ref[2]
    width = own.shape[1]
    for r, (source, start) in enumerate(((own, 0), (near, 0), (far, 0), (far, 8))):
        cols = pl.ds(pl.multiple_of((z ^ r) * width, 128), width)
        mod[0:1, cols] = source[pl.ds(start + half, 1), :]
        mod[1:2, cols] = source[pl.ds(start + 2 + half, 1), :]
    wide = expand_bias.shape[1]
    for k, piece in enumerate(pieces):
        piece[...] = mod[0:1, k * wide : (k + 1) * wide]
    bias = jnp.where(is_own == 1, own[4:5, :], far[4:5, :])
    heads = qkv_bias.shape[1] // 3
    qkv_bias[:, :heads] = bias[:, :heads]
    qkv_bias[:, heads : 2 * heads] = jnp.zeros_like(qkv_bias[:, heads : 2 * heads])
    qkv_bias[:, 2 * heads :] = bias[:, heads : 2 * heads]
    expand_bias[...] = bias[:, 2 * heads :]


def halve_body(own, got, keep, send):
    count = keep.shape[0]
    keep[...] = own[:count, :] + got[:count, :]
    send[...] = (own[count:, :] + got[count:, :]).astype(jnp.bfloat16)


def halve(own, got):
    shape = (own.shape[0] // 2, own.shape[1])
    outs = [(shape, jnp.float32), (shape, jnp.bfloat16)]
    return kernel_call(halve_body, "halve", outs, [own, got], [], 8, 0)


def column_sums(values):
    return jnp.sum(values, axis=0, keepdims=True)


def residual_body(keep, got, tokens, out_bias, gate, shift, gain, attend_out, residual, low):
    attend_out[...] = keep[...] + got[...].astype(jnp.float32) + out_bias[...]
    residual[...] = tokens[...].astype(jnp.float32) + gate[...] * attend_out[...]
    normed, _ = normalize(residual[...])
    low[...] = (normed * (1.0 + gain[...]) + shift[...]).astype(jnp.bfloat16)


def hidden_back_body(
    keep, got, residual, attend_out, upstream, gate_a, gain, gate_m, low, grad_residual, sums
):
    grad = keep[...] + got[...].astype(jnp.float32)
    normed, inverse = normalize(residual[...])
    up = upstream[...].astype(jnp.float32)
    total = up + norm_back(grad * (1.0 + gain[...]), normed, inverse)
    grad_residual[...] = total
    term = total * gate_a[...]
    low[...] = term.astype(jnp.bfloat16)
    sums[0:1, :] = column_sums(total * attend_out[...])
    sums[1:2, :] = column_sums(grad)
    sums[2:3, :] = column_sums(grad * normed)
    sums[3:4, :] = column_sums(term)
    sums[4:5, :] = column_sums(up * gate_m[...])
    sums[5:8, :] = jnp.zeros_like(sums[5:8, :])


def block_out_body(keep, got, residual, upstream, reduce_bias, gate, block, gate_sum):
    hidden_out = keep[...] + got[...].astype(jnp.float32) + reduce_bias[...]
    block[...] = (residual[...] + gate[...] * hidden_out).astype(jnp.bfloat16)
    gate_sum[...] = column_sums(upstream[...].astype(jnp.float32) * hidden_out)


def tokens_back_body(keep, got, tokens, grad_residual, gain, kept, send):
    count = kept.shape[0]
    grad = keep[...] + got[...].astype(jnp.float32)
    normed, inverse = normalize(tokens[...].astype(jnp.float32))
    total = grad_residual[...] + norm_back(grad * (1.0 + gain[...]), normed, inverse)
    kept[...] = total[:count, :]
    send[...] = total[count:, :].astype(jnp.bfloat16)


def outputs_body(half_ref, block, block_moved, kept, moved, block_out, tokens_grad):
    half, count = half_ref[0], kept.shape[0]
    block_out[half] = block[:count, :]
    block_out[1 - half] = block_moved[...]
    tokens_grad[half] = kept[...]
    tokens_grad[1 - half] = moved[...].astype(jnp.float32)


def owner_body(kept, moved, *outs):
    start = 0
    for out in outs:
        stop = start + out.shape[1]
        out[...] = kept[:, start:stop] + moved[:, start:stop].astype(jnp.float32)
        start = stop


def owner_sum(kept, moved, widths):
    outs = [((kept.shape[0], width), jnp.float32) for width in widths]
    return kernel_call(owner_body, "owner_sum", outs, [kept, moved], [], 8, 0)


def pack_body(norm, got, sums, gate_m, expand, bias, packed):
    wide = gate_m.shape[1]
    part = packed.shape[1] - wide
    both = norm[0:1, :] + got[...]
    packed[0:1, :wide] = both[:, :wide]
    packed[0:1, wide:] = both[:, wide : wide + part]
    packed[1:2, : wide - part] = both[:, wide + part :]
    packed[1:2, wide - part :] = sums[0:1, :]
    packed[2:3, :wide] = sums[1:2, :]
    packed[2:3, wide:] = sums[2:3, :part]
    packed[3:4, : wide - part] = sums[2:3, part:]
    packed[3:4, wide - part :] = gate_m[...]
    packed[4:5, :wide] = sums[3:4, :]
    packed[4:5, wide:] = sums[4:5, :part]
    packed[5:6, : wide - part] = sums[4:5, part:]
    packed[5:6, wide - part :] = jnp.zeros_like(packed[5:6, wide - part :])
    heads = bias.shape[1] // 3
    packed[6:7, :wide] = expand[...]
    packed[6:7, wide : wide + heads] = bias[:, :heads]
    packed[6:7, wide + heads :] = bias[:, 2 * heads :]
    packed[7:8, :] = jnp.zeros_like(packed[7:8, :])


def attend_owner_body(kept, moved, attend_grad, output_grad):
    width = output_grad.shape[1]
    for j in range(3):
        cols = slice(j * width, (j + 1) * width)
        attend_grad[j] = kept[:, cols] + moved[:, cols].astype(jnp.float32)
    output_grad[...] = kept[:, 3 * width :] + moved[:, 3 * width :].astype(jnp.float32)


def choose_body(place_ref, line, far, packed):
    z, half, own = place_ref[0], place_ref[1], place_ref[2]
    packed[pl.ds(half, 1), :] = line[pl.ds(z, 1), :]
    packed[pl.ds(1 - half, 1), :] = far[pl.ds(z, 1), :]
    packed[2:3, :] = jnp.where(own == 1, line[6:7, :] + far[6:7, :], 0.0)
    packed[3:5, :] = line[4:6, :] + far[4:6, :]
    packed[5:8, :] = jnp.zeros_like(packed[5:8, :])


def modulation_back_body(gathered, silu, weight, weight_grad, grad_silu, bias_grad, rest, rows):
    parts = [gathered[start : start + 8, :] for start in range(0, gathered.shape[0], 8)]
    for m, part in enumerate(parts):
        rows[2 * m : 2 * m + 2, :] = part[0:2, :]
    low = rows[...].astype(jnp.bfloat16)
    weight_grad[...] = dot(silu[...], low, 0, 0)
    grad_silu[...] = dot(low, weight[...], 1, 1)
    while len(parts) > 1:
        parts = [left + right for left, right in zip(parts[::2], parts[1::2])]
    bias_grad[...] = parts[0][0:1, :] + parts[0][1:2, :]
    rest[...] = parts[0][2:5, :]


def table_body(labels, cond, near, far, table, chosen):
    value = cond[...]
    share = 1.0 / (1.0 + jnp.exp(-value))
    grad = (near[...] + far[...]) * share * (1.0 + value * (1.0 - share))
    place = lax.broadcasted_iota(jnp.int32, (1, chosen.shape[1]), 1)
    for row in range(chosen.shape[0]):
        chosen[row : row + 1, :] = jnp.where(place == labels[row], 1.0, 0.0)
    table[...] = lax.dot_general(
        grad,
        chosen[...],
        (((0,), (0,)), ((), ())),
        precision=lax.Precision.HIGHEST,
        preferred_element_type=jnp.float32,
    )


def join_body(attend, output, joined):
    width = output.shape[1]
    for j in range(3):
        joined[:, j * width : (j + 1) * width] = attend[j]
    joined[:, 3 * width :] = output[...]


def attend_back_body(heads, scale, *refs):
    pieces = refs[:4]
    output_ref, qkv_ref, mixed_ref, attend_ref, normed_ref = refs[4:9]
    rows_ref, low_ref, sums_ref, norm_sums_ref = refs[9:13]
    partials = refs[13:15]
    join_rows(pieces, rows_ref)
    seq = rows_ref.shape[0] // 2
    model_width, width = output_ref.shape
    sums = None
    for n in (1, 0):
        rows = slice(n * seq, (n + 1) * seq)
        grad_mixed = dot(rows_ref[rows, :], output_ref[...]).astype(jnp.bfloat16)
        grads = [[], [], []]
        for head in range(heads):
            query, key, value = (
                qkv_ref[rows, j * width + head * HD : j * width + (head + 1) * HD]
                for j in range(3)
            )
            mixed = mixed_ref[rows, head * HD : (head + 1) * HD]
            up = grad_mixed[:, head * HD : (head + 1) * HD]
            probs = attend_probs(query, key, scale)
            delta = jnp.sum(
                up.astype(jnp.float32) * mixed.astype(jnp.float32), axis=1, keepdims=True
            )
            logit = (probs * (dot(up, value, 1, 1) - delta)).astype(jnp.bfloat16)
            grads[0].append(dot(logit, key) * scale)
            grads[1].append(dot(logit, query, 0, 0) * scale)
            grads[2].append(dot(probs.astype(jnp.bfloat16), up, 0, 0))
        whole = jnp.concatenate([part for group in grads for part in group], axis=1)
        part = jnp.sum(whole, axis=0, keepdims=True)
        sums = part if sums is None else sums + part
        low = whole.astype(jnp.bfloat16)
        low_ref[rows, :] = low
        partial = dot(low, attend_ref[...], 1, 1)
        partials[n][...] = partial
        norm_sums_ref[n : n + 1, :model_width] = jnp.sum(partial, axis=0, keepdims=True)
        norm_sums_ref[n : n + 1, model_width:] = jnp.sum(
            partial * normed_ref[rows, :], axis=0, keepdims=True
        )
    sums_ref[...] = sums


def attend_back(pieces, output_full, qkv, mixed, attend_full, normed, heads, scale):
    rows, model_width = normed.shape
    seq, width = rows // 2, mixed.shape[1]
    return kernel_call(
        functools.partial(attend_back_body, heads, scale),
        "attend_back",
        [
            ((rows, model_width), jnp.bfloat16),
            ((rows, 3 * width), jnp.bfloat16),
            ((1, 3 * width), jnp.float32),
            ((2, 2 * model_width), jnp.float32),
            ((seq, model_width), jnp.float32),
            ((seq, model_width), jnp.float32),
        ],
        [*pieces, output_full, qkv, mixed, attend_full, normed],
        [],
        20,
        2 * rows * model_width * 4 * width + 20 * seq * seq * width,
        2 * 2 * heads * seq * seq,
    )


def on_paired_device(
    tokens,
    cotangent,
    labels,
    timesteps,
    class_table,
    modulation_weight,
    modulation_bias,
    attend_weight,
    attend_bias,
    output_weight,
    output_bias,
    expand_weight,
    expand_bias,
    reduce_weight,
    reduce_bias,
):
    data_index = lax.axis_index("dp")
    tensor_index = lax.axis_index("tensor")
    core, chip = data_index & 1, data_index >> 1
    half = tensor_index >> 1
    is_own = half == core
    model_width = tokens.shape[2]
    row_share = modulation_weight.shape[0]
    head_width = attend_weight.shape[2]
    head_count = head_width // HD
    ff_width = expand_weight.shape[1]
    mod_width = modulation_weight.shape[1]
    latent_total = labels.shape[0]
    classes_total = class_table.shape[0]
    score_scale = 1.0 / math.sqrt(HD)

    count = tokens.shape[1]
    place = jnp.stack([tensor_index, half, is_own.astype(jnp.int32)])

    order = Order()
    mark, hold = order.mark, order.hold

    attn_shard = kernel_call(
        join_body,
        "join_weights",
        [((row_share, 4 * head_width), jnp.bfloat16)],
        [jnp.transpose(attend_weight, (1, 0, 2)), output_weight],
        [],
        4,
        0,
    )[0]
    mark(ATTN_SHARD, attn_shard)
    attn_far = mark(ATTN_FAR, swap(attn_shard, "tensor", 2))
    tokens_sent = pick(hold(TOKENS_SENT, tokens), 1 - half)
    tokens_half = jnp.concatenate([pick(tokens, half), swap(tokens_sent, "tensor", 2)])
    mark(TOKENS_HALF, tokens_half)
    labels, timesteps = (labels, timesteps)

    slot = jnp.arange(latent_total, dtype=jnp.int32)
    latent_ids = ((slot >> 1) ^ data_index) * 2 + (slot & 1)
    chosen = latent_ids[:, None] == slot[None, :]
    labels_rel = jnp.sum(jnp.where(chosen, labels[None, :], 0), axis=1)
    steps_rel = jnp.sum(jnp.where(chosen, timesteps[None, :], 0), axis=1)
    looked = lax.dynamic_slice_in_dim(
        jnp.take(class_table, labels_rel, axis=0), data_index * row_share, row_share, 1
    ).astype(jnp.float32)
    halfway = model_width // 2
    column = data_index * row_share + jnp.arange(row_share, dtype=jnp.int32)
    is_cos = column < halfway
    position = jnp.where(is_cos, column, column - halfway).astype(jnp.float32)
    frequency = jnp.exp(-math.log(10000.0) * position / halfway)
    angles = steps_rel.astype(jnp.float32)[:, None] * frequency[None, :]
    cond = looked + jnp.where(is_cos[None, :], jnp.cos(angles), jnp.sin(angles))
    silu_act = jax.nn.silu(cond).astype(jnp.bfloat16)
    partial = jnp.dot(silu_act, modulation_weight, preferred_element_type=jnp.float32)
    partial = partial[:8] + swap(partial[8:], "dp", 4)
    attn_share = near_weight(attn_shard, attn_far, is_own, core)
    mark(ATTN_SHARE, attn_share)
    partial = partial[:4] + swap(partial[4:], "dp", 2)
    partial = hold(PARTIAL_CORE, partial)
    ff_shard = jnp.concatenate([expand_weight, reduce_weight], axis=1)
    tokens_near = swap(tokens_half, "tensor", 1)
    mod_cols = kernel_call(
        mod_sum_body,
        "mod_sum",
        [((8, mod_width), jnp.float32)],
        [
            partial,
            swap(partial, "dp", 1),
            modulation_bias[None],
            attend_bias,
            expand_bias[None],
        ],
        [],
        4,
        0,
    )[0]
    attn_first = chip_first(attn_share)
    attn_parts = chip_second(attn_share, *attn_first)
    mark(ATTN_PARTS, attn_parts)
    mod_near = swap(mod_cols, "tensor", 1)
    mod_line = jnp.concatenate([mod_cols, mod_near])
    mark(MOD_LINE, mod_line)
    mod_far = swap(mod_line, "tensor", 2)
    ff_far = mark(FF_FAR, swap(ff_shard, "tensor", 2))
    tokens_across = swap(jnp.concatenate([tokens_half, tokens_near]), "dp", 1)
    row = ((1, model_width), jnp.float32)
    mod_full, qkv_bias, expand_row, _, gain_a, gate_a, shift_m, gain_m, gate_m = kernel_call(
        mod_place_body,
        "mod_place",
        [
            ((2, 6 * model_width), jnp.float32),
            ((1, 3 * head_width), jnp.float32),
            ((1, ff_width), jnp.float32),
        ]
        + [row] * 6,
        [place, mod_cols, mod_near, hold(MOD_PLACE, mod_far)],
        [],
        4,
        0,
    )
    ff_share = near_weight(ff_shard, hold(FF_FAR, ff_far), is_own, core)
    mark(FF_SHARE, ff_share)
    upstream_sent = hold(UPSTREAM_SENT, pick(cotangent, 1 - half))
    upstream_far = swap(upstream_sent, "tensor", 2)
    ff_first = chip_first(ff_share)

    (
        attend_rows,
        normed_all,
        projected,
        mixed_rows,
        attend_full,
        output_full,
        own_partial,
        other_partial,
    ) = attend_forward(
        chip,
        [tokens_half, tokens_near, hold(ATTEND, tokens_across)],
        mod_full,
        qkv_bias,
        attn_parts,
        head_count,
        score_scale,
    )
    keep, send = halve(own_partial, swap(other_partial, "dp", 1))
    mark(ATTEND_SEND, send)
    upstream_half = jnp.concatenate([pick(cotangent, half), upstream_far])
    mark(UPSTREAM_HALF, upstream_half)
    ff_first = hold(FF_SECOND, ff_first)
    ff_parts = chip_second(ff_share, *ff_first)
    got = swap(send, "tensor", 1)
    upstream_near = swap(upstream_half, "tensor", 1)
    attend_out, residual, hidden_in = kernel_call(
        residual_body,
        "residual",
        [(keep.shape, jnp.float32), (keep.shape, jnp.float32), (keep.shape, jnp.bfloat16)],
        [
            keep,
            hold(RESIDUAL, got),
            tokens_half,
            output_bias[None],
            gate_a,
            shift_m,
            gain_m,
        ],
        [],
        8,
        0,
    )
    hidden_pieces = collect_pairs(hidden_in)
    upstream_line = jnp.concatenate([upstream_half, upstream_near])
    upstream_across = swap(upstream_line, "dp", 1)

    (
        activated,
        grad_expand_bias,
        reduce_full,
        own_partial,
        other_partial,
        *ff_blocks,
    ) = feed_forward(
        chip,
        hidden_pieces,
        [upstream_half, upstream_near, upstream_across],
        mod_full,
        expand_row,
        ff_parts,
    )
    mark(FEED, own_partial)
    keep, send = halve(own_partial, swap(other_partial, "dp", 1))
    mark(FEED_SEND, send)
    got = swap(send, "tensor", 1)
    ff_first = first_step(hold(FF_BLOCKS, ff_blocks[2:]))
    seq_len = tokens_across.shape[0]
    act_later = hold(ACTIVATED, activated)
    other_out, own_out = (
        jnp.einsum("sf,of->so", act_half, reduce_full, preferred_element_type=jnp.float32)
        for act_half in (act_later[seq_len:], act_later[:seq_len])
    )
    out_keep, out_send = halve(own_out, swap(other_out, "dp", 1))
    mark(OUT_SEND, out_send)
    output_low, grad_residual, row_sums = kernel_call(
        hidden_back_body,
        "hidden_back",
        [(keep.shape, jnp.bfloat16), (keep.shape, jnp.float32), ((8, model_width), jnp.float32)],
        [
            keep,
            hold(HIDDEN_BACK, got),
            residual,
            attend_out,
            upstream_half,
            gate_a,
            gain_m,
            gate_m,
        ],
        [],
        8,
        0,
    )
    output_pieces = collect_pairs(output_low)
    mark(OUTPUT_NEAR, output_pieces[1])
    block_own, gate_sum = kernel_call(
        block_out_body,
        "block_out",
        [(keep.shape, jnp.bfloat16), row],
        [
            out_keep,
            swap(out_send, "tensor", 1),
            residual,
            upstream_half,
            reduce_bias[None],
            gate_m,
        ],
        [],
        8,
        0,
    )
    mark(BLOCK_OUT, block_own)

    def ff_middle():
        *bases, going, going_second = middle_step(ff_blocks[:2], hold(FF_MIDDLE, ff_first))
        mark(FF_GOING, going)
        return bases, second_step([going, going_second])

    ff_bases, ff_second = ff_middle()

    (
        output_rows,
        projected_low,
        bias_sums,
        norm_sums,
        own_partial,
        other_partial,
    ) = attend_back(
        hold(ATTEND_BACK, output_pieces),
        output_full,
        projected,
        mixed_rows,
        attend_full,
        normed_all,
        head_count,
        score_scale,
    )
    block_moved = swap(hold(BLOCK_MOVED, block_own[count:]), "tensor", 2)
    norm_crossed = mark(NORM_CROSSED, swap(norm_sums[1:], "dp", 1))
    ff_mine, ff_other = core_step(core, ff_bases, hold(FF_CORE, ff_second))
    mark(FF_CORE, ff_mine)
    ff_kept, ff_sent = half_step(is_own, ff_mine, swap(ff_other, "dp", 1))
    mark(FF_HALF, ff_sent)

    line = kernel_call(
        pack_body,
        "pack",
        [((8, mod_width), jnp.float32)],
        [
            norm_sums,
            hold(PACK, norm_crossed),
            row_sums,
            gate_sum,
            grad_expand_bias,
            bias_sums,
        ],
        [],
        4,
        0,
    )[0]
    mark(PACK, line)
    keep, send = halve(own_partial, swap(other_partial, "dp", 1))
    grad_got = swap(send, "tensor", 1)
    attn_blocks = grad_blocks(
        [(attend_rows, hold(ATTN_BLOCKS, projected_low)), (output_rows, mixed_rows)], chip
    )
    mark(ATTN_BLOCKS, attn_blocks[2])
    attn_first = first_step(attn_blocks[2:])
    summed = lax.broadcasted_iota(jnp.int32, line.shape, 0) < 6
    near = hold(LINE, swap(hold(LINE_NEAR, line), "tensor", 1))
    line = line + jnp.where(summed, near, 0.0)
    far = mark(FAR, swap(hold(LINE_FAR, line), "tensor", 2))
    packed = kernel_call(
        choose_body,
        "choose",
        [((8, mod_width), jnp.float32)],
        [place, line, far],
        [],
        4,
        0,
    )[0]
    ff_moved = mark(FF_MOVED, swap(ff_sent, "tensor", 2))
    tokens_kept, back_sent = kernel_call(
        tokens_back_body,
        "tokens_back",
        [((count, model_width), jnp.float32), ((count, model_width), jnp.bfloat16)],
        [keep, grad_got, tokens_half, grad_residual, gain_a],
        [],
        8,
        0,
    )
    tokens_moved = swap(hold(BACK_SENT, back_sent), "tensor", 2)
    *attn_bases, attn_going, attn_going_second = middle_step(
        attn_blocks[:2], attn_first
    )
    attn_second = second_step([attn_going, attn_going_second])
    packed = jnp.concatenate([packed, swap(packed, "dp", 1)])
    packed = jnp.concatenate([packed, swap(hold(PACKED_X, packed), "dp", 2)])
    attn_mine, attn_other = core_step(core, attn_bases, attn_second)
    mark(ATTN_CORE, attn_mine)
    packed = jnp.concatenate([packed, swap(hold(PACKED_Y, packed), "dp", 4)])
    modulation_weight_grad, grad_silu, modulation_bias_grad, rest = kernel_call(
        modulation_back_body,
        "modulation_back",
        [
            ((row_share, mod_width), jnp.float32),
            ((latent_total, row_share), jnp.float32),
            ((1, mod_width), jnp.float32),
            ((3, mod_width), jnp.float32),
        ],
        [hold(MODULATION_BACK, packed), silu_act, modulation_weight],
        [pltpu.VMEM((latent_total, mod_width), jnp.float32)],
        8,
        4 * latent_total * row_share * mod_width,
    )
    mark(MODULATION_BACK, grad_silu)
    attn_kept, attn_sent = half_step(is_own, attn_mine, hold(ATTN_HALF, swap(attn_other, "dp", 1)))
    attn_moved = swap(attn_sent, "tensor", 2)
    near = grad_silu + swap(hold(GRAD_SILU, grad_silu), "tensor", 1)
    mark(NEAR, near)
    table_grad = kernel_call(
        table_body,
        "table",
        [((row_share, classes_total), jnp.float32)],
        [labels_rel, cond, near, swap(near, "tensor", 2)],
        [pltpu.VMEM((latent_total, classes_total), jnp.float32)],
        4,
        0,
    )[0]
    mark(TABLE, table_grad)
    expand_grad, reduce_grad = owner_sum(
        ff_kept, hold(FF_OWNER, ff_moved), [ff_width, ff_width]
    )
    attend_grad, output_grad = kernel_call(
        attend_owner_body,
        "owner_sum",
        [((3, row_share, head_width), jnp.float32), (output_weight.shape, jnp.float32)],
        [attn_kept, hold(ATTN_OWNER, attn_moved)],
        [],
        8,
        0,
    )
    block_output, tokens_grad = kernel_call(
        outputs_body,
        "outputs",
        [(tokens.shape, jnp.bfloat16), (tokens.shape, jnp.float32)],
        [half.reshape(1), block_own, block_moved, tokens_kept, hold(OUTPUTS, tokens_moved)],
        [],
        8,
        0,
    )
    wide = model_width
    return (
        block_output,
        tokens_grad,
        table_grad.T,
        modulation_weight_grad,
        modulation_bias_grad[0],
        jnp.transpose(attend_grad, (1, 0, 2)),
        rest[0, wide:].reshape(2, head_width),
        output_grad,
        rest[1, :wide],
        expand_grad,
        rest[0, :wide],
        reduce_grad,
        jnp.concatenate([rest[1, wide:], rest[2, : 2 * wide - mod_width]]),
    )


def solution(mesh):
    paired = mesh.shape["dp"] == 8 and mesh.shape["tensor"] == 4
    per_device = on_paired_device if paired else on_device
    placed = (
        P("dp", "tensor", None),
        P("dp", "tensor", None),
        P(),
        P(),
        P(),
        P("dp", "tensor"),
        P("tensor"),
        P("dp", None, "tensor"),
        P(None, "tensor"),
        P("dp", "tensor"),
        P(),
        P("dp", "tensor"),
        P("tensor"),
        P("dp", "tensor"),
        P(),
    )
    return jax.shard_map(
        per_device,
        mesh=mesh,
        in_specs=placed,
        out_specs=(
            P("dp", "tensor", None),
            P("dp", "tensor", None),
            P(None, "dp"),
            P("dp", "tensor"),
            P("tensor"),
            P("dp", None, "tensor"),
            P(None, "tensor"),
            P("dp", "tensor"),
            P(),
            P("dp", "tensor"),
            P("tensor"),
            P("dp", "tensor"),
            P(),
        ),
        check_vma=False,
    )
```

```python
import functools
import math

import jax
import jax.numpy as jnp
from jax import lax
from jax.experimental import pallas as pl
from jax.experimental.pallas import tpu as pltpu
from jax.sharding import PartitionSpec as P

HD = 64


norm_eps = 1e-06


def timestep_features(steps_in, model_width):
    halfway = model_width // 2
    frequency = jnp.exp(-math.log(10000.0) * jnp.arange(halfway, dtype=jnp.float32) / halfway)
    angles = steps_in.astype(jnp.float32)[:, None] * frequency[None, :]
    return jnp.concatenate([jnp.cos(angles), jnp.sin(angles)], axis=1)


def condition(label_ids, steps_in, class_table):
    looked = jnp.take(class_table, label_ids, axis=0).astype(jnp.float32)
    return looked + timestep_features(steps_in, class_table.shape[1])


def silu_back(inputs, upstream):
    sigmoid = jax.nn.sigmoid(inputs)
    return upstream * sigmoid * (1.0 + inputs * (1.0 - sigmoid))


def gelu_back(inputs, upstream):
    outputs, pullback = jax.vjp(lambda inner: jax.nn.gelu(inner, approximate=True), inputs)
    return pullback(upstream)[0]


def normalize(inputs):
    centered = inputs - jnp.mean(inputs, axis=-1, keepdims=True)
    inverse = lax.rsqrt(jnp.mean(centered * centered, axis=-1, keepdims=True) + norm_eps)
    return (centered * inverse, inverse)


def norm_back(upstream, normed, inverse):
    return inverse * (
        upstream
        - jnp.mean(upstream, axis=-1, keepdims=True)
        - normed * jnp.mean(upstream * normed, axis=-1, keepdims=True)
    )


def collect(local_rows):
    return lax.all_gather(local_rows, "tensor", axis=1, tiled=True)


def spread(partial_rows):
    return lax.psum_scatter(partial_rows, "tensor", scatter_dimension=1, tiled=True)


def on_device(
    tokens,
    cotangent,
    labels,
    timesteps,
    class_table,
    modulation_weight,
    modulation_bias,
    attend_weight,
    attend_bias,
    output_weight,
    output_bias,
    expand_weight,
    expand_bias,
    reduce_weight,
    reduce_bias,
):
    tensor_count = lax.axis_size("tensor")
    data_index = lax.axis_index("dp")
    tensor_index = lax.axis_index("tensor")
    latent_count = tokens.shape[0]
    model_width = tokens.shape[2]
    row_share = modulation_weight.shape[0]
    head_width = attend_weight.shape[2]
    head_count = head_width // HD
    classes_total = class_table.shape[0]
    score_scale = 1.0 / math.sqrt(HD)
    row_start = data_index * row_share
    zero_index = jnp.zeros((), jnp.int32)
    modulation_full, attend_full, output_full, expand_full, reduce_full = (
        lax.all_gather(modulation_weight, "dp", axis=0, tiled=True),
        lax.all_gather(attend_weight, "dp", axis=0, tiled=True),
        lax.all_gather(output_weight, "dp", axis=0, tiled=True),
        lax.all_gather(expand_weight, "dp", axis=0, tiled=True),
        lax.all_gather(reduce_weight, "dp", axis=0, tiled=True),
    )
    own_labels = lax.dynamic_slice_in_dim(labels, data_index * latent_count, latent_count)
    own_steps = lax.dynamic_slice_in_dim(timesteps, data_index * latent_count, latent_count)
    cond_own = condition(own_labels, own_steps, class_table)
    silu_own = jax.nn.silu(cond_own).astype(jnp.bfloat16)
    modulation_share = jnp.dot(silu_own, modulation_full, preferred_element_type=jnp.float32)
    modulation = lax.all_gather(modulation_share + modulation_bias, "tensor", axis=1, tiled=True)
    pieces = modulation.reshape(latent_count, 6, 1, model_width)
    shift_attend, scale_attend, gate_attend = (pieces[:, 0], pieces[:, 1], pieces[:, 2])
    shift_hidden, scale_hidden, gate_hidden = (pieces[:, 3], pieces[:, 4], pieces[:, 5])
    tokens_wide = tokens.astype(jnp.float32)
    normed_first, inverse_first = normalize(tokens_wide)
    attend_in = (normed_first * (1.0 + scale_attend) + shift_attend).astype(jnp.bfloat16)
    attend_rows = collect(attend_in)
    seq_len = attend_rows.shape[1]
    bias_rows = jnp.stack([attend_bias[0], jnp.zeros_like(attend_bias[0]), attend_bias[1]])
    projected = (
        jnp.einsum("bsd,dje->jbse", attend_rows, attend_full, preferred_element_type=jnp.float32)
        + bias_rows[:, None, None, :]
    ).astype(jnp.bfloat16)
    split_heads = projected.reshape(3, latent_count, seq_len, head_count, HD)
    query_heads, key_heads, value_heads = (split_heads[0], split_heads[1], split_heads[2])
    scores = (
        jnp.einsum("bqhe,bkhe->bhqk", query_heads, key_heads, preferred_element_type=jnp.float32)
        * score_scale
    )
    log_total = jax.nn.logsumexp(scores, axis=-1)
    probs = jnp.exp(scores - log_total[..., None]).astype(jnp.bfloat16)
    mixed = jnp.einsum(
        "bhqk,bkhe->bqhe", probs, value_heads, preferred_element_type=jnp.float32
    ).astype(jnp.bfloat16)
    mixed_rows = mixed.reshape(latent_count, seq_len, head_width)
    attend_out = (
        spread(
            jnp.einsum("bsi,oi->bso", mixed_rows, output_full, preferred_element_type=jnp.float32)
        )
        + output_bias
    )
    residual = tokens_wide + gate_attend * attend_out
    normed_second, inverse_second = normalize(residual)
    hidden_in = (normed_second * (1.0 + scale_hidden) + shift_hidden).astype(jnp.bfloat16)
    hidden_rows = collect(hidden_in)
    pre_act = (
        jnp.einsum("bsd,df->bsf", hidden_rows, expand_full, preferred_element_type=jnp.float32)
        + expand_bias
    )
    activated = jax.nn.gelu(pre_act, approximate=True).astype(jnp.bfloat16)
    hidden_out = (
        spread(
            jnp.einsum("bsf,of->bso", activated, reduce_full, preferred_element_type=jnp.float32)
        )
        + reduce_bias
    )
    block_output = (residual + gate_hidden * hidden_out).astype(jnp.bfloat16)
    upstream = cotangent.astype(jnp.float32)
    grad_gate_hidden = jnp.sum(upstream * hidden_out, axis=1)
    reduce_term = upstream * gate_hidden
    grad_reduce_bias = jnp.sum(reduce_term, axis=(0, 1))
    reduce_rows = collect(reduce_term.astype(jnp.bfloat16))
    grad_act = jnp.einsum(
        "bso,of->bsf", reduce_rows, reduce_full, preferred_element_type=jnp.float32
    )
    grad_reduce = jnp.einsum(
        "bso,bsf->of", reduce_rows, activated, preferred_element_type=jnp.float32
    )
    grad_pre = gelu_back(pre_act, grad_act)
    grad_expand_bias = jnp.sum(grad_pre, axis=(0, 1))
    grad_pre_low = grad_pre.astype(jnp.bfloat16)
    grad_expand = jnp.einsum(
        "bsd,bsf->df", hidden_rows, grad_pre_low, preferred_element_type=jnp.float32
    )
    grad_hidden_in = spread(
        jnp.einsum("bsf,df->bsd", grad_pre_low, expand_full, preferred_element_type=jnp.float32)
    )
    grad_shift_hidden = jnp.sum(grad_hidden_in, axis=1)
    grad_scale_hidden = jnp.sum(grad_hidden_in * normed_second, axis=1)
    grad_residual = upstream + norm_back(
        grad_hidden_in * (1.0 + scale_hidden), normed_second, inverse_second
    )
    grad_gate_attend = jnp.sum(grad_residual * attend_out, axis=1)
    output_term = grad_residual * gate_attend
    grad_output_bias = jnp.sum(output_term, axis=(0, 1))
    output_rows = collect(output_term.astype(jnp.bfloat16))
    grad_output = jnp.einsum(
        "bso,bsi->oi", output_rows, mixed_rows, preferred_element_type=jnp.float32
    )
    grad_mixed = jnp.einsum(
        "bso,oi->bsi", output_rows, output_full, preferred_element_type=jnp.float32
    ).astype(jnp.bfloat16)
    grad_mixed_heads = grad_mixed.reshape(latent_count, seq_len, head_count, HD)
    recomputed = jnp.exp(
        jnp.einsum("bqhe,bkhe->bhqk", query_heads, key_heads, preferred_element_type=jnp.float32)
        * score_scale
        - log_total[..., None]
    )
    row_dot = jnp.einsum(
        "bqhe,bqhe->bhq", grad_mixed_heads, mixed, preferred_element_type=jnp.float32
    )
    grad_probs = jnp.einsum(
        "bqhe,bkhe->bhqk", grad_mixed_heads, value_heads, preferred_element_type=jnp.float32
    )
    grad_logit = (recomputed * (grad_probs - row_dot[..., None])).astype(jnp.bfloat16)
    grad_query = (
        jnp.einsum("bhqk,bkhe->bqhe", grad_logit, key_heads, preferred_element_type=jnp.float32)
        * score_scale
    )
    grad_key = (
        jnp.einsum("bhqk,bqhe->bkhe", grad_logit, query_heads, preferred_element_type=jnp.float32)
        * score_scale
    )
    grad_value = jnp.einsum(
        "bhqk,bqhe->bkhe", probs, grad_mixed_heads, preferred_element_type=jnp.float32
    )
    grad_projected = jnp.stack([grad_query, grad_key, grad_value]).reshape(
        3, latent_count, seq_len, head_width
    )
    grad_attend_bias = jnp.stack(
        [jnp.sum(grad_projected[0], axis=(0, 1)), jnp.sum(grad_projected[2], axis=(0, 1))]
    )
    grad_projected_low = grad_projected.astype(jnp.bfloat16)
    grad_attend = jnp.einsum(
        "bsd,jbse->dje", attend_rows, grad_projected_low, preferred_element_type=jnp.float32
    )
    grad_attend_in = spread(
        jnp.einsum(
            "jbse,dje->bsd", grad_projected_low, attend_full, preferred_element_type=jnp.float32
        )
    )
    grad_shift_attend = jnp.sum(grad_attend_in, axis=1)
    grad_scale_attend = jnp.sum(grad_attend_in * normed_first, axis=1)
    tokens_grad = grad_residual + norm_back(
        grad_attend_in * (1.0 + scale_attend), normed_first, inverse_first
    )
    grad_modulation_rows = jnp.concatenate(
        [
            grad_shift_attend,
            grad_scale_attend,
            grad_gate_attend,
            grad_shift_hidden,
            grad_scale_hidden,
            grad_gate_hidden,
        ],
        axis=1,
    )
    grad_modulation = lax.psum_scatter(
        grad_modulation_rows, "tensor", scatter_dimension=1, tiled=True
    )
    grad_modulation_bias = jnp.sum(grad_modulation, axis=0)
    grad_modulation_low = grad_modulation.astype(jnp.bfloat16)
    grad_modulation_weight = jnp.einsum(
        "ld,lc->dc", silu_own, grad_modulation_low, preferred_element_type=jnp.float32
    )
    grad_modulation_weight, grad_attend, grad_output, grad_expand, grad_reduce = (
        lax.psum_scatter(grad_modulation_weight, "dp", scatter_dimension=0, tiled=True),
        lax.psum_scatter(grad_attend, "dp", scatter_dimension=0, tiled=True),
        lax.psum_scatter(grad_output, "dp", scatter_dimension=0, tiled=True),
        lax.psum_scatter(grad_expand, "dp", scatter_dimension=0, tiled=True),
        lax.psum_scatter(grad_reduce, "dp", scatter_dimension=0, tiled=True),
    )
    grad_silu = jnp.einsum(
        "lc,dc->ld", grad_modulation_low, modulation_full, preferred_element_type=jnp.float32
    )
    grad_cond = silu_back(cond_own, grad_silu)
    shard_rows = lax.all_gather(grad_cond, ("dp", "tensor"), axis=0, tiled=True)
    row_count = shard_rows.shape[0]
    positions = jnp.arange(row_count, dtype=jnp.int32)
    latent_ids = positions // latent_count // tensor_count * latent_count + positions % latent_count
    picked = jnp.take(labels, latent_ids)
    onehot = (picked[:, None] == jnp.arange(classes_total, dtype=jnp.int32)[None, :]).astype(
        jnp.float32
    )
    columns = lax.dynamic_slice_in_dim(shard_rows, row_start, row_share, 1)
    table_grad = jnp.einsum(
        "rc,rd->cd",
        onehot,
        columns,
        precision=lax.Precision.HIGHEST,
        preferred_element_type=jnp.float32,
    )
    expand_share = grad_expand_bias.shape[0]
    modulation_cols = grad_modulation_bias.shape[0]
    padded_attend = lax.dynamic_update_slice(
        jnp.zeros((2, head_width * tensor_count), jnp.float32),
        grad_attend_bias,
        (zero_index, tensor_index * head_width),
    )
    padded_expand = lax.dynamic_update_slice(
        jnp.zeros((expand_share * tensor_count,), jnp.float32),
        grad_expand_bias,
        (tensor_index * expand_share,),
    )
    padded_modulation = lax.dynamic_update_slice(
        jnp.zeros((modulation_cols * tensor_count,), jnp.float32),
        grad_modulation_bias,
        (tensor_index * modulation_cols,),
    )
    summed_attend, summed_expand, summed_modulation, summed_output, summed_reduce = lax.psum(
        (padded_attend, padded_expand, padded_modulation, grad_output_bias, grad_reduce_bias),
        ("dp", "tensor"),
    )
    attend_bias_grad = lax.dynamic_slice_in_dim(
        summed_attend, tensor_index * head_width, head_width, 1
    )
    expand_bias_grad = lax.dynamic_slice_in_dim(
        summed_expand, tensor_index * expand_share, expand_share, 0
    )
    modulation_bias_grad = lax.dynamic_slice_in_dim(
        summed_modulation, tensor_index * modulation_cols, modulation_cols, 0
    )
    return (
        block_output,
        tokens_grad,
        table_grad,
        grad_modulation_weight,
        modulation_bias_grad,
        grad_attend,
        attend_bias_grad,
        grad_output,
        summed_output,
        grad_expand,
        expand_bias_grad,
        grad_reduce,
        summed_reduce,
    )


def swap(values, axis, mask):
    count = lax.axis_size(axis)
    return lax.ppermute(values, axis, [(place, place ^ mask) for place in range(count)])


def pick(values, place):
    return lax.dynamic_index_in_dim(values, place, 0, keepdims=False)


def collect_pairs(rows):
    near = swap(rows, "tensor", 1)
    return [rows, near, swap(rows, "dp", 1), swap(near, "dp", 1)]


(
    ACTIVATED,
    ATTEND,
    ATTEND_BACK,
    ATTEND_SEND,
    ATTN_BLOCKS,
    ATTN_FAR,
    ATTN_HALF,
    ATTN_PARTS,
    ATTN_SENT,
    ATTN_SHARD,
    ATTN_SHARE,
    BACK_SENT,
    BLOCK_OUT,
    FAR,
    FEED,
    FF_BACK_SECOND,
    FF_CORE,
    FF_FAR,
    FF_GOING,
    FF_HALF,
    FF_MIDDLE,
    FF_MOVED,
    FF_OWNER,
    FF_SECOND,
    FF_SHARD,
    FF_SHARE,
    GRAD_SILU,
    HIDDEN_BACK,
    LINE,
    LINE_FAR,
    MOD_LINE,
    MOD_PLACE,
    MODULATION_BACK,
    NEAR,
    NORM_CROSSED,
    OUT_SEND,
    OUTPUT_NEAR,
    OUTPUTS,
    PACK,
    PACKED_Y,
    PARTIAL_CORE,
    RESIDUAL,
    TABLE,
    TOKENS_HALF,
    TOKENS_SENT,
    UPSTREAM_HALF,
    UPSTREAM_SENT,
) = range(47)

HOLDS = {
    TOKENS_SENT: (ATTN_SHARD,),
    PARTIAL_CORE: (ATTN_SHARE,),
    FF_SHARD: (ATTN_FAR, TOKENS_HALF,),
    MOD_PLACE: (ATTN_PARTS,),
    FF_FAR: (MOD_LINE,),
    UPSTREAM_SENT: (FF_FAR, FF_SHARE,),
    ATTEND: (FF_SHARE,),
    FF_SECOND: (ATTEND_SEND,),
    RESIDUAL: (UPSTREAM_HALF,),
    ACTIVATED: (FEED,),
    HIDDEN_BACK: (OUT_SEND,),
    FF_MIDDLE: (BLOCK_OUT, OUTPUT_NEAR,),
    ATTEND_BACK: (BLOCK_OUT, FF_GOING,),
    PACK: (FF_BACK_SECOND, FF_CORE,),
    ATTN_BLOCKS: (PACK,),
    LINE: (FF_HALF,),
    LINE_FAR: (ATTN_BLOCKS,),
    FF_CORE: (NORM_CROSSED,),
    BACK_SENT: (FAR,),
    PACKED_Y: (FF_MOVED,),
    ATTN_HALF: (MODULATION_BACK,),
    ATTN_SENT: (FF_MOVED, MODULATION_BACK,),
    GRAD_SILU: (FF_MOVED,),
    TABLE: (FF_MOVED,),
    FF_OWNER: (NEAR,),
    OUTPUTS: (MODULATION_BACK,),
}


class Order:
    def __init__(self):
        self.marks = {}

    def mark(self, name, values):
        self.marks[name] = values
        return values

    def hold(self, name, values):
        earlier = [self.marks[mark] for mark in HOLDS.get(name, ())]
        return lax.optimization_barrier((values, earlier))[0] if earlier else values


def near_weight(shard, far, is_own, core):
    mine = jnp.where(is_own, shard, far)
    other = swap(jnp.where(is_own, far, shard), "dp", 1)
    first = core == 0
    return jnp.concatenate(
        [jnp.where(first, mine, other), jnp.where(first, other, mine)], axis=0
    )


def chip_first(share):
    count = share.shape[0] // 2
    return swap(share[:count], "dp", 2), swap(share[count:], "dp", 4)


def chip_second(share, first_x, second_y):
    count = share.shape[0] // 2
    first_y = swap(jnp.concatenate([share[:count], first_x]), "dp", 4)
    second_x = swap(jnp.concatenate([share[count:], second_y]), "dp", 2)
    return [share, first_x, second_y, first_y, second_x]


def place_rows(chip, parts, out_refs):
    share, first_x, second_y, first_y, second_x = parts
    count = first_x.shape[0]
    plan = [
        (0, 0, share, 0),
        (0, 1, share, 1),
        (1, 0, first_x, 0),
        (1, 1, second_x, 0),
        (2, 0, first_y, 0),
        (2, 1, second_y, 0),
        (3, 0, first_y, 1),
        (3, 1, second_x, 1),
    ]
    for r, part, source, block in plan:
        target = pl.ds(pl.multiple_of((chip ^ r) * (2 * count) + part * count, 16), count)
        start = 0
        for out_ref in out_refs:
            stop = start + out_ref.shape[1]
            out_ref[target, :] = source[block * count : (block + 1) * count, start:stop]
            start = stop


def dot(left, right, left_dim=1, right_dim=0):
    return lax.dot_general(
        left, right, (((left_dim,), (right_dim,)), ((), ())), preferred_element_type=jnp.float32
    )


def join_rows(pieces, target):
    start = 0
    for piece in pieces:
        target[start : start + piece.shape[0], :] = piece[...]
        start += piece.shape[0]


def attend_probs(query, key, scale):
    scores = dot(query, key, 1, 1) * scale
    top = jnp.max(scores, axis=1, keepdims=True)
    total = jnp.log(jnp.sum(jnp.exp(scores - top), axis=1, keepdims=True)) + top
    return jnp.exp(scores - total)


def attend_forward_body(heads, scale, chip_ref, *refs):
    pieces, mod_ref, bias_ref, parts = refs[:3], refs[3], refs[4], refs[5:10]
    rows_ref, normed_ref, qkv_ref, mixed_ref, attend_ref, output_ref = refs[10:16]
    partials, joined = refs[16:18], refs[18]
    place_rows(chip_ref[0], parts, (attend_ref, output_ref))
    join_rows(pieces, joined)
    seq = joined.shape[0] // 2
    model_width = joined.shape[1]
    width = output_ref.shape[1]
    for n in (1, 0):
        rows = slice(n * seq, (n + 1) * seq)
        normed, _ = normalize(joined[rows, :].astype(jnp.float32))
        normed_ref[rows, :] = normed
        shift = mod_ref[n : n + 1, :model_width]
        gain = mod_ref[n : n + 1, model_width : 2 * model_width]
        attend_in = (normed * (1.0 + gain) + shift).astype(jnp.bfloat16)
        rows_ref[rows, :] = attend_in
        qkv_ref[rows, :] = (dot(attend_in, attend_ref[...]) + bias_ref[...]).astype(jnp.bfloat16)
        mixed = []
        for head in range(heads):
            query, key, value = (
                qkv_ref[rows, j * width + head * HD : j * width + (head + 1) * HD]
                for j in range(3)
            )
            probs = attend_probs(query, key, scale).astype(jnp.bfloat16)
            mixed.append(dot(probs, value))
        mixed = jnp.concatenate(mixed, axis=1).astype(jnp.bfloat16)
        mixed_ref[rows, :] = mixed
        partials[n][...] = dot(mixed, output_ref[...], 1, 1)


def kernel_call(body, name, outs, operands, scratch, limit, flops, transcendentals=0):
    specs = [
        pl.BlockSpec(memory_space=pltpu.SMEM if x.dtype == jnp.int32 else pltpu.VMEM)
        for x in operands
    ]
    shapes = [jax.ShapeDtypeStruct(*out) for out in outs]
    moved = sum(x.size * x.dtype.itemsize for x in list(operands) + shapes)
    return pl.pallas_call(
        body,
        out_shape=shapes,
        in_specs=specs,
        out_specs=[pl.BlockSpec(memory_space=pltpu.VMEM)] * len(outs),
        scratch_shapes=scratch,
        compiler_params=pltpu.CompilerParams(vmem_limit_bytes=limit * 2**20),
        cost_estimate=pl.CostEstimate(
            flops=flops, bytes_accessed=moved, transcendentals=transcendentals
        ),
        name=name,
    )(*operands)


def attend_forward(chip, pieces, mod_full, bias_rows, parts, heads, scale):
    seq = pieces[-1].shape[0]
    rows, model_width = 2 * seq, pieces[0].shape[1]
    width = heads * HD
    return kernel_call(
        functools.partial(attend_forward_body, heads, scale),
        "attend_forward",
        [
            ((rows, model_width), jnp.bfloat16),
            ((rows, model_width), jnp.float32),
            ((rows, 3 * width), jnp.bfloat16),
            ((rows, width), jnp.bfloat16),
            ((model_width, 3 * width), jnp.bfloat16),
            ((model_width, width), jnp.bfloat16),
            ((seq, model_width), jnp.float32),
            ((seq, model_width), jnp.float32),
        ],
        [chip.reshape(1), *pieces, mod_full, bias_rows, *parts],
        [pltpu.VMEM((rows, model_width), jnp.bfloat16)],
        20,
        2 * rows * model_width * 4 * width + 8 * seq * seq * width,
        2 * 2 * heads * seq * seq,
    )


def feed_forward_body(chip_ref, *refs):
    pieces, ups, mod_ref, bias_ref, parts = refs[:4], refs[4:7], refs[7], refs[8], refs[9:14]
    act_ref, sums_ref, reduce_ref = refs[14:17]
    partials, blocks, expand_ref, joined = refs[17:19], refs[19:23], refs[23], refs[24]
    rows_ref, back_ref, low_ref, grad_ref = refs[25:29]
    place_rows(chip_ref[0], parts, (expand_ref, reduce_ref))
    join_rows(pieces, rows_ref)
    join_rows(ups, joined)
    seq = joined.shape[0] // 2
    model_width = joined.shape[1]
    sums = None
    for n in (1, 0):
        rows = slice(n * seq, (n + 1) * seq)
        value = dot(rows_ref[rows, :], expand_ref[...]) + bias_ref[...]
        gate = mod_ref[n : n + 1, 5 * model_width : 6 * model_width]
        back = (joined[rows, :].astype(jnp.float32) * gate).astype(jnp.bfloat16)
        back_ref[rows, :] = back
        grad_act = dot(back, reduce_ref[...])
        square = value * value
        slope = math.sqrt(2.0 / math.pi)
        bent = jnp.tanh(slope * (value + 0.044715 * (square * value)))
        share = 0.5 * (1.0 + bent)
        act_ref[rows, :] = (value * share).astype(jnp.bfloat16)
        curve = 0.5 * value * (1.0 - bent * bent) * (slope * (1.0 + 3 * 0.044715 * square))
        grad_pre = grad_act * (share + curve)
        part = jnp.sum(grad_pre, axis=0, keepdims=True)
        sums = part if sums is None else sums + part
        low = grad_pre.astype(jnp.bfloat16)
        low_ref[rows, :] = low
        partials[n][...] = dot(low, expand_ref[...], 1, 1)
    sums_ref[...] = sums
    width = act_ref.shape[1]
    grad_ref[:, :width] = dot(rows_ref[...], low_ref[...], 0, 0)
    grad_ref[:, width:] = dot(back_ref[...], act_ref[...], 0, 0)
    write_blocks(chip_ref[0], grad_ref, blocks)


def feed_forward(chip, pieces, ups, mod_full, bias, parts):
    seq = ups[-1].shape[0]
    rows, model_width = 2 * seq, pieces[0].shape[1]
    width = bias.shape[1]
    return kernel_call(
        feed_forward_body,
        "feed_forward",
        [
            ((rows, width), jnp.bfloat16),
            ((1, width), jnp.float32),
            ((model_width, width), jnp.bfloat16),
            ((seq, model_width), jnp.float32),
            ((seq, model_width), jnp.float32),
        ]
        + block_shapes(model_width, 2 * width),
        [chip.reshape(1), *pieces, *ups, mod_full, bias, *parts],
        [
            pltpu.VMEM((model_width, width), jnp.bfloat16),
            pltpu.VMEM((rows, model_width), jnp.bfloat16),
            pltpu.VMEM((rows, model_width), jnp.bfloat16),
            pltpu.VMEM((rows, model_width), jnp.bfloat16),
            pltpu.VMEM((rows, width), jnp.bfloat16),
            pltpu.VMEM((model_width, 2 * width), jnp.float32),
        ],
        36,
        10 * rows * model_width * width,
        rows * width,
    )


def write_blocks(chip, grad_ref, out_refs):
    keep_first, keep_second, send_first, send_second = out_refs
    count = keep_first.shape[0] // 2
    plan = [
        (keep_first, 0, (0, 2)),
        (keep_second, 1, (0, 1)),
        (send_first, 0, (1, 3)),
        (send_second, 1, (2, 3)),
    ]
    for out_ref, part, places in plan:
        for block, r in enumerate(places):
            source = pl.ds(pl.multiple_of((chip ^ r) * (2 * count) + part * count, 8), count)
            out_ref[block * count : (block + 1) * count, :] = grad_ref[source, :].astype(
                out_ref.dtype
            )


def block_shapes(height, width):
    shape = (height // 4, width)
    return [(shape, jnp.float32)] * 2 + [(shape, jnp.bfloat16)] * 2


def grad_blocks_body(chip_ref, *refs):
    out_refs, grad_ref = refs[-5:-1], refs[-1]
    start = 0
    for rows, cols in zip(refs[:-5:2], refs[1:-5:2]):
        stop = start + cols.shape[1]
        grad_ref[:, start:stop] = dot(rows[...], cols[...], 0, 0)
        start = stop
    write_blocks(chip_ref[0], grad_ref, out_refs)


def grad_blocks(pairs, chip):
    height = pairs[0][0].shape[1]
    width = sum(cols.shape[1] for _, cols in pairs)
    return kernel_call(
        grad_blocks_body,
        "grad_blocks",
        block_shapes(height, width),
        [chip.reshape(1)] + [part for pair in pairs for part in pair],
        [pltpu.VMEM((height, width), jnp.float32)],
        16,
        sum(2 * rows.size * cols.shape[1] for rows, cols in pairs),
    )


def first_step(sends):
    return [swap(sends[0], "dp", 2), swap(sends[1], "dp", 4)]


def middle_body(keep_first, keep_second, got_first, got_second, *outs):
    count = keep_first.shape[0] // 2
    for keep, got, base, going in (
        (keep_first, got_first, outs[0], outs[2]),
        (keep_second, got_second, outs[1], outs[3]),
    ):
        total = keep[...] + got[...].astype(jnp.float32)
        base[...] = total[:count]
        going[...] = total[count:].astype(jnp.bfloat16)


def middle_step(keeps, received):
    rows, width = keeps[0].shape
    shape = (rows // 2, width)
    outs = [(shape, jnp.float32)] * 2 + [(shape, jnp.bfloat16)] * 2
    return kernel_call(middle_body, "middle_step", outs, [*keeps, *received], [], 16, 0)


def second_step(going):
    return [swap(going[0], "dp", 4), swap(going[1], "dp", 2)]


def core_body(core_ref, base_first, base_second, got_first, got_second, mine, other):
    first = base_first[...] + got_first[...].astype(jnp.float32)
    second = base_second[...] + got_second[...].astype(jnp.float32)
    is_first = core_ref[0] == 0
    mine[...] = jnp.where(is_first, first, second)
    other[...] = jnp.where(is_first, second, first)


def core_step(core, bases, received):
    outs = [(bases[0].shape, jnp.float32)] * 2
    operands = [core.reshape(1), *bases, *received]
    return kernel_call(core_body, "core_step", outs, operands, [], 12, 0)


def half_body(own_ref, mine, other, kept, sent):
    is_own = own_ref[0] == 1
    kept[...] = jnp.where(is_own, mine[...], other[...])
    sent[...] = jnp.where(is_own, other[...], mine[...]).astype(jnp.bfloat16)


def half_step(is_own, mine, other):
    outs = [(mine.shape, jnp.float32), (mine.shape, jnp.bfloat16)]
    operands = [is_own.astype(jnp.int32).reshape(1), mine, other]
    return kernel_call(half_body, "half_step", outs, operands, [], 12, 0)


def mod_sum_body(partial, crossed, mod_bias, attend_bias, expand_bias, out):
    heads = attend_bias.shape[1]
    out[...] = jnp.zeros_like(out)
    out[0:2, :] = partial[0:2, :] + crossed[2:4, :] + mod_bias[...]
    out[2:4, :] = partial[2:4, :] + crossed[0:2, :] + mod_bias[...]
    out[4:5, :heads] = attend_bias[0:1, :]
    out[4:5, heads : 2 * heads] = attend_bias[1:2, :]
    out[4:5, 2 * heads :] = expand_bias[...]


def mod_place_body(place_ref, own, near, far, mod, qkv_bias, expand_bias, *pieces):
    z, half, is_own = place_ref[0], place_ref[1], place_ref[2]
    width = own.shape[1]
    for r, (source, start) in enumerate(((own, 0), (near, 0), (far, 0), (far, 8))):
        cols = pl.ds(pl.multiple_of((z ^ r) * width, 128), width)
        mod[0:1, cols] = source[pl.ds(start + half, 1), :]
        mod[1:2, cols] = source[pl.ds(start + 2 + half, 1), :]
    wide = expand_bias.shape[1]
    for k, piece in enumerate(pieces):
        piece[...] = mod[0:1, k * wide : (k + 1) * wide]
    bias = jnp.where(is_own == 1, own[4:5, :], far[4:5, :])
    heads = qkv_bias.shape[1] // 3
    qkv_bias[:, :heads] = bias[:, :heads]
    qkv_bias[:, heads : 2 * heads] = jnp.zeros_like(qkv_bias[:, heads : 2 * heads])
    qkv_bias[:, 2 * heads :] = bias[:, heads : 2 * heads]
    expand_bias[...] = bias[:, 2 * heads :]


def halve_body(own, got, keep, send):
    count = keep.shape[0]
    keep[...] = own[:count, :] + got[:count, :]
    send[...] = (own[count:, :] + got[count:, :]).astype(jnp.bfloat16)


def halve(own, got):
    shape = (own.shape[0] // 2, own.shape[1])
    outs = [(shape, jnp.float32), (shape, jnp.bfloat16)]
    return kernel_call(halve_body, "halve", outs, [own, got], [], 8, 0)


def column_sums(values):
    return jnp.sum(values, axis=0, keepdims=True)


def residual_body(keep, got, tokens, out_bias, gate, shift, gain, attend_out, residual, low):
    attend_out[...] = keep[...] + got[...].astype(jnp.float32) + out_bias[...]
    residual[...] = tokens[...].astype(jnp.float32) + gate[...] * attend_out[...]
    normed, _ = normalize(residual[...])
    low[...] = (normed * (1.0 + gain[...]) + shift[...]).astype(jnp.bfloat16)


def hidden_back_body(
    keep, got, residual, attend_out, upstream, gate_a, gain, gate_m, low, grad_residual, sums
):
    grad = keep[...] + got[...].astype(jnp.float32)
    normed, inverse = normalize(residual[...])
    up = upstream[...].astype(jnp.float32)
    total = up + norm_back(grad * (1.0 + gain[...]), normed, inverse)
    grad_residual[...] = total
    term = total * gate_a[...]
    low[...] = term.astype(jnp.bfloat16)
    sums[0:1, :] = column_sums(total * attend_out[...])
    sums[1:2, :] = column_sums(grad)
    sums[2:3, :] = column_sums(grad * normed)
    sums[3:4, :] = column_sums(term)
    sums[4:5, :] = column_sums(up * gate_m[...])
    sums[5:8, :] = jnp.zeros_like(sums[5:8, :])


def block_out_body(keep, got, residual, upstream, reduce_bias, gate, block, gate_sum):
    hidden_out = keep[...] + got[...].astype(jnp.float32) + reduce_bias[...]
    block[...] = (residual[...] + gate[...] * hidden_out).astype(jnp.bfloat16)
    gate_sum[...] = column_sums(upstream[...].astype(jnp.float32) * hidden_out)


def tokens_back_body(keep, got, tokens, grad_residual, gain, kept, send):
    count = kept.shape[0]
    grad = keep[...] + got[...].astype(jnp.float32)
    normed, inverse = normalize(tokens[...].astype(jnp.float32))
    total = grad_residual[...] + norm_back(grad * (1.0 + gain[...]), normed, inverse)
    kept[...] = total[:count, :]
    send[...] = total[count:, :].astype(jnp.bfloat16)


def outputs_body(half_ref, block, block_moved, kept, moved, block_out, tokens_grad):
    half, count = half_ref[0], kept.shape[0]
    block_out[half] = block[:count, :]
    block_out[1 - half] = block_moved[...]
    tokens_grad[half] = kept[...]
    tokens_grad[1 - half] = moved[...].astype(jnp.float32)


def owner_body(kept, moved, *outs):
    start = 0
    for out in outs:
        stop = start + out.shape[1]
        out[...] = kept[:, start:stop] + moved[:, start:stop].astype(jnp.float32)
        start = stop


def owner_sum(kept, moved, widths):
    outs = [((kept.shape[0], width), jnp.float32) for width in widths]
    return kernel_call(owner_body, "owner_sum", outs, [kept, moved], [], 8, 0)


def pack_body(norm, got, sums, gate_m, expand, bias, packed):
    wide = gate_m.shape[1]
    part = packed.shape[1] - wide
    both = norm[0:1, :] + got[...]
    packed[0:1, :wide] = both[:, :wide]
    packed[0:1, wide:] = both[:, wide : wide + part]
    packed[1:2, : wide - part] = both[:, wide + part :]
    packed[1:2, wide - part :] = sums[0:1, :]
    packed[2:3, :wide] = sums[1:2, :]
    packed[2:3, wide:] = sums[2:3, :part]
    packed[3:4, : wide - part] = sums[2:3, part:]
    packed[3:4, wide - part :] = gate_m[...]
    packed[4:5, :wide] = sums[3:4, :]
    packed[4:5, wide:] = sums[4:5, :part]
    packed[5:6, : wide - part] = sums[4:5, part:]
    packed[5:6, wide - part :] = jnp.zeros_like(packed[5:6, wide - part :])
    heads = bias.shape[1] // 3
    packed[6:7, :wide] = expand[...]
    packed[6:7, wide : wide + heads] = bias[:, :heads]
    packed[6:7, wide + heads :] = bias[:, 2 * heads :]
    packed[7:8, :] = jnp.zeros_like(packed[7:8, :])


def attend_owner_body(kept, moved, attend_grad, output_grad):
    width = output_grad.shape[1]
    for j in range(3):
        cols = slice(j * width, (j + 1) * width)
        attend_grad[j] = kept[:, cols] + moved[:, cols].astype(jnp.float32)
    output_grad[...] = kept[:, 3 * width :] + moved[:, 3 * width :].astype(jnp.float32)


def choose_body(place_ref, line, far, packed):
    z, half, own = place_ref[0], place_ref[1], place_ref[2]
    packed[pl.ds(half, 1), :] = line[pl.ds(z, 1), :]
    packed[pl.ds(1 - half, 1), :] = far[pl.ds(z, 1), :]
    packed[2:3, :] = jnp.where(own == 1, line[6:7, :] + far[6:7, :], 0.0)
    packed[3:5, :] = line[4:6, :] + far[4:6, :]
    packed[5:8, :] = jnp.zeros_like(packed[5:8, :])


def modulation_back_body(gathered, silu, weight, weight_grad, grad_silu, bias_grad, rest, rows):
    parts = [gathered[start : start + 8, :] for start in range(0, gathered.shape[0], 8)]
    for m, part in enumerate(parts):
        rows[2 * m : 2 * m + 2, :] = part[0:2, :]
    low = rows[...].astype(jnp.bfloat16)
    weight_grad[...] = dot(silu[...], low, 0, 0)
    grad_silu[...] = dot(low, weight[...], 1, 1)
    while len(parts) > 1:
        parts = [left + right for left, right in zip(parts[::2], parts[1::2])]
    bias_grad[...] = parts[0][0:1, :] + parts[0][1:2, :]
    rest[...] = parts[0][2:5, :]


def table_body(labels, cond, near, far, table, chosen):
    value = cond[...]
    share = 1.0 / (1.0 + jnp.exp(-value))
    grad = (near[...] + far[...]) * share * (1.0 + value * (1.0 - share))
    place = lax.broadcasted_iota(jnp.int32, (1, chosen.shape[1]), 1)
    for row in range(chosen.shape[0]):
        chosen[row : row + 1, :] = jnp.where(place == labels[row], 1.0, 0.0)
    table[...] = lax.dot_general(
        grad,
        chosen[...],
        (((0,), (0,)), ((), ())),
        precision=lax.Precision.HIGHEST,
        preferred_element_type=jnp.float32,
    )


def join_body(attend, output, joined):
    width = output.shape[1]
    for j in range(3):
        joined[:, j * width : (j + 1) * width] = attend[j]
    joined[:, 3 * width :] = output[...]


def attend_back_body(heads, scale, *refs):
    pieces = refs[:4]
    output_ref, qkv_ref, mixed_ref, attend_ref, normed_ref = refs[4:9]
    rows_ref, low_ref, sums_ref, norm_sums_ref = refs[9:13]
    partials = refs[13:15]
    join_rows(pieces, rows_ref)
    seq = rows_ref.shape[0] // 2
    model_width, width = output_ref.shape
    sums = None
    for n in (1, 0):
        rows = slice(n * seq, (n + 1) * seq)
        grad_mixed = dot(rows_ref[rows, :], output_ref[...]).astype(jnp.bfloat16)
        grads = [[], [], []]
        for head in range(heads):
            query, key, value = (
                qkv_ref[rows, j * width + head * HD : j * width + (head + 1) * HD]
                for j in range(3)
            )
            mixed = mixed_ref[rows, head * HD : (head + 1) * HD]
            up = grad_mixed[:, head * HD : (head + 1) * HD]
            probs = attend_probs(query, key, scale)
            delta = jnp.sum(
                up.astype(jnp.float32) * mixed.astype(jnp.float32), axis=1, keepdims=True
            )
            logit = (probs * (dot(up, value, 1, 1) - delta)).astype(jnp.bfloat16)
            grads[0].append(dot(logit, key) * scale)
            grads[1].append(dot(logit, query, 0, 0) * scale)
            grads[2].append(dot(probs.astype(jnp.bfloat16), up, 0, 0))
        whole = jnp.concatenate([part for group in grads for part in group], axis=1)
        part = jnp.sum(whole, axis=0, keepdims=True)
        sums = part if sums is None else sums + part
        low = whole.astype(jnp.bfloat16)
        low_ref[rows, :] = low
        partial = dot(low, attend_ref[...], 1, 1)
        partials[n][...] = partial
        norm_sums_ref[n : n + 1, :model_width] = jnp.sum(partial, axis=0, keepdims=True)
        norm_sums_ref[n : n + 1, model_width:] = jnp.sum(
            partial * normed_ref[rows, :], axis=0, keepdims=True
        )
    sums_ref[...] = sums


def attend_back(pieces, output_full, qkv, mixed, attend_full, normed, heads, scale):
    rows, model_width = normed.shape
    seq, width = rows // 2, mixed.shape[1]
    return kernel_call(
        functools.partial(attend_back_body, heads, scale),
        "attend_back",
        [
            ((rows, model_width), jnp.bfloat16),
            ((rows, 3 * width), jnp.bfloat16),
            ((1, 3 * width), jnp.float32),
            ((2, 2 * model_width), jnp.float32),
            ((seq, model_width), jnp.float32),
            ((seq, model_width), jnp.float32),
        ],
        [*pieces, output_full, qkv, mixed, attend_full, normed],
        [],
        20,
        2 * rows * model_width * 4 * width + 20 * seq * seq * width,
        2 * 2 * heads * seq * seq,
    )


def on_paired_device(
    tokens,
    cotangent,
    labels,
    timesteps,
    class_table,
    modulation_weight,
    modulation_bias,
    attend_weight,
    attend_bias,
    output_weight,
    output_bias,
    expand_weight,
    expand_bias,
    reduce_weight,
    reduce_bias,
):
    data_index = lax.axis_index("dp")
    tensor_index = lax.axis_index("tensor")
    core, chip = data_index & 1, data_index >> 1
    half = tensor_index >> 1
    is_own = half == core
    model_width = tokens.shape[2]
    row_share = modulation_weight.shape[0]
    head_width = attend_weight.shape[2]
    head_count = head_width // HD
    ff_width = expand_weight.shape[1]
    mod_width = modulation_weight.shape[1]
    latent_total = labels.shape[0]
    classes_total = class_table.shape[0]
    score_scale = 1.0 / math.sqrt(HD)

    count = tokens.shape[1]
    place = jnp.stack([tensor_index, half, is_own.astype(jnp.int32)])

    order = Order()
    mark, hold = order.mark, order.hold

    attn_shard = kernel_call(
        join_body,
        "join_weights",
        [((row_share, 4 * head_width), jnp.bfloat16)],
        [jnp.transpose(attend_weight, (1, 0, 2)), output_weight],
        [],
        4,
        0,
    )[0]
    mark(ATTN_SHARD, attn_shard)
    attn_far = mark(ATTN_FAR, swap(attn_shard, "tensor", 2))
    tokens_sent = pick(hold(TOKENS_SENT, tokens), 1 - half)
    tokens_half = jnp.concatenate([pick(tokens, half), swap(tokens_sent, "tensor", 2)])
    mark(TOKENS_HALF, tokens_half)
    labels, timesteps = (labels, timesteps)

    slot = jnp.arange(latent_total, dtype=jnp.int32)
    latent_ids = ((slot >> 1) ^ data_index) * 2 + (slot & 1)
    chosen = latent_ids[:, None] == slot[None, :]
    labels_rel = jnp.sum(jnp.where(chosen, labels[None, :], 0), axis=1)
    steps_rel = jnp.sum(jnp.where(chosen, timesteps[None, :], 0), axis=1)
    looked = lax.dynamic_slice_in_dim(
        jnp.take(class_table, labels_rel, axis=0), data_index * row_share, row_share, 1
    ).astype(jnp.float32)
    halfway = model_width // 2
    column = data_index * row_share + jnp.arange(row_share, dtype=jnp.int32)
    is_cos = column < halfway
    position = jnp.where(is_cos, column, column - halfway).astype(jnp.float32)
    frequency = jnp.exp(-math.log(10000.0) * position / halfway)
    angles = steps_rel.astype(jnp.float32)[:, None] * frequency[None, :]
    cond = looked + jnp.where(is_cos[None, :], jnp.cos(angles), jnp.sin(angles))
    silu_act = jax.nn.silu(cond).astype(jnp.bfloat16)
    partial = jnp.dot(silu_act, modulation_weight, preferred_element_type=jnp.float32)
    partial = partial[:8] + swap(partial[8:], "dp", 4)
    attn_share = near_weight(attn_shard, attn_far, is_own, core)
    mark(ATTN_SHARE, attn_share)
    partial = partial[:4] + swap(partial[4:], "dp", 2)
    partial = hold(PARTIAL_CORE, partial)
    ff_shard = jnp.concatenate([expand_weight, reduce_weight], axis=1)
    tokens_near = swap(tokens_half, "tensor", 1)
    mod_cols = kernel_call(
        mod_sum_body,
        "mod_sum",
        [((8, mod_width), jnp.float32)],
        [
            partial,
            swap(partial, "dp", 1),
            modulation_bias[None],
            attend_bias,
            expand_bias[None],
        ],
        [],
        4,
        0,
    )[0]
    attn_first = chip_first(attn_share)
    attn_parts = chip_second(attn_share, *attn_first)
    mark(ATTN_PARTS, attn_parts)
    mod_near = swap(mod_cols, "tensor", 1)
    mod_line = jnp.concatenate([mod_cols, mod_near])
    mark(MOD_LINE, mod_line)
    mod_far = swap(mod_line, "tensor", 2)
    ff_far = mark(FF_FAR, swap(hold(FF_SHARD, ff_shard), "tensor", 2))
    tokens_across = swap(jnp.concatenate([tokens_half, tokens_near]), "dp", 1)
    row = ((1, model_width), jnp.float32)
    mod_full, qkv_bias, expand_row, _, gain_a, gate_a, shift_m, gain_m, gate_m = kernel_call(
        mod_place_body,
        "mod_place",
        [
            ((2, 6 * model_width), jnp.float32),
            ((1, 3 * head_width), jnp.float32),
            ((1, ff_width), jnp.float32),
        ]
        + [row] * 6,
        [place, mod_cols, mod_near, hold(MOD_PLACE, mod_far)],
        [],
        4,
        0,
    )
    ff_share = near_weight(ff_shard, hold(FF_FAR, ff_far), is_own, core)
    mark(FF_SHARE, ff_share)
    upstream_sent = hold(UPSTREAM_SENT, pick(cotangent, 1 - half))
    upstream_far = swap(upstream_sent, "tensor", 2)
    ff_first = chip_first(ff_share)

    (
        attend_rows,
        normed_all,
        projected,
        mixed_rows,
        attend_full,
        output_full,
        own_partial,
        other_partial,
    ) = attend_forward(
        chip,
        [tokens_half, tokens_near, hold(ATTEND, tokens_across)],
        mod_full,
        qkv_bias,
        attn_parts,
        head_count,
        score_scale,
    )
    keep, send = halve(own_partial, swap(other_partial, "dp", 1))
    mark(ATTEND_SEND, send)
    upstream_half = jnp.concatenate([pick(cotangent, half), upstream_far])
    mark(UPSTREAM_HALF, upstream_half)
    ff_first = hold(FF_SECOND, ff_first)
    ff_parts = chip_second(ff_share, *ff_first)
    got = swap(send, "tensor", 1)
    upstream_near = swap(upstream_half, "tensor", 1)
    attend_out, residual, hidden_in = kernel_call(
        residual_body,
        "residual",
        [(keep.shape, jnp.float32), (keep.shape, jnp.float32), (keep.shape, jnp.bfloat16)],
        [
            keep,
            hold(RESIDUAL, got),
            tokens_half,
            output_bias[None],
            gate_a,
            shift_m,
            gain_m,
        ],
        [],
        8,
        0,
    )
    hidden_pieces = collect_pairs(hidden_in)
    upstream_line = jnp.concatenate([upstream_half, upstream_near])
    upstream_across = swap(upstream_line, "dp", 1)

    (
        activated,
        grad_expand_bias,
        reduce_full,
        own_partial,
        other_partial,
        *ff_blocks,
    ) = feed_forward(
        chip,
        hidden_pieces,
        [upstream_half, upstream_near, upstream_across],
        mod_full,
        expand_row,
        ff_parts,
    )
    mark(FEED, own_partial)
    keep, send = halve(own_partial, swap(other_partial, "dp", 1))
    got = swap(send, "tensor", 1)
    ff_first = first_step(ff_blocks[2:])
    seq_len = tokens_across.shape[0]
    act_later = hold(ACTIVATED, activated)
    other_out, own_out = (
        jnp.einsum("sf,of->so", act_half, reduce_full, preferred_element_type=jnp.float32)
        for act_half in (act_later[seq_len:], act_later[:seq_len])
    )
    out_keep, out_send = halve(own_out, swap(other_out, "dp", 1))
    mark(OUT_SEND, out_send)
    output_low, grad_residual, row_sums = kernel_call(
        hidden_back_body,
        "hidden_back",
        [(keep.shape, jnp.bfloat16), (keep.shape, jnp.float32), ((8, model_width), jnp.float32)],
        [
            keep,
            hold(HIDDEN_BACK, got),
            residual,
            attend_out,
            upstream_half,
            gate_a,
            gain_m,
            gate_m,
        ],
        [],
        8,
        0,
    )
    output_pieces = collect_pairs(output_low)
    mark(OUTPUT_NEAR, output_pieces[1])
    block_own, gate_sum = kernel_call(
        block_out_body,
        "block_out",
        [(keep.shape, jnp.bfloat16), row],
        [
            out_keep,
            swap(out_send, "tensor", 1),
            residual,
            upstream_half,
            reduce_bias[None],
            gate_m,
        ],
        [],
        8,
        0,
    )
    mark(BLOCK_OUT, block_own)

    def ff_middle():
        *bases, going, going_second = middle_step(ff_blocks[:2], hold(FF_MIDDLE, ff_first))
        mark(FF_GOING, going)
        return bases, mark(FF_BACK_SECOND, second_step([going, going_second]))

    ff_bases, ff_second = ff_middle()

    (
        output_rows,
        projected_low,
        bias_sums,
        norm_sums,
        own_partial,
        other_partial,
    ) = attend_back(
        hold(ATTEND_BACK, output_pieces),
        output_full,
        projected,
        mixed_rows,
        attend_full,
        normed_all,
        head_count,
        score_scale,
    )
    block_moved = swap(block_own[count:], "tensor", 2)
    norm_crossed = mark(NORM_CROSSED, swap(norm_sums[1:], "dp", 1))
    ff_mine, ff_other = core_step(core, ff_bases, hold(FF_CORE, ff_second))
    mark(FF_CORE, ff_mine)
    ff_kept, ff_sent = half_step(is_own, ff_mine, swap(ff_other, "dp", 1))
    mark(FF_HALF, ff_sent)

    line = kernel_call(
        pack_body,
        "pack",
        [((8, mod_width), jnp.float32)],
        [
            norm_sums,
            hold(PACK, norm_crossed),
            row_sums,
            gate_sum,
            grad_expand_bias,
            bias_sums,
        ],
        [],
        4,
        0,
    )[0]
    mark(PACK, line)
    keep, send = halve(own_partial, swap(other_partial, "dp", 1))
    grad_got = swap(send, "tensor", 1)
    attn_blocks = grad_blocks(
        [(attend_rows, hold(ATTN_BLOCKS, projected_low)), (output_rows, mixed_rows)], chip
    )
    mark(ATTN_BLOCKS, attn_blocks[2])
    attn_first = first_step(attn_blocks[2:])
    summed = lax.broadcasted_iota(jnp.int32, line.shape, 0) < 6
    near = hold(LINE, swap(line, "tensor", 1))
    line = line + jnp.where(summed, near, 0.0)
    far = mark(FAR, swap(hold(LINE_FAR, line), "tensor", 2))
    packed = kernel_call(
        choose_body,
        "choose",
        [((8, mod_width), jnp.float32)],
        [place, line, far],
        [],
        4,
        0,
    )[0]
    ff_moved = mark(FF_MOVED, swap(ff_sent, "tensor", 2))
    tokens_kept, back_sent = kernel_call(
        tokens_back_body,
        "tokens_back",
        [((count, model_width), jnp.float32), ((count, model_width), jnp.bfloat16)],
        [keep, grad_got, tokens_half, grad_residual, gain_a],
        [],
        8,
        0,
    )
    tokens_moved = swap(hold(BACK_SENT, back_sent), "tensor", 2)
    *attn_bases, attn_going, attn_going_second = middle_step(
        attn_blocks[:2], attn_first
    )
    attn_second = second_step([attn_going, attn_going_second])
    packed = jnp.concatenate([packed, swap(packed, "dp", 1)])
    packed = jnp.concatenate([packed, swap(packed, "dp", 2)])
    attn_mine, attn_other = core_step(core, attn_bases, attn_second)
    packed = jnp.concatenate([packed, swap(hold(PACKED_Y, packed), "dp", 4)])
    modulation_weight_grad, grad_silu, modulation_bias_grad, rest = kernel_call(
        modulation_back_body,
        "modulation_back",
        [
            ((row_share, mod_width), jnp.float32),
            ((latent_total, row_share), jnp.float32),
            ((1, mod_width), jnp.float32),
            ((3, mod_width), jnp.float32),
        ],
        [packed, silu_act, modulation_weight],
        [pltpu.VMEM((latent_total, mod_width), jnp.float32)],
        8,
        4 * latent_total * row_share * mod_width,
    )
    mark(MODULATION_BACK, grad_silu)
    attn_kept, attn_sent = half_step(is_own, attn_mine, hold(ATTN_HALF, swap(attn_other, "dp", 1)))
    attn_moved = swap(hold(ATTN_SENT, attn_sent), "tensor", 2)
    near = grad_silu + swap(hold(GRAD_SILU, grad_silu), "tensor", 1)
    mark(NEAR, near)
    table_grad = kernel_call(
        table_body,
        "table",
        [((row_share, classes_total), jnp.float32)],
        [labels_rel, cond, near, hold(TABLE, swap(near, "tensor", 2))],
        [pltpu.VMEM((latent_total, classes_total), jnp.float32)],
        4,
        0,
    )[0]
    expand_grad, reduce_grad = owner_sum(
        ff_kept, hold(FF_OWNER, ff_moved), [ff_width, ff_width]
    )
    attend_grad, output_grad = kernel_call(
        attend_owner_body,
        "owner_sum",
        [((3, row_share, head_width), jnp.float32), (output_weight.shape, jnp.float32)],
        [attn_kept, attn_moved],
        [],
        8,
        0,
    )
    block_output, tokens_grad = kernel_call(
        outputs_body,
        "outputs",
        [(tokens.shape, jnp.bfloat16), (tokens.shape, jnp.float32)],
        [half.reshape(1), block_own, block_moved, tokens_kept, hold(OUTPUTS, tokens_moved)],
        [],
        8,
        0,
    )
    wide = model_width
    return (
        block_output,
        tokens_grad,
        table_grad.T,
        modulation_weight_grad,
        modulation_bias_grad[0],
        jnp.transpose(attend_grad, (1, 0, 2)),
        rest[0, wide:].reshape(2, head_width),
        output_grad,
        rest[1, :wide],
        expand_grad,
        rest[0, :wide],
        reduce_grad,
        jnp.concatenate([rest[1, wide:], rest[2, : 2 * wide - mod_width]]),
    )


def solution(mesh):
    paired = mesh.shape["dp"] == 8 and mesh.shape["tensor"] == 4
    per_device = on_paired_device if paired else on_device
    placed = (
        P("dp", "tensor", None),
        P("dp", "tensor", None),
        P(),
        P(),
        P(),
        P("dp", "tensor"),
        P("tensor"),
        P("dp", None, "tensor"),
        P(None, "tensor"),
        P("dp", "tensor"),
        P(),
        P("dp", "tensor"),
        P("tensor"),
        P("dp", "tensor"),
        P(),
    )
    return jax.shard_map(
        per_device,
        mesh=mesh,
        in_specs=placed,
        out_specs=(
            P("dp", "tensor", None),
            P("dp", "tensor", None),
            P(None, "dp"),
            P("dp", "tensor"),
            P("tensor"),
            P("dp", None, "tensor"),
            P(None, "tensor"),
            P("dp", "tensor"),
            P(),
            P("dp", "tensor"),
            P("tensor"),
            P("dp", "tensor"),
            P(),
        ),
        check_vma=False,
    )
```

```python
import functools
import math

import jax
import jax.numpy as jnp
from jax import lax
from jax.experimental import pallas as pl
from jax.experimental.pallas import tpu as pltpu
from jax.sharding import PartitionSpec as P

HD = 64


norm_eps = 1e-06


def timestep_features(steps_in, model_width):
    halfway = model_width // 2
    frequency = jnp.exp(-math.log(10000.0) * jnp.arange(halfway, dtype=jnp.float32) / halfway)
    angles = steps_in.astype(jnp.float32)[:, None] * frequency[None, :]
    return jnp.concatenate([jnp.cos(angles), jnp.sin(angles)], axis=1)


def condition(label_ids, steps_in, class_table):
    looked = jnp.take(class_table, label_ids, axis=0).astype(jnp.float32)
    return looked + timestep_features(steps_in, class_table.shape[1])


def silu_back(inputs, upstream):
    sigmoid = jax.nn.sigmoid(inputs)
    return upstream * sigmoid * (1.0 + inputs * (1.0 - sigmoid))


def gelu_back(inputs, upstream):
    outputs, pullback = jax.vjp(lambda inner: jax.nn.gelu(inner, approximate=True), inputs)
    return pullback(upstream)[0]


def normalize(inputs):
    centered = inputs - jnp.mean(inputs, axis=-1, keepdims=True)
    inverse = lax.rsqrt(jnp.mean(centered * centered, axis=-1, keepdims=True) + norm_eps)
    return (centered * inverse, inverse)


def norm_back(upstream, normed, inverse):
    return inverse * (
        upstream
        - jnp.mean(upstream, axis=-1, keepdims=True)
        - normed * jnp.mean(upstream * normed, axis=-1, keepdims=True)
    )


def collect(local_rows):
    return lax.all_gather(local_rows, "tensor", axis=1, tiled=True)


def spread(partial_rows):
    return lax.psum_scatter(partial_rows, "tensor", scatter_dimension=1, tiled=True)


def on_device(
    tokens,
    cotangent,
    labels,
    timesteps,
    class_table,
    modulation_weight,
    modulation_bias,
    attend_weight,
    attend_bias,
    output_weight,
    output_bias,
    expand_weight,
    expand_bias,
    reduce_weight,
    reduce_bias,
):
    tensor_count = lax.axis_size("tensor")
    data_index = lax.axis_index("dp")
    tensor_index = lax.axis_index("tensor")
    latent_count = tokens.shape[0]
    model_width = tokens.shape[2]
    row_share = modulation_weight.shape[0]
    head_width = attend_weight.shape[2]
    head_count = head_width // HD
    classes_total = class_table.shape[0]
    score_scale = 1.0 / math.sqrt(HD)
    row_start = data_index * row_share
    zero_index = jnp.zeros((), jnp.int32)
    modulation_full, attend_full, output_full, expand_full, reduce_full = (
        lax.all_gather(modulation_weight, "dp", axis=0, tiled=True),
        lax.all_gather(attend_weight, "dp", axis=0, tiled=True),
        lax.all_gather(output_weight, "dp", axis=0, tiled=True),
        lax.all_gather(expand_weight, "dp", axis=0, tiled=True),
        lax.all_gather(reduce_weight, "dp", axis=0, tiled=True),
    )
    own_labels = lax.dynamic_slice_in_dim(labels, data_index * latent_count, latent_count)
    own_steps = lax.dynamic_slice_in_dim(timesteps, data_index * latent_count, latent_count)
    cond_own = condition(own_labels, own_steps, class_table)
    silu_own = jax.nn.silu(cond_own).astype(jnp.bfloat16)
    modulation_share = jnp.dot(silu_own, modulation_full, preferred_element_type=jnp.float32)
    modulation = lax.all_gather(modulation_share + modulation_bias, "tensor", axis=1, tiled=True)
    pieces = modulation.reshape(latent_count, 6, 1, model_width)
    shift_attend, scale_attend, gate_attend = (pieces[:, 0], pieces[:, 1], pieces[:, 2])
    shift_hidden, scale_hidden, gate_hidden = (pieces[:, 3], pieces[:, 4], pieces[:, 5])
    tokens_wide = tokens.astype(jnp.float32)
    normed_first, inverse_first = normalize(tokens_wide)
    attend_in = (normed_first * (1.0 + scale_attend) + shift_attend).astype(jnp.bfloat16)
    attend_rows = collect(attend_in)
    seq_len = attend_rows.shape[1]
    bias_rows = jnp.stack([attend_bias[0], jnp.zeros_like(attend_bias[0]), attend_bias[1]])
    projected = (
        jnp.einsum("bsd,dje->jbse", attend_rows, attend_full, preferred_element_type=jnp.float32)
        + bias_rows[:, None, None, :]
    ).astype(jnp.bfloat16)
    split_heads = projected.reshape(3, latent_count, seq_len, head_count, HD)
    query_heads, key_heads, value_heads = (split_heads[0], split_heads[1], split_heads[2])
    scores = (
        jnp.einsum("bqhe,bkhe->bhqk", query_heads, key_heads, preferred_element_type=jnp.float32)
        * score_scale
    )
    log_total = jax.nn.logsumexp(scores, axis=-1)
    probs = jnp.exp(scores - log_total[..., None]).astype(jnp.bfloat16)
    mixed = jnp.einsum(
        "bhqk,bkhe->bqhe", probs, value_heads, preferred_element_type=jnp.float32
    ).astype(jnp.bfloat16)
    mixed_rows = mixed.reshape(latent_count, seq_len, head_width)
    attend_out = (
        spread(
            jnp.einsum("bsi,oi->bso", mixed_rows, output_full, preferred_element_type=jnp.float32)
        )
        + output_bias
    )
    residual = tokens_wide + gate_attend * attend_out
    normed_second, inverse_second = normalize(residual)
    hidden_in = (normed_second * (1.0 + scale_hidden) + shift_hidden).astype(jnp.bfloat16)
    hidden_rows = collect(hidden_in)
    pre_act = (
        jnp.einsum("bsd,df->bsf", hidden_rows, expand_full, preferred_element_type=jnp.float32)
        + expand_bias
    )
    activated = jax.nn.gelu(pre_act, approximate=True).astype(jnp.bfloat16)
    hidden_out = (
        spread(
            jnp.einsum("bsf,of->bso", activated, reduce_full, preferred_element_type=jnp.float32)
        )
        + reduce_bias
    )
    block_output = (residual + gate_hidden * hidden_out).astype(jnp.bfloat16)
    upstream = cotangent.astype(jnp.float32)
    grad_gate_hidden = jnp.sum(upstream * hidden_out, axis=1)
    reduce_term = upstream * gate_hidden
    grad_reduce_bias = jnp.sum(reduce_term, axis=(0, 1))
    reduce_rows = collect(reduce_term.astype(jnp.bfloat16))
    grad_act = jnp.einsum(
        "bso,of->bsf", reduce_rows, reduce_full, preferred_element_type=jnp.float32
    )
    grad_reduce = jnp.einsum(
        "bso,bsf->of", reduce_rows, activated, preferred_element_type=jnp.float32
    )
    grad_pre = gelu_back(pre_act, grad_act)
    grad_expand_bias = jnp.sum(grad_pre, axis=(0, 1))
    grad_pre_low = grad_pre.astype(jnp.bfloat16)
    grad_expand = jnp.einsum(
        "bsd,bsf->df", hidden_rows, grad_pre_low, preferred_element_type=jnp.float32
    )
    grad_hidden_in = spread(
        jnp.einsum("bsf,df->bsd", grad_pre_low, expand_full, preferred_element_type=jnp.float32)
    )
    grad_shift_hidden = jnp.sum(grad_hidden_in, axis=1)
    grad_scale_hidden = jnp.sum(grad_hidden_in * normed_second, axis=1)
    grad_residual = upstream + norm_back(
        grad_hidden_in * (1.0 + scale_hidden), normed_second, inverse_second
    )
    grad_gate_attend = jnp.sum(grad_residual * attend_out, axis=1)
    output_term = grad_residual * gate_attend
    grad_output_bias = jnp.sum(output_term, axis=(0, 1))
    output_rows = collect(output_term.astype(jnp.bfloat16))
    grad_output = jnp.einsum(
        "bso,bsi->oi", output_rows, mixed_rows, preferred_element_type=jnp.float32
    )
    grad_mixed = jnp.einsum(
        "bso,oi->bsi", output_rows, output_full, preferred_element_type=jnp.float32
    ).astype(jnp.bfloat16)
    grad_mixed_heads = grad_mixed.reshape(latent_count, seq_len, head_count, HD)
    recomputed = jnp.exp(
        jnp.einsum("bqhe,bkhe->bhqk", query_heads, key_heads, preferred_element_type=jnp.float32)
        * score_scale
        - log_total[..., None]
    )
    row_dot = jnp.einsum(
        "bqhe,bqhe->bhq", grad_mixed_heads, mixed, preferred_element_type=jnp.float32
    )
    grad_probs = jnp.einsum(
        "bqhe,bkhe->bhqk", grad_mixed_heads, value_heads, preferred_element_type=jnp.float32
    )
    grad_logit = (recomputed * (grad_probs - row_dot[..., None])).astype(jnp.bfloat16)
    grad_query = (
        jnp.einsum("bhqk,bkhe->bqhe", grad_logit, key_heads, preferred_element_type=jnp.float32)
        * score_scale
    )
    grad_key = (
        jnp.einsum("bhqk,bqhe->bkhe", grad_logit, query_heads, preferred_element_type=jnp.float32)
        * score_scale
    )
    grad_value = jnp.einsum(
        "bhqk,bqhe->bkhe", probs, grad_mixed_heads, preferred_element_type=jnp.float32
    )
    grad_projected = jnp.stack([grad_query, grad_key, grad_value]).reshape(
        3, latent_count, seq_len, head_width
    )
    grad_attend_bias = jnp.stack(
        [jnp.sum(grad_projected[0], axis=(0, 1)), jnp.sum(grad_projected[2], axis=(0, 1))]
    )
    grad_projected_low = grad_projected.astype(jnp.bfloat16)
    grad_attend = jnp.einsum(
        "bsd,jbse->dje", attend_rows, grad_projected_low, preferred_element_type=jnp.float32
    )
    grad_attend_in = spread(
        jnp.einsum(
            "jbse,dje->bsd", grad_projected_low, attend_full, preferred_element_type=jnp.float32
        )
    )
    grad_shift_attend = jnp.sum(grad_attend_in, axis=1)
    grad_scale_attend = jnp.sum(grad_attend_in * normed_first, axis=1)
    tokens_grad = grad_residual + norm_back(
        grad_attend_in * (1.0 + scale_attend), normed_first, inverse_first
    )
    grad_modulation_rows = jnp.concatenate(
        [
            grad_shift_attend,
            grad_scale_attend,
            grad_gate_attend,
            grad_shift_hidden,
            grad_scale_hidden,
            grad_gate_hidden,
        ],
        axis=1,
    )
    grad_modulation = lax.psum_scatter(
        grad_modulation_rows, "tensor", scatter_dimension=1, tiled=True
    )
    grad_modulation_bias = jnp.sum(grad_modulation, axis=0)
    grad_modulation_low = grad_modulation.astype(jnp.bfloat16)
    grad_modulation_weight = jnp.einsum(
        "ld,lc->dc", silu_own, grad_modulation_low, preferred_element_type=jnp.float32
    )
    grad_modulation_weight, grad_attend, grad_output, grad_expand, grad_reduce = (
        lax.psum_scatter(grad_modulation_weight, "dp", scatter_dimension=0, tiled=True),
        lax.psum_scatter(grad_attend, "dp", scatter_dimension=0, tiled=True),
        lax.psum_scatter(grad_output, "dp", scatter_dimension=0, tiled=True),
        lax.psum_scatter(grad_expand, "dp", scatter_dimension=0, tiled=True),
        lax.psum_scatter(grad_reduce, "dp", scatter_dimension=0, tiled=True),
    )
    grad_silu = jnp.einsum(
        "lc,dc->ld", grad_modulation_low, modulation_full, preferred_element_type=jnp.float32
    )
    grad_cond = silu_back(cond_own, grad_silu)
    shard_rows = lax.all_gather(grad_cond, ("dp", "tensor"), axis=0, tiled=True)
    row_count = shard_rows.shape[0]
    positions = jnp.arange(row_count, dtype=jnp.int32)
    latent_ids = positions // latent_count // tensor_count * latent_count + positions % latent_count
    picked = jnp.take(labels, latent_ids)
    onehot = (picked[:, None] == jnp.arange(classes_total, dtype=jnp.int32)[None, :]).astype(
        jnp.float32
    )
    columns = lax.dynamic_slice_in_dim(shard_rows, row_start, row_share, 1)
    table_grad = jnp.einsum(
        "rc,rd->cd",
        onehot,
        columns,
        precision=lax.Precision.HIGHEST,
        preferred_element_type=jnp.float32,
    )
    expand_share = grad_expand_bias.shape[0]
    modulation_cols = grad_modulation_bias.shape[0]
    padded_attend = lax.dynamic_update_slice(
        jnp.zeros((2, head_width * tensor_count), jnp.float32),
        grad_attend_bias,
        (zero_index, tensor_index * head_width),
    )
    padded_expand = lax.dynamic_update_slice(
        jnp.zeros((expand_share * tensor_count,), jnp.float32),
        grad_expand_bias,
        (tensor_index * expand_share,),
    )
    padded_modulation = lax.dynamic_update_slice(
        jnp.zeros((modulation_cols * tensor_count,), jnp.float32),
        grad_modulation_bias,
        (tensor_index * modulation_cols,),
    )
    summed_attend, summed_expand, summed_modulation, summed_output, summed_reduce = lax.psum(
        (padded_attend, padded_expand, padded_modulation, grad_output_bias, grad_reduce_bias),
        ("dp", "tensor"),
    )
    attend_bias_grad = lax.dynamic_slice_in_dim(
        summed_attend, tensor_index * head_width, head_width, 1
    )
    expand_bias_grad = lax.dynamic_slice_in_dim(
        summed_expand, tensor_index * expand_share, expand_share, 0
    )
    modulation_bias_grad = lax.dynamic_slice_in_dim(
        summed_modulation, tensor_index * modulation_cols, modulation_cols, 0
    )
    return (
        block_output,
        tokens_grad,
        table_grad,
        grad_modulation_weight,
        modulation_bias_grad,
        grad_attend,
        attend_bias_grad,
        grad_output,
        summed_output,
        grad_expand,
        expand_bias_grad,
        grad_reduce,
        summed_reduce,
    )


def swap(values, axis, mask):
    count = lax.axis_size(axis)
    return lax.ppermute(values, axis, [(place, place ^ mask) for place in range(count)])


def pick(values, place):
    return lax.dynamic_index_in_dim(values, place, 0, keepdims=False)


def collect_pairs(rows):
    near = swap(rows, "tensor", 1)
    return [rows, near, swap(rows, "dp", 1), swap(near, "dp", 1)]


(
    ACTIVATED,
    ATTEND,
    ATTEND_BACK,
    ATTEND_SEND,
    ATTN_BLOCKS,
    ATTN_CORE,
    ATTN_FAR,
    ATTN_FIRST,
    ATTN_HALF,
    ATTN_PARTS,
    ATTN_SENT,
    ATTN_SHARD,
    ATTN_SHARE,
    BLOCK_OUT,
    FEED,
    FEED_SEND,
    FF_BLOCKS,
    FF_CORE,
    FF_FAR,
    FF_GOING,
    FF_HALF,
    FF_MIDDLE,
    FF_MOVED,
    FF_OWNER,
    FF_SECOND,
    FF_SHARD,
    FF_SHARE,
    GRAD_SILU,
    HIDDEN_BACK,
    LINE,
    LINE_FAR,
    LINE_NEAR,
    MOD_LINE,
    MOD_PLACE,
    MODULATION_BACK,
    NEAR,
    NORM_CROSSED,
    OUT_SEND,
    OUTPUT_NEAR,
    OUTPUTS,
    PACK,
    PACKED_X,
    PACKED_Y,
    PARTIAL_CORE,
    TABLE,
    TOKENS_HALF,
    TOKENS_SENT,
    UPSTREAM_FAR,
    UPSTREAM_SENT,
) = range(49)

HOLDS = {
    TOKENS_SENT: (ATTN_SHARD,),
    PARTIAL_CORE: (ATTN_FAR, ATTN_SHARE,),
    FF_SHARD: (ATTN_FAR, TOKENS_HALF,),
    MOD_LINE: (ATTN_FIRST,),
    MOD_PLACE: (ATTN_PARTS,),
    FF_FAR: (MOD_LINE,),
    UPSTREAM_SENT: (FF_FAR, FF_SHARE,),
    ATTEND: (FF_SHARE,),
    UPSTREAM_FAR: (ATTEND_SEND,),
    FF_SECOND: (ATTEND_SEND,),
    FF_BLOCKS: (FEED_SEND,),
    ACTIVATED: (FEED,),
    HIDDEN_BACK: (OUT_SEND,),
    FF_MIDDLE: (BLOCK_OUT, OUTPUT_NEAR,),
    ATTEND_BACK: (BLOCK_OUT, FF_GOING,),
    PACK: (FF_CORE,),
    ATTN_BLOCKS: (FF_HALF, PACK,),
    LINE_NEAR: (FF_CORE,),
    LINE: (FF_HALF,),
    LINE_FAR: (ATTN_BLOCKS, FF_HALF,),
    FF_CORE: (NORM_CROSSED,),
    PACKED_X: (FF_CORE, FF_HALF,),
    PACKED_Y: (FF_MOVED,),
    MODULATION_BACK: (ATTN_CORE,),
    ATTN_HALF: (MODULATION_BACK,),
    ATTN_SENT: (FF_MOVED, MODULATION_BACK,),
    GRAD_SILU: (FF_MOVED,),
    TABLE: (FF_MOVED,),
    FF_OWNER: (NEAR,),
    OUTPUTS: (MODULATION_BACK,),
}


class Order:
    def __init__(self):
        self.marks = {}

    def mark(self, name, values):
        self.marks[name] = values
        return values

    def hold(self, name, values):
        earlier = [self.marks[mark] for mark in HOLDS.get(name, ())]
        return lax.optimization_barrier((values, earlier))[0] if earlier else values


def near_weight(shard, far, is_own, core):
    mine = jnp.where(is_own, shard, far)
    other = swap(jnp.where(is_own, far, shard), "dp", 1)
    first = core == 0
    return jnp.concatenate(
        [jnp.where(first, mine, other), jnp.where(first, other, mine)], axis=0
    )


def chip_first(share):
    count = share.shape[0] // 2
    return swap(share[:count], "dp", 2), swap(share[count:], "dp", 4)


def chip_second(share, first_x, second_y):
    count = share.shape[0] // 2
    first_y = swap(jnp.concatenate([share[:count], first_x]), "dp", 4)
    second_x = swap(jnp.concatenate([share[count:], second_y]), "dp", 2)
    return [share, first_x, second_y, first_y, second_x]


def place_rows(chip, parts, out_refs):
    share, first_x, second_y, first_y, second_x = parts
    count = first_x.shape[0]
    plan = [
        (0, 0, share, 0),
        (0, 1, share, 1),
        (1, 0, first_x, 0),
        (1, 1, second_x, 0),
        (2, 0, first_y, 0),
        (2, 1, second_y, 0),
        (3, 0, first_y, 1),
        (3, 1, second_x, 1),
    ]
    for r, part, source, block in plan:
        target = pl.ds(pl.multiple_of((chip ^ r) * (2 * count) + part * count, 16), count)
        start = 0
        for out_ref in out_refs:
            stop = start + out_ref.shape[1]
            out_ref[target, :] = source[block * count : (block + 1) * count, start:stop]
            start = stop


def dot(left, right, left_dim=1, right_dim=0):
    return lax.dot_general(
        left, right, (((left_dim,), (right_dim,)), ((), ())), preferred_element_type=jnp.float32
    )


def join_rows(pieces, target):
    start = 0
    for piece in pieces:
        target[start : start + piece.shape[0], :] = piece[...]
        start += piece.shape[0]


def attend_probs(query, key, scale):
    scores = dot(query, key, 1, 1) * scale
    top = jnp.max(scores, axis=1, keepdims=True)
    total = jnp.log(jnp.sum(jnp.exp(scores - top), axis=1, keepdims=True)) + top
    return jnp.exp(scores - total)


def attend_forward_body(heads, scale, chip_ref, *refs):
    pieces, mod_ref, bias_ref, parts = refs[:3], refs[3], refs[4], refs[5:10]
    rows_ref, normed_ref, qkv_ref, mixed_ref, attend_ref, output_ref = refs[10:16]
    partials, joined = refs[16:18], refs[18]
    place_rows(chip_ref[0], parts, (attend_ref, output_ref))
    join_rows(pieces, joined)
    seq = joined.shape[0] // 2
    model_width = joined.shape[1]
    width = output_ref.shape[1]
    for n in (1, 0):
        rows = slice(n * seq, (n + 1) * seq)
        normed, _ = normalize(joined[rows, :].astype(jnp.float32))
        normed_ref[rows, :] = normed
        shift = mod_ref[n : n + 1, :model_width]
        gain = mod_ref[n : n + 1, model_width : 2 * model_width]
        attend_in = (normed * (1.0 + gain) + shift).astype(jnp.bfloat16)
        rows_ref[rows, :] = attend_in
        qkv_ref[rows, :] = (dot(attend_in, attend_ref[...]) + bias_ref[...]).astype(jnp.bfloat16)
        mixed = []
        for head in range(heads):
            query, key, value = (
                qkv_ref[rows, j * width + head * HD : j * width + (head + 1) * HD]
                for j in range(3)
            )
            probs = attend_probs(query, key, scale).astype(jnp.bfloat16)
            mixed.append(dot(probs, value))
        mixed = jnp.concatenate(mixed, axis=1).astype(jnp.bfloat16)
        mixed_ref[rows, :] = mixed
        partials[n][...] = dot(mixed, output_ref[...], 1, 1)


def kernel_call(body, name, outs, operands, scratch, limit, flops, transcendentals=0):
    specs = [
        pl.BlockSpec(memory_space=pltpu.SMEM if x.dtype == jnp.int32 else pltpu.VMEM)
        for x in operands
    ]
    shapes = [jax.ShapeDtypeStruct(*out) for out in outs]
    moved = sum(x.size * x.dtype.itemsize for x in list(operands) + shapes)
    return pl.pallas_call(
        body,
        out_shape=shapes,
        in_specs=specs,
        out_specs=[pl.BlockSpec(memory_space=pltpu.VMEM)] * len(outs),
        scratch_shapes=scratch,
        compiler_params=pltpu.CompilerParams(vmem_limit_bytes=limit * 2**20),
        cost_estimate=pl.CostEstimate(
            flops=flops, bytes_accessed=moved, transcendentals=transcendentals
        ),
        name=name,
    )(*operands)


def attend_forward(chip, pieces, mod_full, bias_rows, parts, heads, scale):
    seq = pieces[-1].shape[0]
    rows, model_width = 2 * seq, pieces[0].shape[1]
    width = heads * HD
    return kernel_call(
        functools.partial(attend_forward_body, heads, scale),
        "attend_forward",
        [
            ((rows, model_width), jnp.bfloat16),
            ((rows, model_width), jnp.float32),
            ((rows, 3 * width), jnp.bfloat16),
            ((rows, width), jnp.bfloat16),
            ((model_width, 3 * width), jnp.bfloat16),
            ((model_width, width), jnp.bfloat16),
            ((seq, model_width), jnp.float32),
            ((seq, model_width), jnp.float32),
        ],
        [chip.reshape(1), *pieces, mod_full, bias_rows, *parts],
        [pltpu.VMEM((rows, model_width), jnp.bfloat16)],
        20,
        2 * rows * model_width * 4 * width + 8 * seq * seq * width,
        2 * 2 * heads * seq * seq,
    )


def feed_forward_body(chip_ref, *refs):
    pieces, ups, mod_ref, bias_ref, parts = refs[:4], refs[4:7], refs[7], refs[8], refs[9:14]
    act_ref, sums_ref, reduce_ref = refs[14:17]
    partials, blocks, expand_ref, joined = refs[17:19], refs[19:23], refs[23], refs[24]
    rows_ref, back_ref, low_ref, grad_ref = refs[25:29]
    place_rows(chip_ref[0], parts, (expand_ref, reduce_ref))
    join_rows(pieces, rows_ref)
    join_rows(ups, joined)
    seq = joined.shape[0] // 2
    model_width = joined.shape[1]
    sums = None
    for n in (1, 0):
        rows = slice(n * seq, (n + 1) * seq)
        value = dot(rows_ref[rows, :], expand_ref[...]) + bias_ref[...]
        gate = mod_ref[n : n + 1, 5 * model_width : 6 * model_width]
        back = (joined[rows, :].astype(jnp.float32) * gate).astype(jnp.bfloat16)
        back_ref[rows, :] = back
        grad_act = dot(back, reduce_ref[...])
        square = value * value
        slope = math.sqrt(2.0 / math.pi)
        bent = jnp.tanh(slope * (value + 0.044715 * (square * value)))
        share = 0.5 * (1.0 + bent)
        act_ref[rows, :] = (value * share).astype(jnp.bfloat16)
        curve = 0.5 * value * (1.0 - bent * bent) * (slope * (1.0 + 3 * 0.044715 * square))
        grad_pre = grad_act * (share + curve)
        part = jnp.sum(grad_pre, axis=0, keepdims=True)
        sums = part if sums is None else sums + part
        low = grad_pre.astype(jnp.bfloat16)
        low_ref[rows, :] = low
        partials[n][...] = dot(low, expand_ref[...], 1, 1)
    sums_ref[...] = sums
    width = act_ref.shape[1]
    grad_ref[:, :width] = dot(rows_ref[...], low_ref[...], 0, 0)
    grad_ref[:, width:] = dot(back_ref[...], act_ref[...], 0, 0)
    write_blocks(chip_ref[0], grad_ref, blocks)


def feed_forward(chip, pieces, ups, mod_full, bias, parts):
    seq = ups[-1].shape[0]
    rows, model_width = 2 * seq, pieces[0].shape[1]
    width = bias.shape[1]
    return kernel_call(
        feed_forward_body,
        "feed_forward",
        [
            ((rows, width), jnp.bfloat16),
            ((1, width), jnp.float32),
            ((model_width, width), jnp.bfloat16),
            ((seq, model_width), jnp.float32),
            ((seq, model_width), jnp.float32),
        ]
        + block_shapes(model_width, 2 * width),
        [chip.reshape(1), *pieces, *ups, mod_full, bias, *parts],
        [
            pltpu.VMEM((model_width, width), jnp.bfloat16),
            pltpu.VMEM((rows, model_width), jnp.bfloat16),
            pltpu.VMEM((rows, model_width), jnp.bfloat16),
            pltpu.VMEM((rows, model_width), jnp.bfloat16),
            pltpu.VMEM((rows, width), jnp.bfloat16),
            pltpu.VMEM((model_width, 2 * width), jnp.float32),
        ],
        36,
        10 * rows * model_width * width,
        rows * width,
    )


def write_blocks(chip, grad_ref, out_refs):
    keep_first, keep_second, send_first, send_second = out_refs
    count = keep_first.shape[0] // 2
    plan = [
        (keep_first, 0, (0, 2)),
        (keep_second, 1, (0, 1)),
        (send_first, 0, (1, 3)),
        (send_second, 1, (2, 3)),
    ]
    for out_ref, part, places in plan:
        for block, r in enumerate(places):
            source = pl.ds(pl.multiple_of((chip ^ r) * (2 * count) + part * count, 8), count)
            out_ref[block * count : (block + 1) * count, :] = grad_ref[source, :].astype(
                out_ref.dtype
            )


def block_shapes(height, width):
    shape = (height // 4, width)
    return [(shape, jnp.float32)] * 2 + [(shape, jnp.bfloat16)] * 2


def grad_blocks_body(chip_ref, *refs):
    out_refs, grad_ref = refs[-5:-1], refs[-1]
    start = 0
    for rows, cols in zip(refs[:-5:2], refs[1:-5:2]):
        stop = start + cols.shape[1]
        grad_ref[:, start:stop] = dot(rows[...], cols[...], 0, 0)
        start = stop
    write_blocks(chip_ref[0], grad_ref, out_refs)


def grad_blocks(pairs, chip):
    height = pairs[0][0].shape[1]
    width = sum(cols.shape[1] for _, cols in pairs)
    return kernel_call(
        grad_blocks_body,
        "grad_blocks",
        block_shapes(height, width),
        [chip.reshape(1)] + [part for pair in pairs for part in pair],
        [pltpu.VMEM((height, width), jnp.float32)],
        16,
        sum(2 * rows.size * cols.shape[1] for rows, cols in pairs),
    )


def first_step(sends):
    return [swap(sends[0], "dp", 2), swap(sends[1], "dp", 4)]


def middle_body(keep_first, keep_second, got_first, got_second, *outs):
    count = keep_first.shape[0] // 2
    for keep, got, base, going in (
        (keep_first, got_first, outs[0], outs[2]),
        (keep_second, got_second, outs[1], outs[3]),
    ):
        total = keep[...] + got[...].astype(jnp.float32)
        base[...] = total[:count]
        going[...] = total[count:].astype(jnp.bfloat16)


def middle_step(keeps, received):
    rows, width = keeps[0].shape
    shape = (rows // 2, width)
    outs = [(shape, jnp.float32)] * 2 + [(shape, jnp.bfloat16)] * 2
    return kernel_call(middle_body, "middle_step", outs, [*keeps, *received], [], 16, 0)


def second_step(going):
    return [swap(going[0], "dp", 4), swap(going[1], "dp", 2)]


def core_body(core_ref, base_first, base_second, got_first, got_second, mine, other):
    first = base_first[...] + got_first[...].astype(jnp.float32)
    second = base_second[...] + got_second[...].astype(jnp.float32)
    is_first = core_ref[0] == 0
    mine[...] = jnp.where(is_first, first, second)
    other[...] = jnp.where(is_first, second, first)


def core_step(core, bases, received):
    outs = [(bases[0].shape, jnp.float32)] * 2
    operands = [core.reshape(1), *bases, *received]
    return kernel_call(core_body, "core_step", outs, operands, [], 12, 0)


def half_body(own_ref, mine, other, kept, sent):
    is_own = own_ref[0] == 1
    kept[...] = jnp.where(is_own, mine[...], other[...])
    sent[...] = jnp.where(is_own, other[...], mine[...]).astype(jnp.bfloat16)


def half_step(is_own, mine, other):
    outs = [(mine.shape, jnp.float32), (mine.shape, jnp.bfloat16)]
    operands = [is_own.astype(jnp.int32).reshape(1), mine, other]
    return kernel_call(half_body, "half_step", outs, operands, [], 12, 0)


def mod_sum_body(partial, crossed, mod_bias, attend_bias, expand_bias, out):
    heads = attend_bias.shape[1]
    out[...] = jnp.zeros_like(out)
    out[0:2, :] = partial[0:2, :] + crossed[2:4, :] + mod_bias[...]
    out[2:4, :] = partial[2:4, :] + crossed[0:2, :] + mod_bias[...]
    out[4:5, :heads] = attend_bias[0:1, :]
    out[4:5, heads : 2 * heads] = attend_bias[1:2, :]
    out[4:5, 2 * heads :] = expand_bias[...]


def mod_place_body(place_ref, own, near, far, mod, qkv_bias, expand_bias, *pieces):
    z, half, is_own = place_ref[0], place_ref[1], place_ref[2]
    width = own.shape[1]
    for r, (source, start) in enumerate(((own, 0), (near, 0), (far, 0), (far, 8))):
        cols = pl.ds(pl.multiple_of((z ^ r) * width, 128), width)
        mod[0:1, cols] = source[pl.ds(start + half, 1), :]
        mod[1:2, cols] = source[pl.ds(start + 2 + half, 1), :]
    wide = expand_bias.shape[1]
    for k, piece in enumerate(pieces):
        piece[...] = mod[0:1, k * wide : (k + 1) * wide]
    bias = jnp.where(is_own == 1, own[4:5, :], far[4:5, :])
    heads = qkv_bias.shape[1] // 3
    qkv_bias[:, :heads] = bias[:, :heads]
    qkv_bias[:, heads : 2 * heads] = jnp.zeros_like(qkv_bias[:, heads : 2 * heads])
    qkv_bias[:, 2 * heads :] = bias[:, heads : 2 * heads]
    expand_bias[...] = bias[:, 2 * heads :]


def halve_body(own, got, keep, send):
    count = keep.shape[0]
    keep[...] = own[:count, :] + got[:count, :]
    send[...] = (own[count:, :] + got[count:, :]).astype(jnp.bfloat16)


def halve(own, got):
    shape = (own.shape[0] // 2, own.shape[1])
    outs = [(shape, jnp.float32), (shape, jnp.bfloat16)]
    return kernel_call(halve_body, "halve", outs, [own, got], [], 8, 0)


def column_sums(values):
    return jnp.sum(values, axis=0, keepdims=True)


def residual_body(keep, got, tokens, out_bias, gate, shift, gain, attend_out, residual, low):
    attend_out[...] = keep[...] + got[...].astype(jnp.float32) + out_bias[...]
    residual[...] = tokens[...].astype(jnp.float32) + gate[...] * attend_out[...]
    normed, _ = normalize(residual[...])
    low[...] = (normed * (1.0 + gain[...]) + shift[...]).astype(jnp.bfloat16)


def hidden_back_body(
    keep, got, residual, attend_out, upstream, gate_a, gain, gate_m, low, grad_residual, sums
):
    grad = keep[...] + got[...].astype(jnp.float32)
    normed, inverse = normalize(residual[...])
    up = upstream[...].astype(jnp.float32)
    total = up + norm_back(grad * (1.0 + gain[...]), normed, inverse)
    grad_residual[...] = total
    term = total * gate_a[...]
    low[...] = term.astype(jnp.bfloat16)
    sums[0:1, :] = column_sums(total * attend_out[...])
    sums[1:2, :] = column_sums(grad)
    sums[2:3, :] = column_sums(grad * normed)
    sums[3:4, :] = column_sums(term)
    sums[4:5, :] = column_sums(up * gate_m[...])
    sums[5:8, :] = jnp.zeros_like(sums[5:8, :])


def block_out_body(keep, got, residual, upstream, reduce_bias, gate, block, gate_sum):
    hidden_out = keep[...] + got[...].astype(jnp.float32) + reduce_bias[...]
    block[...] = (residual[...] + gate[...] * hidden_out).astype(jnp.bfloat16)
    gate_sum[...] = column_sums(upstream[...].astype(jnp.float32) * hidden_out)


def tokens_back_body(keep, got, tokens, grad_residual, gain, kept, send):
    count = kept.shape[0]
    grad = keep[...] + got[...].astype(jnp.float32)
    normed, inverse = normalize(tokens[...].astype(jnp.float32))
    total = grad_residual[...] + norm_back(grad * (1.0 + gain[...]), normed, inverse)
    kept[...] = total[:count, :]
    send[...] = total[count:, :].astype(jnp.bfloat16)


def outputs_body(half_ref, block, block_moved, kept, moved, block_out, tokens_grad):
    half, count = half_ref[0], kept.shape[0]
    block_out[half] = block[:count, :]
    block_out[1 - half] = block_moved[...]
    tokens_grad[half] = kept[...]
    tokens_grad[1 - half] = moved[...].astype(jnp.float32)


def owner_body(kept, moved, *outs):
    start = 0
    for out in outs:
        stop = start + out.shape[1]
        out[...] = kept[:, start:stop] + moved[:, start:stop].astype(jnp.float32)
        start = stop


def owner_sum(kept, moved, widths):
    outs = [((kept.shape[0], width), jnp.float32) for width in widths]
    return kernel_call(owner_body, "owner_sum", outs, [kept, moved], [], 8, 0)


def pack_body(norm, got, sums, gate_m, expand, bias, packed):
    wide = gate_m.shape[1]
    part = packed.shape[1] - wide
    both = norm[0:1, :] + got[...]
    packed[0:1, :wide] = both[:, :wide]
    packed[0:1, wide:] = both[:, wide : wide + part]
    packed[1:2, : wide - part] = both[:, wide + part :]
    packed[1:2, wide - part :] = sums[0:1, :]
    packed[2:3, :wide] = sums[1:2, :]
    packed[2:3, wide:] = sums[2:3, :part]
    packed[3:4, : wide - part] = sums[2:3, part:]
    packed[3:4, wide - part :] = gate_m[...]
    packed[4:5, :wide] = sums[3:4, :]
    packed[4:5, wide:] = sums[4:5, :part]
    packed[5:6, : wide - part] = sums[4:5, part:]
    packed[5:6, wide - part :] = jnp.zeros_like(packed[5:6, wide - part :])
    heads = bias.shape[1] // 3
    packed[6:7, :wide] = expand[...]
    packed[6:7, wide : wide + heads] = bias[:, :heads]
    packed[6:7, wide + heads :] = bias[:, 2 * heads :]
    packed[7:8, :] = jnp.zeros_like(packed[7:8, :])


def attend_owner_body(kept, moved, attend_grad, output_grad):
    width = output_grad.shape[1]
    for j in range(3):
        cols = slice(j * width, (j + 1) * width)
        attend_grad[j] = kept[:, cols] + moved[:, cols].astype(jnp.float32)
    output_grad[...] = kept[:, 3 * width :] + moved[:, 3 * width :].astype(jnp.float32)


def choose_body(place_ref, line, far, packed):
    z, half, own = place_ref[0], place_ref[1], place_ref[2]
    packed[pl.ds(half, 1), :] = line[pl.ds(z, 1), :]
    packed[pl.ds(1 - half, 1), :] = far[pl.ds(z, 1), :]
    packed[2:3, :] = jnp.where(own == 1, line[6:7, :] + far[6:7, :], 0.0)
    packed[3:5, :] = line[4:6, :] + far[4:6, :]
    packed[5:8, :] = jnp.zeros_like(packed[5:8, :])


def modulation_back_body(gathered, silu, weight, weight_grad, grad_silu, bias_grad, rest, rows):
    parts = [gathered[start : start + 8, :] for start in range(0, gathered.shape[0], 8)]
    for m, part in enumerate(parts):
        rows[2 * m : 2 * m + 2, :] = part[0:2, :]
    low = rows[...].astype(jnp.bfloat16)
    weight_grad[...] = dot(silu[...], low, 0, 0)
    grad_silu[...] = dot(low, weight[...], 1, 1)
    while len(parts) > 1:
        parts = [left + right for left, right in zip(parts[::2], parts[1::2])]
    bias_grad[...] = parts[0][0:1, :] + parts[0][1:2, :]
    rest[...] = parts[0][2:5, :]


def table_body(labels, cond, near, far, table, chosen):
    value = cond[...]
    share = 1.0 / (1.0 + jnp.exp(-value))
    grad = (near[...] + far[...]) * share * (1.0 + value * (1.0 - share))
    place = lax.broadcasted_iota(jnp.int32, (1, chosen.shape[1]), 1)
    for row in range(chosen.shape[0]):
        chosen[row : row + 1, :] = jnp.where(place == labels[row], 1.0, 0.0)
    table[...] = lax.dot_general(
        grad,
        chosen[...],
        (((0,), (0,)), ((), ())),
        precision=lax.Precision.HIGHEST,
        preferred_element_type=jnp.float32,
    )


def join_body(attend, output, joined):
    width = output.shape[1]
    for j in range(3):
        joined[:, j * width : (j + 1) * width] = attend[j]
    joined[:, 3 * width :] = output[...]


def attend_back_body(heads, scale, *refs):
    pieces = refs[:4]
    output_ref, qkv_ref, mixed_ref, attend_ref, normed_ref = refs[4:9]
    rows_ref, low_ref, sums_ref, norm_sums_ref = refs[9:13]
    partials = refs[13:15]
    join_rows(pieces, rows_ref)
    seq = rows_ref.shape[0] // 2
    model_width, width = output_ref.shape
    sums = None
    for n in (1, 0):
        rows = slice(n * seq, (n + 1) * seq)
        grad_mixed = dot(rows_ref[rows, :], output_ref[...]).astype(jnp.bfloat16)
        grads = [[], [], []]
        for head in range(heads):
            query, key, value = (
                qkv_ref[rows, j * width + head * HD : j * width + (head + 1) * HD]
                for j in range(3)
            )
            mixed = mixed_ref[rows, head * HD : (head + 1) * HD]
            up = grad_mixed[:, head * HD : (head + 1) * HD]
            probs = attend_probs(query, key, scale)
            delta = jnp.sum(
                up.astype(jnp.float32) * mixed.astype(jnp.float32), axis=1, keepdims=True
            )
            logit = (probs * (dot(up, value, 1, 1) - delta)).astype(jnp.bfloat16)
            grads[0].append(dot(logit, key) * scale)
            grads[1].append(dot(logit, query, 0, 0) * scale)
            grads[2].append(dot(probs.astype(jnp.bfloat16), up, 0, 0))
        whole = jnp.concatenate([part for group in grads for part in group], axis=1)
        part = jnp.sum(whole, axis=0, keepdims=True)
        sums = part if sums is None else sums + part
        low = whole.astype(jnp.bfloat16)
        low_ref[rows, :] = low
        partial = dot(low, attend_ref[...], 1, 1)
        partials[n][...] = partial
        norm_sums_ref[n : n + 1, :model_width] = jnp.sum(partial, axis=0, keepdims=True)
        norm_sums_ref[n : n + 1, model_width:] = jnp.sum(
            partial * normed_ref[rows, :], axis=0, keepdims=True
        )
    sums_ref[...] = sums


def attend_back(pieces, output_full, qkv, mixed, attend_full, normed, heads, scale):
    rows, model_width = normed.shape
    seq, width = rows // 2, mixed.shape[1]
    return kernel_call(
        functools.partial(attend_back_body, heads, scale),
        "attend_back",
        [
            ((rows, model_width), jnp.bfloat16),
            ((rows, 3 * width), jnp.bfloat16),
            ((1, 3 * width), jnp.float32),
            ((2, 2 * model_width), jnp.float32),
            ((seq, model_width), jnp.float32),
            ((seq, model_width), jnp.float32),
        ],
        [*pieces, output_full, qkv, mixed, attend_full, normed],
        [],
        20,
        2 * rows * model_width * 4 * width + 20 * seq * seq * width,
        2 * 2 * heads * seq * seq,
    )


def on_paired_device(
    tokens,
    cotangent,
    labels,
    timesteps,
    class_table,
    modulation_weight,
    modulation_bias,
    attend_weight,
    attend_bias,
    output_weight,
    output_bias,
    expand_weight,
    expand_bias,
    reduce_weight,
    reduce_bias,
):
    data_index = lax.axis_index("dp")
    tensor_index = lax.axis_index("tensor")
    core, chip = data_index & 1, data_index >> 1
    half = tensor_index >> 1
    is_own = half == core
    model_width = tokens.shape[2]
    row_share = modulation_weight.shape[0]
    head_width = attend_weight.shape[2]
    head_count = head_width // HD
    ff_width = expand_weight.shape[1]
    mod_width = modulation_weight.shape[1]
    latent_total = labels.shape[0]
    classes_total = class_table.shape[0]
    score_scale = 1.0 / math.sqrt(HD)

    count = tokens.shape[1]
    place = jnp.stack([tensor_index, half, is_own.astype(jnp.int32)])

    order = Order()
    mark, hold = order.mark, order.hold

    attn_shard = kernel_call(
        join_body,
        "join_weights",
        [((row_share, 4 * head_width), jnp.bfloat16)],
        [jnp.transpose(attend_weight, (1, 0, 2)), output_weight],
        [],
        4,
        0,
    )[0]
    mark(ATTN_SHARD, attn_shard)
    attn_far = mark(ATTN_FAR, swap(attn_shard, "tensor", 2))
    tokens_sent = pick(hold(TOKENS_SENT, tokens), 1 - half)
    tokens_half = jnp.concatenate([pick(tokens, half), swap(tokens_sent, "tensor", 2)])
    mark(TOKENS_HALF, tokens_half)
    labels, timesteps = (labels, timesteps)

    slot = jnp.arange(latent_total, dtype=jnp.int32)
    latent_ids = ((slot >> 1) ^ data_index) * 2 + (slot & 1)
    chosen = latent_ids[:, None] == slot[None, :]
    labels_rel = jnp.sum(jnp.where(chosen, labels[None, :], 0), axis=1)
    steps_rel = jnp.sum(jnp.where(chosen, timesteps[None, :], 0), axis=1)
    looked = lax.dynamic_slice_in_dim(
        jnp.take(class_table, labels_rel, axis=0), data_index * row_share, row_share, 1
    ).astype(jnp.float32)
    halfway = model_width // 2
    column = data_index * row_share + jnp.arange(row_share, dtype=jnp.int32)
    is_cos = column < halfway
    position = jnp.where(is_cos, column, column - halfway).astype(jnp.float32)
    frequency = jnp.exp(-math.log(10000.0) * position / halfway)
    angles = steps_rel.astype(jnp.float32)[:, None] * frequency[None, :]
    cond = looked + jnp.where(is_cos[None, :], jnp.cos(angles), jnp.sin(angles))
    silu_act = jax.nn.silu(cond).astype(jnp.bfloat16)
    partial = jnp.dot(silu_act, modulation_weight, preferred_element_type=jnp.float32)
    partial = partial[:8] + swap(partial[8:], "dp", 4)
    attn_share = near_weight(attn_shard, attn_far, is_own, core)
    mark(ATTN_SHARE, attn_share)
    partial = partial[:4] + swap(partial[4:], "dp", 2)
    partial = hold(PARTIAL_CORE, partial)
    ff_shard = jnp.concatenate([expand_weight, reduce_weight], axis=1)
    tokens_near = swap(tokens_half, "tensor", 1)
    mod_cols = kernel_call(
        mod_sum_body,
        "mod_sum",
        [((8, mod_width), jnp.float32)],
        [
            partial,
            swap(partial, "dp", 1),
            modulation_bias[None],
            attend_bias,
            expand_bias[None],
        ],
        [],
        4,
        0,
    )[0]
    attn_first = mark(ATTN_FIRST, chip_first(attn_share))
    attn_parts = chip_second(attn_share, *attn_first)
    mark(ATTN_PARTS, attn_parts)
    mod_near = swap(mod_cols, "tensor", 1)
    mod_line = jnp.concatenate([mod_cols, mod_near])
    mark(MOD_LINE, mod_line)
    mod_far = swap(hold(MOD_LINE, mod_line), "tensor", 2)
    ff_far = mark(FF_FAR, swap(hold(FF_SHARD, ff_shard), "tensor", 2))
    tokens_across = swap(jnp.concatenate([tokens_half, tokens_near]), "dp", 1)
    row = ((1, model_width), jnp.float32)
    mod_full, qkv_bias, expand_row, _, gain_a, gate_a, shift_m, gain_m, gate_m = kernel_call(
        mod_place_body,
        "mod_place",
        [
            ((2, 6 * model_width), jnp.float32),
            ((1, 3 * head_width), jnp.float32),
            ((1, ff_width), jnp.float32),
        ]
        + [row] * 6,
        [place, mod_cols, mod_near, hold(MOD_PLACE, mod_far)],
        [],
        4,
        0,
    )
    ff_share = near_weight(ff_shard, hold(FF_FAR, ff_far), is_own, core)
    mark(FF_SHARE, ff_share)
    upstream_sent = hold(UPSTREAM_SENT, pick(cotangent, 1 - half))
    upstream_far = swap(upstream_sent, "tensor", 2)
    ff_first = chip_first(ff_share)

    (
        attend_rows,
        normed_all,
        projected,
        mixed_rows,
        attend_full,
        output_full,
        own_partial,
        other_partial,
    ) = attend_forward(
        chip,
        [tokens_half, tokens_near, hold(ATTEND, tokens_across)],
        mod_full,
        qkv_bias,
        attn_parts,
        head_count,
        score_scale,
    )
    keep, send = halve(own_partial, swap(other_partial, "dp", 1))
    mark(ATTEND_SEND, send)
    upstream_half = jnp.concatenate([pick(cotangent, half), hold(UPSTREAM_FAR, upstream_far)])
    ff_first = hold(FF_SECOND, ff_first)
    ff_parts = chip_second(ff_share, *ff_first)
    got = swap(send, "tensor", 1)
    upstream_near = swap(upstream_half, "tensor", 1)
    attend_out, residual, hidden_in = kernel_call(
        residual_body,
        "residual",
        [(keep.shape, jnp.float32), (keep.shape, jnp.float32), (keep.shape, jnp.bfloat16)],
        [
            keep,
            got,
            tokens_half,
            output_bias[None],
            gate_a,
            shift_m,
            gain_m,
        ],
        [],
        8,
        0,
    )
    hidden_pieces = collect_pairs(hidden_in)
    upstream_line = jnp.concatenate([upstream_half, upstream_near])
    upstream_across = swap(upstream_line, "dp", 1)

    (
        activated,
        grad_expand_bias,
        reduce_full,
        own_partial,
        other_partial,
        *ff_blocks,
    ) = feed_forward(
        chip,
        hidden_pieces,
        [upstream_half, upstream_near, upstream_across],
        mod_full,
        expand_row,
        ff_parts,
    )
    mark(FEED, own_partial)
    keep, send = halve(own_partial, swap(other_partial, "dp", 1))
    mark(FEED_SEND, send)
    got = swap(send, "tensor", 1)
    ff_first = first_step(hold(FF_BLOCKS, ff_blocks[2:]))
    seq_len = tokens_across.shape[0]
    act_later = hold(ACTIVATED, activated)
    other_out, own_out = (
        jnp.einsum("sf,of->so", act_half, reduce_full, preferred_element_type=jnp.float32)
        for act_half in (act_later[seq_len:], act_later[:seq_len])
    )
    out_keep, out_send = halve(own_out, swap(other_out, "dp", 1))
    mark(OUT_SEND, out_send)
    output_low, grad_residual, row_sums = kernel_call(
        hidden_back_body,
        "hidden_back",
        [(keep.shape, jnp.bfloat16), (keep.shape, jnp.float32), ((8, model_width), jnp.float32)],
        [
            keep,
            hold(HIDDEN_BACK, got),
            residual,
            attend_out,
            upstream_half,
            gate_a,
            gain_m,
            gate_m,
        ],
        [],
        8,
        0,
    )
    output_pieces = collect_pairs(output_low)
    mark(OUTPUT_NEAR, output_pieces[1])
    block_own, gate_sum = kernel_call(
        block_out_body,
        "block_out",
        [(keep.shape, jnp.bfloat16), row],
        [
            out_keep,
            swap(out_send, "tensor", 1),
            residual,
            upstream_half,
            reduce_bias[None],
            gate_m,
        ],
        [],
        8,
        0,
    )
    mark(BLOCK_OUT, block_own)

    def ff_middle():
        *bases, going, going_second = middle_step(ff_blocks[:2], hold(FF_MIDDLE, ff_first))
        mark(FF_GOING, going)
        return bases, second_step([going, going_second])

    ff_bases, ff_second = ff_middle()

    (
        output_rows,
        projected_low,
        bias_sums,
        norm_sums,
        own_partial,
        other_partial,
    ) = attend_back(
        hold(ATTEND_BACK, output_pieces),
        output_full,
        projected,
        mixed_rows,
        attend_full,
        normed_all,
        head_count,
        score_scale,
    )
    block_moved = swap(block_own[count:], "tensor", 2)
    norm_crossed = mark(NORM_CROSSED, swap(norm_sums[1:], "dp", 1))
    ff_mine, ff_other = core_step(core, ff_bases, hold(FF_CORE, ff_second))
    mark(FF_CORE, ff_mine)
    ff_kept, ff_sent = half_step(is_own, ff_mine, swap(ff_other, "dp", 1))
    mark(FF_HALF, ff_sent)

    line = kernel_call(
        pack_body,
        "pack",
        [((8, mod_width), jnp.float32)],
        [
            norm_sums,
            hold(PACK, norm_crossed),
            row_sums,
            gate_sum,
            grad_expand_bias,
            bias_sums,
        ],
        [],
        4,
        0,
    )[0]
    mark(PACK, line)
    keep, send = halve(own_partial, swap(other_partial, "dp", 1))
    grad_got = swap(send, "tensor", 1)
    attn_blocks = grad_blocks(
        [(attend_rows, hold(ATTN_BLOCKS, projected_low)), (output_rows, mixed_rows)], chip
    )
    mark(ATTN_BLOCKS, attn_blocks[2])
    attn_first = first_step(attn_blocks[2:])
    summed = lax.broadcasted_iota(jnp.int32, line.shape, 0) < 6
    near = hold(LINE, swap(hold(LINE_NEAR, line), "tensor", 1))
    line = line + jnp.where(summed, near, 0.0)
    far = swap(hold(LINE_FAR, line), "tensor", 2)
    packed = kernel_call(
        choose_body,
        "choose",
        [((8, mod_width), jnp.float32)],
        [place, line, far],
        [],
        4,
        0,
    )[0]
    ff_moved = mark(FF_MOVED, swap(ff_sent, "tensor", 2))
    tokens_kept, back_sent = kernel_call(
        tokens_back_body,
        "tokens_back",
        [((count, model_width), jnp.float32), ((count, model_width), jnp.bfloat16)],
        [keep, grad_got, tokens_half, grad_residual, gain_a],
        [],
        8,
        0,
    )
    tokens_moved = swap(back_sent, "tensor", 2)
    *attn_bases, attn_going, attn_going_second = middle_step(
        attn_blocks[:2], attn_first
    )
    attn_second = second_step([attn_going, attn_going_second])
    packed = jnp.concatenate([packed, swap(packed, "dp", 1)])
    packed = jnp.concatenate([packed, swap(hold(PACKED_X, packed), "dp", 2)])
    attn_mine, attn_other = core_step(core, attn_bases, attn_second)
    mark(ATTN_CORE, attn_mine)
    packed = jnp.concatenate([packed, swap(hold(PACKED_Y, packed), "dp", 4)])
    modulation_weight_grad, grad_silu, modulation_bias_grad, rest = kernel_call(
        modulation_back_body,
        "modulation_back",
        [
            ((row_share, mod_width), jnp.float32),
            ((latent_total, row_share), jnp.float32),
            ((1, mod_width), jnp.float32),
            ((3, mod_width), jnp.float32),
        ],
        [hold(MODULATION_BACK, packed), silu_act, modulation_weight],
        [pltpu.VMEM((latent_total, mod_width), jnp.float32)],
        8,
        4 * latent_total * row_share * mod_width,
    )
    mark(MODULATION_BACK, grad_silu)
    attn_kept, attn_sent = half_step(is_own, attn_mine, hold(ATTN_HALF, swap(attn_other, "dp", 1)))
    attn_moved = swap(hold(ATTN_SENT, attn_sent), "tensor", 2)
    near = grad_silu + swap(hold(GRAD_SILU, grad_silu), "tensor", 1)
    mark(NEAR, near)
    table_grad = kernel_call(
        table_body,
        "table",
        [((row_share, classes_total), jnp.float32)],
        [labels_rel, cond, near, hold(TABLE, swap(near, "tensor", 2))],
        [pltpu.VMEM((latent_total, classes_total), jnp.float32)],
        4,
        0,
    )[0]
    expand_grad, reduce_grad = owner_sum(
        ff_kept, hold(FF_OWNER, ff_moved), [ff_width, ff_width]
    )
    attend_grad, output_grad = kernel_call(
        attend_owner_body,
        "owner_sum",
        [((3, row_share, head_width), jnp.float32), (output_weight.shape, jnp.float32)],
        [attn_kept, attn_moved],
        [],
        8,
        0,
    )
    block_output, tokens_grad = kernel_call(
        outputs_body,
        "outputs",
        [(tokens.shape, jnp.bfloat16), (tokens.shape, jnp.float32)],
        [half.reshape(1), block_own, block_moved, tokens_kept, hold(OUTPUTS, tokens_moved)],
        [],
        8,
        0,
    )
    wide = model_width
    return (
        block_output,
        tokens_grad,
        table_grad.T,
        modulation_weight_grad,
        modulation_bias_grad[0],
        jnp.transpose(attend_grad, (1, 0, 2)),
        rest[0, wide:].reshape(2, head_width),
        output_grad,
        rest[1, :wide],
        expand_grad,
        rest[0, :wide],
        reduce_grad,
        jnp.concatenate([rest[1, wide:], rest[2, : 2 * wide - mod_width]]),
    )


def solution(mesh):
    paired = mesh.shape["dp"] == 8 and mesh.shape["tensor"] == 4
    per_device = on_paired_device if paired else on_device
    placed = (
        P("dp", "tensor", None),
        P("dp", "tensor", None),
        P(),
        P(),
        P(),
        P("dp", "tensor"),
        P("tensor"),
        P("dp", None, "tensor"),
        P(None, "tensor"),
        P("dp", "tensor"),
        P(),
        P("dp", "tensor"),
        P("tensor"),
        P("dp", "tensor"),
        P(),
    )
    return jax.shard_map(
        per_device,
        mesh=mesh,
        in_specs=placed,
        out_specs=(
            P("dp", "tensor", None),
            P("dp", "tensor", None),
            P(None, "dp"),
            P("dp", "tensor"),
            P("tensor"),
            P("dp", None, "tensor"),
            P(None, "tensor"),
            P("dp", "tensor"),
            P(),
            P("dp", "tensor"),
            P("tensor"),
            P("dp", "tensor"),
            P(),
        ),
        check_vma=False,
    )
```
